128 devices in a mesh: ctx: 8 (over y, z_hi), chan: 16 (over x, z_lo, core).
Axes of the slice: x: 4, y: 4, z: 4 (z_hi: 2, z_lo: 2; z = z_hi * 2 + z_lo), core: 2. Of those that a mesh axis runs over, the one named last changes fastest.
Arguments:
- featurized: bfloat16 [16384, 3, 8192], P('ctx', None, 'chan'), may hold values from -6 to 6
- short_filter: float32 [3, 3, 8192], P(None, None, 'chan'), may hold values from -2.5 to 2.5
- decay_rate: float32 [512, 16], P('chan'), as said below
- residue: float32 [512, 16], P('chan'), may hold values from -2.5 to 2.5
- skip_gain: float32 [8192], P('chan'), may hold values from 0.25 to 1.5
- out_weight: bfloat16 [8192, 4096], P('chan'), may hold values from -0.0625 to 0.0625
Outputs:
- output: bfloat16 [16384, 4096], P(('ctx', 'chan'))
The draws below stay inside these ranges and needn't reach their ends.
Inputs may be any that keep to these rules, and one draw needn't show every extreme that they name: `decay_rate`: each rate is at least 0.2 / 16384.
All inputs are finite; a program needn't handle non-finite values.
Results may differ from the reference program's by a relative error of at most 0.02.
Values may be sent and summed in bfloat16 or wider, within the bound.
A program may use at most 256 MiB of HBM per device.

```python
import math
import jax
import jax.numpy as jnp
from jax import lax

D = 8192
FGROUP = 16
MODES = 16
OUTC = 4096
LENGTH = 16384
N_CHAN = 16


def draw_decay_rate(key, part):
    filter_count = D // FGROUP
    subkeys = jax.random.split(key, 3)
    slow_share = 0.5
    slow_pick = jax.random.uniform(subkeys[0], (filter_count, MODES)) < slow_share
    fast_rate = jnp.exp(jax.random.uniform(subkeys[1], (filter_count, MODES), minval=math.log(1.0 / 50.0), maxval=math.log(1.0 / 20.0)))
    slow_rate = jnp.exp(jax.random.uniform(subkeys[2], (filter_count, MODES), minval=math.log(0.2), maxval=math.log(1.5))) / LENGTH
    return jnp.where(slow_pick, slow_rate, fast_rate).astype(jnp.float32)


def steps_of(own_key, dims, cuts, low, largest):
    def one(position, parts):
        draws = jax.random.uniform(jax.random.fold_in(jax.random.fold_in(own_key, 6), position), (parts,), jnp.float32, low / len(cuts), largest / len(cuts))
        return jnp.repeat(jnp.exp(draws), dims[position] // parts).reshape((-1,) + (1,) * (len(dims) - position - 1))

    factor_of = one(*cuts[0])
    for cut in cuts[1:]:
        factor_of = factor_of * one(*cut)
    return factor_of


def gaussian(key, shape, spread, reach, pieces=(), kind=jnp.bfloat16):
    level = steps_of(key, shape, pieces, -0.22, 0.18) if pieces else 1.0
    array = jax.random.normal(key, shape, jnp.float32) * spread * level
    return jnp.minimum(jnp.maximum(array, -reach), reach).astype(kind)


def setup_inputs(seed: int = 0) -> dict:
    key_list = jax.random.split(jax.random.key(seed), 7)
    return {
        "featurized": gaussian(key_list[0], (LENGTH, 3, D), 1.0, 6.0, ((0, 8), (2, 16))),
        "short_filter": gaussian(key_list[1], (3, 3, D), 0.5, 2.5, ((2, 16),), jnp.float32),
        "decay_rate": draw_decay_rate(jax.random.fold_in(key_list[6], 71), 0),
        "residue": gaussian(key_list[3], (D // FGROUP, MODES), 0.5, 2.5, ((0, 16),), jnp.float32),
        "skip_gain": jnp.clip(0.25 + 1.25 * jax.random.uniform(key_list[4], (D,), jnp.float32) ** steps_of(key_list[4], (D,), ((0, 16),), -0.2, 0.2), 0.25, 1.5),
        "out_weight": gaussian(key_list[5], (D, OUTC), D ** -0.5, 0.0625, ((0, 16),)),
    }


def reference(featurized, short_filter, decay_rate, residue, skip_gain, out_weight):
    inputs = featurized.astype(jnp.float32)
    padded = jnp.pad(inputs, ((2, 0), (0, 0), (0, 0)))
    shortened = short_filter[0] * padded[2:] + short_filter[1] * padded[1:-1] + short_filter[2] * padded[:-2]
    query_part = shortened[:, 0]
    gated = (shortened[:, 1] * shortened[:, 2]).astype(jnp.bfloat16)
    gated_float = gated.astype(jnp.float32)
    seq_length = gated.shape[0]
    filter_count = decay_rate.shape[0]
    scaled = residue * jnp.sqrt(-jnp.expm1(-2.0 * decay_rate))
    lags = jnp.arange(seq_length, dtype=jnp.float32)
    fft_len = 2 * seq_length
    signals = gated_float.reshape(seq_length, filter_count, FGROUP).transpose(1, 2, 0)

    def one_filter(triple):
        rates, weights, rows = triple
        kernel = lax.optimization_barrier(jnp.sum(weights[:, None] * jnp.exp(-rates[:, None] * lags[None, :]), axis=0))
        spectrum = jnp.fft.rfft(rows, n=fft_len, axis=1) * jnp.fft.rfft(kernel, n=fft_len)[None, :]
        return jnp.fft.irfft(spectrum, n=fft_len, axis=1)[:, :seq_length]
    convolved = lax.map(one_filter, (decay_rate, scaled, signals))
    long_conv = convolved.transpose(2, 0, 1).reshape(seq_length, D)
    mixed_rows = (query_part * (long_conv + skip_gain * gated_float)).astype(jnp.bfloat16)
    group_cols = D // N_CHAN
    grouped = mixed_rows.reshape(seq_length, N_CHAN, group_cols).transpose(1, 0, 2)
    weights = out_weight.reshape(N_CHAN, group_cols, OUTC)

    def add_group(summed, group_pair):
        rows_part, weight_part = group_pair
        partial_value = jnp.dot(rows_part.astype(jnp.float32), weight_part.astype(jnp.float32), preferred_element_type=jnp.float32)
        rounded = lax.optimization_barrier(partial_value.astype(jnp.bfloat16))
        return (summed + rounded.astype(jnp.float32), None)
    summed_all, unused = lax.scan(add_group, jnp.zeros((seq_length, OUTC), jnp.float32), (grouped, weights))
    return summed_all.astype(jnp.bfloat16)
```

```python
import jax
import jax.numpy as jnp
from jax import lax
from jax.experimental import pallas as pl
from jax.experimental.pallas import tpu as pltpu
from jax.sharding import Mesh
from jax.sharding import PartitionSpec as P

CHAN = ("chan_0", "chan_1", "chan_2")
CTX_CHAN = ("ctx", "chan_0", "chan_1", "chan_2")
MESH = pl.DeviceIdType.MESH
F32 = jnp.float32
BF16 = jnp.bfloat16
LANES = 128
STEP = 128
GROUP = 16
PACK = LANES // GROUP
MODES = 16
STRIP = 32
RIM = 16


def swapped(parts, lane_group):
    parts = list(parts)
    for bit in (1, 2, 4):
        low = (lane_group & bit) == 0
        for k in range(PACK):
            if k & bit == 0:
                a, b = parts[k], parts[k | bit]
                parts[k] = jnp.where(low, a, pltpu.roll(b, bit * GROUP, 1))
                parts[k | bit] = jnp.where(low, pltpu.roll(a, LANES - bit * GROUP, 1), b)
    return parts


def hi_lo(value):
    hi = value.astype(BF16).astype(F32)
    return hi, value - hi


def chunk_scan(state, rate, lane):
    width = state.shape[1]
    hop = 1
    while hop * GROUP < width:
        decay = jnp.exp(rate * (-float(hop * STEP)))
        moved = pltpu.roll(state, hop * GROUP, 1)
        state = state + jnp.where(lane >= hop * GROUP, decay * moved, 0.0)
        hop *= 2
    return state


def conv_kernel(
    feat_hbm,
    taps_ref,
    rate_row_ref,
    scale_row_ref,
    rate_ref,
    scale_ref,
    rate_chan_ref,
    skip_ref,
    mixed_ref,
    feat,
    rim,
    gated,
    query,
    source,
    left,
    local,
    total,
    totals,
    result,
    load_sem,
    rim_sem,
    sum_send,
    sum_recv,
):
    tokens, channels = feat.shape[1], feat.shape[2]
    chunks = tokens // STEP
    blocks = channels // LANES
    width = chunks * GROUP
    halves = width // LANES
    ctx = lax.axis_index("ctx")
    peers = lax.axis_size("ctx")

    loads = []
    for v in range(blocks):
        at = pl.ds(v * LANES, LANES)
        copy = pltpu.make_async_copy(feat_hbm.at[:, :, at], feat.at[:, :, at], load_sem.at[v])
        copy.start()
        loads.append(copy)

    barrier = pltpu.get_barrier_semaphore()
    for d in range(1, peers):
        pl.semaphore_signal(
            barrier, inc=1, device_id={"ctx": lax.rem(ctx + d, peers)}, device_id_type=MESH
        )
    pl.semaphore_wait(barrier, peers - 1)
    rim_copy = pltpu.make_async_remote_copy(
        src_ref=feat_hbm.at[:, pl.ds(tokens - RIM, RIM), :],
        dst_ref=rim,
        send_sem=rim_sem.at[0],
        recv_sem=rim_sem.at[1],
        device_id={"ctx": lax.rem(ctx + 1, peers)},
        device_id_type=MESH,
    )
    rim_copy.start()

    lane = lax.broadcasted_iota(jnp.int32, (1, LANES), 1)
    lane_group = lane // GROUP
    lane_wide = lax.broadcasted_iota(jnp.int32, (MODES, width), 1)
    lane_mode = lax.broadcasted_iota(jnp.int32, (MODES, LANES), 1)
    source[:, STEP + 3 * MODES :, :] = jnp.zeros(
        (source.shape[0], source.shape[1] - STEP - 3 * MODES, width), BF16
    )

    row = lax.broadcasted_iota(jnp.int32, (STEP, LANES), 0)
    col = lax.broadcasted_iota(jnp.int32, (STEP, LANES), 1)
    after = (row + 1).astype(F32)
    back = lax.rem(STEP - lane_mode, STEP).astype(F32)
    ahead = (STEP - 1 - lane_mode).astype(F32)

    def build(f, carry):
        first = jnp.sum(
            scale_ref[f] * jnp.exp(-rate_ref[f] * back), axis=0, keepdims=True
        )
        turned = pltpu.roll(
            jnp.broadcast_to(first, (STEP, LANES)), 0, 1, stride=1, stride_axis=0
        )
        left[f, :, :LANES] = jnp.where(col <= row, turned, 0.0).astype(BF16)
        rate = rate_row_ref[pl.ds(f, 1), :]
        scale = scale_row_ref[pl.ds(f, 1), :]
        hi, lo = hi_lo(scale * jnp.exp(-rate * after))
        second = (col >= MODES) & (col < 2 * MODES)
        left[f, :, LANES:] = jnp.where(second, lo, hi).astype(BF16)
        return carry

    for copy in loads:
        copy.wait()
    rim_copy.wait()

    def chunk_of(v, c):
        at = pl.ds(pl.multiple_of(v * LANES, LANES), LANES)
        here = pl.ds(pl.multiple_of(c * STEP, STEP), STEP)
        before = pl.ds(pl.multiple_of(jnp.maximum(c * STEP - RIM, 0), RIM), RIM)
        parts = []
        for i in range(3):
            earlier = feat[i, before, at].astype(F32)
            outside = jnp.where(ctx > 0, rim[i, :, at].astype(F32), 0.0)
            earlier = jnp.where(c > 0, earlier, outside)
            rows = jnp.concatenate([earlier, feat[i, here, at].astype(F32)], axis=0)
            tap = taps_ref[:, i, at]
            value = (
                tap[0:1] * rows[RIM:]
                + tap[1:2] * pltpu.roll(rows, 1, 0)[RIM:]
                + tap[2:3] * pltpu.roll(rows, 2, 0)[RIM:]
            )
            parts.append(value)
        query[here, at] = parts[0]
        gated[c] = (parts[1] * parts[2]).astype(BF16).astype(F32)

    def block_in(v, carry):
        at = pl.ds(pl.multiple_of(v * LANES, LANES), LANES)

        def one_chunk(c, inner):
            chunk_of(v, c)
            return inner

        lax.fori_loop(0, chunks, one_chunk, 0)

        def one_strip(s, inner):
            rows = pl.ds(pl.multiple_of(s * STRIP, STRIP), STRIP)
            for h in range(halves):
                parts = swapped([gated[h * PACK + k, rows, :] for k in range(PACK)], lane_group)
                for g in range(PACK):
                    source[v * PACK + g, rows, h * LANES : (h + 1) * LANES] = parts[g].astype(BF16)
            return inner

        lax.fori_loop(0, STEP // STRIP, one_strip, 0)
        packed = jnp.zeros((MODES, LANES), F32)
        for g in range(PACK):
            f = v * PACK + g
            rate = rate_ref[f]
            hi, lo = hi_lo(jnp.exp(-rate * ahead))
            weight = jnp.concatenate([hi, lo], axis=0).astype(BF16)
            product = jnp.dot(weight, source[f, :STEP, :], preferred_element_type=F32)
            ends = product[:MODES] + product[MODES:]
            local[f] = ends
            summed = chunk_scan(ends, jnp.concatenate([rate] * halves, axis=1), lane_wide)
            last = summed[:, width - LANES :]
            last = pltpu.roll(last, (g * GROUP + GROUP) % LANES, 1)
            packed = jnp.where(lane_group == g, last, packed)
        total[:, at] = packed
        return carry

    lax.fori_loop(0, blocks, block_in, 0)

    sums = []
    for d in range(1, peers):
        copy = pltpu.make_async_remote_copy(
            src_ref=total,
            dst_ref=totals.at[d - 1],
            send_sem=sum_send.at[d - 1],
            recv_sem=sum_recv.at[d - 1],
            device_id={"ctx": lax.rem(ctx + d, peers)},
            device_id_type=MESH,
        )
        copy.start()
        sums.append(copy)
    lax.fori_loop(0, left.shape[0], build, 0)
    for copy in sums:
        copy.wait()
    carried = jnp.zeros((MODES, channels), F32)
    for d in range(1, peers):
        weight = jnp.exp(rate_chan_ref[...] * (-float((d - 1) * tokens)))
        carried = carried + jnp.where(ctx >= d, weight * totals[d - 1], 0.0)
    total[...] = carried

    def block_out(v, carry):
        at = pl.ds(pl.multiple_of(v * LANES, LANES), LANES)
        incoming = total[:, at]
        for g in range(PACK):
            f = v * PACK + g
            entry = pltpu.roll(incoming, (LANES - g * GROUP) % LANES, 1)
            entry = jnp.concatenate([entry] * halves, axis=1)
            states = jnp.where(lane_wide < GROUP, entry, pltpu.roll(local[f], GROUP, 1))
            states = chunk_scan(
                states, jnp.concatenate([rate_ref[f]] * halves, axis=1), lane_wide
            )
            hi, lo = hi_lo(states)
            source[f, STEP : STEP + 3 * MODES, :] = jnp.concatenate([hi, hi, lo], axis=0).astype(
                BF16
            )
            out = jnp.dot(left[f], source[f], preferred_element_type=F32)
            result[g] = out + skip_ref[pl.ds(f, 1), :] * source[f, :STEP, :].astype(F32)

        def one_strip(s, inner):
            rows = pl.ds(pl.multiple_of(s * STRIP, STRIP), STRIP)
            for h in range(halves):
                parts = swapped(
                    [result[g, rows, h * LANES : (h + 1) * LANES] for g in range(PACK)],
                    lane_group,
                )
                for k in range(PACK):
                    here = pl.ds(
                        pl.multiple_of((h * PACK + k) * STEP + s * STRIP, STRIP), STRIP
                    )
                    mixed_ref[here, at] = (query[here, at] * parts[k]).astype(BF16)
            return inner

        lax.fori_loop(0, STEP // STRIP, one_strip, 0)
        return carry

    lax.fori_loop(0, blocks, block_out, 0)


def convolved(featurized, short_filter, decay_rate, residue, skip_gain):
    tokens, _, channels = featurized.shape
    filters = decay_rate.shape[0]
    chunks = tokens // STEP
    width = chunks * GROUP
    peers = lax.axis_size("ctx")
    scaled = residue * jnp.sqrt(-jnp.expm1(-2.0 * decay_rate))
    none = jnp.zeros((filters, LANES - 3 * MODES), F32)
    rate_row = jnp.concatenate([decay_rate] * 3 + [none], axis=1)
    scale_row = jnp.concatenate([scaled] * 3 + [none], axis=1)
    rate = jnp.broadcast_to(decay_rate[:, :, None], (filters, MODES, LANES))
    scale = jnp.broadcast_to(scaled[:, :, None], (filters, MODES, LANES))
    rate_chan = jnp.repeat(decay_rate.T, GROUP, axis=1)
    skip = jnp.tile(skip_gain.reshape(filters, GROUP), (1, chunks))
    vmem = pl.BlockSpec(memory_space=pltpu.VMEM)
    return pl.pallas_call(
        conv_kernel,
        out_shape=jax.ShapeDtypeStruct((tokens, channels), BF16),
        in_specs=[pl.BlockSpec(memory_space=pl.ANY)] + [vmem] * 7,
        out_specs=vmem,
        scratch_shapes=[
            pltpu.VMEM((3, tokens, channels), BF16),
            pltpu.VMEM((3, RIM, channels), BF16),
            pltpu.VMEM((chunks, STEP, LANES), F32),
            pltpu.VMEM((tokens, channels), F32),
            pltpu.VMEM((filters, 2 * STEP, width), BF16),
            pltpu.VMEM((filters, STEP, 2 * LANES), BF16),
            pltpu.VMEM((filters, MODES, width), F32),
            pltpu.VMEM((MODES, channels), F32),
            pltpu.VMEM((peers - 1, MODES, channels), F32),
            pltpu.VMEM((PACK, STEP, width), F32),
            pltpu.SemaphoreType.DMA((channels // LANES,)),
            pltpu.SemaphoreType.DMA((2,)),
            pltpu.SemaphoreType.DMA((peers - 1,)),
            pltpu.SemaphoreType.DMA((peers - 1,)),
        ],
        compiler_params=pltpu.CompilerParams(
            collective_id=0, has_side_effects=True, vmem_limit_bytes=48 * 2**20
        ),
        name="conv",
    )(
        featurized.transpose(1, 0, 2),
        short_filter,
        rate_row,
        scale_row,
        rate,
        scale,
        rate_chan,
        skip,
    )


TILE = 256


def project_kernel(
    mixed_hbm,
    weight_hbm,
    out_ref,
    mixed,
    weight,
    z_send,
    z_recv,
    far_send,
    far_recv,
    near_send,
    near_recv,
    far2_send,
    far2_recv,
    near2_send,
    near2_recv,
    turn_send,
    turn_recv,
    held,
    last_send,
    last_recv,
    load_sem,
    send_sem,
    recv_sem,
):
    depth = mixed_hbm.shape[1]
    cols = weight.shape[1]
    half = cols // 2
    quarter = cols // 4
    block = mixed_hbm.shape[0] // 4
    sub = block // 2
    own = sub // 2
    x = lax.axis_index("chan_0")
    z = lax.axis_index("chan_1")
    core = lax.axis_index("chan_2")
    right, far, lefts = lax.rem(x + 1, 4), lax.rem(x + 2, 4), lax.rem(x + 3, 4)
    to_right, to_left = {"chan_0": right}, {"chan_0": lefts}
    to_z, to_core = {"chan_1": 1 - z}, {"chan_2": 1 - core}
    order = (far, right, lefts, x)

    used = []

    def sent(src, dst, to):
        k = len(used)
        copy = pltpu.make_async_remote_copy(
            src_ref=src,
            dst_ref=dst,
            send_sem=send_sem.at[k],
            recv_sem=recv_sem.at[k],
            device_id=to,
            device_id_type=MESH,
        )
        copy.start()
        used.append(copy)
        return copy

    my_cols = pl.ds(pl.multiple_of(core * cols, cols), cols)
    other_cols = pl.ds(pl.multiple_of((1 - core) * cols, cols), cols)
    load = pltpu.make_async_copy(
        weight_hbm.at[:, my_cols], weight.at[pl.ds(0, depth), :], load_sem.at[0]
    )
    load.start()
    loads = []
    for k, at in enumerate(order):
        rows = pl.ds(pl.multiple_of(at * block, block), block)
        copy = pltpu.make_async_copy(
            mixed_hbm.at[rows, :], mixed.at[rows, pl.ds(0, depth)], load_sem.at[1 + k]
        )
        copy.start()
        loads.append(copy)

    barrier = pltpu.get_barrier_semaphore()
    for to in (to_right, to_left, to_z, to_core):
        pl.semaphore_signal(barrier, inc=1, device_id=to, device_id_type=MESH)
    pl.semaphore_wait(barrier, 4)

    passed = []
    for k, at in enumerate(order):
        rows = pl.ds(pl.multiple_of(at * block, block), block)
        if k == 1:
            weight_copy = sent(
                weight_hbm.at[:, other_cols], weight.at[pl.ds(depth, depth), :], to_core
            )
        passed.append(
            sent(mixed_hbm.at[rows, :], mixed.at[rows, pl.ds(depth, depth)], to_core)
        )

    def tiles(token, rows, first, count, store):
        wide = count // TILE

        def one(n, carry):
            i, j = n // wide, lax.rem(n, wide)
            r = pl.multiple_of(i * sub, sub)
            c = pl.multiple_of(j * TILE, TILE)
            value = jnp.dot(
                mixed[pl.ds(pl.multiple_of(token + r, sub), sub), :],
                weight[:, pl.ds(pl.multiple_of(first + c, TILE), TILE)],
                preferred_element_type=F32,
            )
            store(pl.ds(r, sub), pl.ds(c, TILE), value)
            return carry

        lax.fori_loop(0, (rows // sub) * wide, one, 0)

    def start_of(at):
        return at * block

    def plain(dst, extra=()):
        def store(r, c, value):
            for e in extra:
                value = value + e[r, c].astype(F32)
            dst[r, c] = value.astype(BF16)

        return store

    mine, others = z * sub, (1 - z) * sub

    def z_first(k):
        at = order[k]
        tiles(start_of(at) + others, sub, half, half, plain(z_send.at[k]))
        return sent(z_send.at[k], z_recv.at[k], to_z)

    load.wait()
    weight_copy.wait_recv()
    loads[0].wait()
    passed[0].wait_recv()
    zs = [z_first(0)]
    fars = []
    for s, to in ((0, to_right), (1, to_left)):
        tiles(start_of(far), block, s * quarter, quarter, plain(far_send.at[s]))
        fars.append(sent(far_send.at[s], far_recv.at[s], to))

    loads[1].wait()
    passed[1].wait_recv()
    zs.append(z_first(1))
    loads[2].wait()
    passed[2].wait_recv()
    zs.append(z_first(2))
    nears = {}
    for s, at, to in ((0, right, to_right), (1, lefts, to_left)):
        side = 1 - s
        tiles(start_of(at), block, side * quarter, quarter, plain(near_send.at[s, side]))
        nears[s, side] = sent(near_send.at[s, side], near_recv.at[s, side], to)
    loads[3].wait()
    passed[3].wait_recv()
    zs.append(z_first(3))
    for s, at, to in ((0, right, to_right), (1, lefts, to_left)):
        fars[s].wait_recv()
        tiles(
            start_of(at), block, s * quarter, quarter, plain(near_send.at[s, s], (far_recv.at[s],))
        )
        nears[s, s] = sent(near_send.at[s, s], near_recv.at[s, s], to)

    zs[0].wait_recv()
    fars2 = []
    for s, to in ((0, to_right), (1, to_left)):
        at = pl.ds(s * quarter, quarter)
        tiles(
            start_of(far) + mine,
            sub,
            half + s * quarter,
            quarter,
            plain(far2_send.at[s], (z_recv.at[0, :, at],)),
        )
        fars2.append(sent(far2_send.at[s], far2_recv.at[s], to))
    nears2 = {}
    for s, at, to in ((0, right, to_right), (1, lefts, to_left)):
        zs[1 + s].wait_recv()
        side = 1 - s
        piece = pl.ds(side * quarter, quarter)
        tiles(
            start_of(at) + mine,
            sub,
            half + side * quarter,
            quarter,
            plain(near2_send.at[s, side], (z_recv.at[1 + s, :, piece],)),
        )
        nears2[s, side] = sent(near2_send.at[s, side], near2_recv.at[s, side], to)
    for s, at, to in ((0, right, to_right), (1, lefts, to_left)):
        fars2[s].wait_recv()
        piece = pl.ds(s * quarter, quarter)
        tiles(
            start_of(at) + mine,
            sub,
            half + s * quarter,
            quarter,
            plain(near2_send.at[s, s], (z_recv.at[1 + s, :, piece], far2_recv.at[s])),
        )
        nears2[s, s] = sent(near2_send.at[s, s], near2_recv.at[s, s], to)

    for copy in nears.values():
        copy.wait_recv()
    for side in (0, 1):
        piece = pl.ds(side * quarter, quarter)
        away = pl.ds(pl.multiple_of(others, sub), sub)
        tiles(
            start_of(x) + others,
            sub,
            side * quarter,
            quarter,
            plain(
                turn_send.at[:, piece],
                (near_recv.at[0, side, away], near_recv.at[1, side, away]),
            ),
        )
    turn = sent(turn_send, turn_recv, to_z)

    def kept(offset, extra):
        def store(r, c, value):
            for e in extra:
                value = value + e[r, c].astype(F32)
            held[r, pl.ds(pl.multiple_of(offset + c.start, TILE), TILE)] = value

        return store

    for side in (0, 1):
        here = pl.ds(pl.multiple_of(mine, sub), sub)
        tiles(
            start_of(x) + mine,
            sub,
            side * quarter,
            quarter,
            kept(side * quarter, (near_recv.at[0, side, here], near_recv.at[1, side, here])),
        )
    zs[3].wait_recv()
    for copy in nears2.values():
        copy.wait_recv()
    for side in (0, 1):
        piece = pl.ds(side * quarter, quarter)
        tiles(
            start_of(x) + mine,
            sub,
            half + side * quarter,
            quarter,
            kept(
                half + side * quarter,
                (z_recv.at[3, :, piece], near2_recv.at[0, side], near2_recv.at[1, side]),
            ),
        )
    my_rows = pl.ds(pl.multiple_of(core * own, own), own)
    other_rows = pl.ds(pl.multiple_of((1 - core) * own, own), own)
    second = pl.ds(half, half)
    last_send[1] = held[other_rows, second].astype(BF16)
    lasts = [sent(last_send.at[1], last_recv.at[1], to_core)]
    out_ref[:, pl.ds(pl.multiple_of(core * cols + half, half), half)] = held[
        my_rows, second
    ].astype(BF16)
    turn.wait_recv()
    first = pl.ds(0, half)
    last_send[0] = (held[other_rows, first] + turn_recv[other_rows, :].astype(F32)).astype(BF16)
    lasts.append(sent(last_send.at[0], last_recv.at[0], to_core))
    out_ref[:, pl.ds(pl.multiple_of(core * cols, half), half)] = (
        held[my_rows, first] + turn_recv[my_rows, :].astype(F32)
    ).astype(BF16)
    for s, copy in ((1, lasts[0]), (0, lasts[1])):
        copy.wait_recv()
        out_ref[:, pl.ds(pl.multiple_of((1 - core) * cols + s * half, half), half)] = last_recv[s]
    for copy in used:
        copy.wait_send()


COPIES = 24


def projected(mixed, weight):
    tokens, depth = mixed.shape
    outs = weight.shape[1]
    cols = outs // 2
    half, quarter = cols // 2, cols // 4
    block = tokens // 4
    sub = block // 2
    own = sub // 2
    anywhere = pl.BlockSpec(memory_space=pl.ANY)
    pairs = [
        (4, sub, half),
        (2, block, quarter),
        (2, 2, block, quarter),
        (2, sub, quarter),
        (2, 2, sub, quarter),
        (sub, half),
    ]
    return pl.pallas_call(
        project_kernel,
        out_shape=jax.ShapeDtypeStruct((own, outs), BF16),
        in_specs=[anywhere, anywhere],
        out_specs=pl.BlockSpec(memory_space=pltpu.VMEM),
        scratch_shapes=[
            pltpu.VMEM((tokens, 2 * depth), BF16),
            pltpu.VMEM((2 * depth, cols), BF16),
        ]
        + [pltpu.VMEM(shape, BF16) for shape in pairs for _ in range(2)]
        + [
            pltpu.VMEM((sub, cols), F32),
            pltpu.VMEM((2, own, half), BF16),
            pltpu.VMEM((2, own, half), BF16),
            pltpu.SemaphoreType.DMA((5,)),
            pltpu.SemaphoreType.DMA((COPIES,)),
            pltpu.SemaphoreType.DMA((COPIES,)),
        ],
        compiler_params=pltpu.CompilerParams(
            collective_id=1, has_side_effects=True, vmem_limit_bytes=56 * 2**20
        ),
        name="project",
    )(mixed, weight)


def on_device(featurized, short_filter, decay_rate, residue, skip_gain, out_weight):
    mixed = convolved(featurized, short_filter, decay_rate, residue, skip_gain)
    return projected(mixed, out_weight)


def solution(mesh):
    finer = Mesh(
        mesh.devices.reshape(mesh.shape["ctx"], 4, 2, 2), ("ctx", "chan_0", "chan_1", "chan_2")
    )
    placed = (
        P("ctx", None, CHAN),
        P(None, None, CHAN),
        P(CHAN, None),
        P(CHAN, None),
        P(CHAN),
        P(CHAN, None),
    )
    return jax.shard_map(
        on_device, mesh=finer, in_specs=placed, out_specs=P(CTX_CHAN, None), check_vma=False
    )
```

```python
import jax
import jax.numpy as jnp
from jax import lax
from jax.experimental import pallas as pl
from jax.experimental.pallas import tpu as pltpu
from jax.sharding import Mesh
from jax.sharding import PartitionSpec as P

CHAN = ("chan_0", "chan_1", "chan_2")
CTX_CHAN = ("ctx", "chan_0", "chan_1", "chan_2")
MESH = pl.DeviceIdType.MESH
F32 = jnp.float32
BF16 = jnp.bfloat16
LANES = 128
TILE = 256
COPIES = 24
STEP = 128
GROUP = 16
PACK = LANES // GROUP
MODES = 16
STRIP = 64
RIM = 16


def swapped(parts, lane_group):
    parts = list(parts)
    for bit in (1, 2, 4):
        low = (lane_group & bit) == 0
        for k in range(PACK):
            if k & bit == 0:
                a, b = parts[k], parts[k | bit]
                parts[k] = jnp.where(low, a, pltpu.roll(b, bit * GROUP, 1))
                parts[k | bit] = jnp.where(low, pltpu.roll(a, LANES - bit * GROUP, 1), b)
    return parts


def hi_lo(value):
    hi = value.astype(BF16).astype(F32)
    return hi, value - hi


def one_less_exp(x):
    series = jnp.ones_like(x)
    for n in range(9, 1, -1):
        series = 1.0 - x * (1.0 / n) * series
    return jnp.where(x < 0.5, x * series, 1.0 - jnp.exp(-x))


def chunk_scan(state, rate, lane):
    width = state.shape[1]
    hop = 1
    while hop * GROUP < width:
        decay = jnp.exp(rate * (-float(hop * STEP)))
        moved = pltpu.roll(state, hop * GROUP, 1)
        state = state + jnp.where(lane >= hop * GROUP, decay * moved, 0.0)
        hop *= 2
    return state


def kernel(
    feat_hbm,
    taps_hbm,
    rate_hbm,
    residue_hbm,
    skip_hbm,
    weight_hbm,
    out_ref,
    feat,
    taps,
    rate_in,
    residue_in,
    skip_in,
    skip,
    square,
    rate_row,
    scale_row,
    rates,
    scales,
    rim,
    gated,
    query,
    source,
    left,
    local,
    total,
    totals,
    result,
    mixed,
    weight,
    z_send,
    z_recv,
    far_send,
    far_recv,
    near_send,
    near_recv,
    far2_send,
    far2_recv,
    near2_send,
    near2_recv,
    turn_send,
    turn_recv,
    held,
    last_send,
    last_recv,
    small_sem,
    load_sem,
    rim_sem,
    sum_send,
    sum_recv,
    send_sem,
    recv_sem,
):
    tokens, channels = feat.shape[1], feat.shape[2]
    filters = rates.shape[0]
    chunks = tokens // STEP
    blocks = channels // LANES
    width = chunks * GROUP
    halves = width // LANES
    depth = channels
    cols = weight.shape[1]
    half = cols // 2
    quarter = cols // 4
    block = tokens // 4
    sub = block // 2
    own = sub // 2
    ctx = lax.axis_index("ctx")
    peers = lax.axis_size("ctx")
    x = lax.axis_index("chan_0")
    z = lax.axis_index("chan_1")
    core = lax.axis_index("chan_2")
    right, far, lefts = lax.rem(x + 1, 4), lax.rem(x + 2, 4), lax.rem(x + 3, 4)
    to_right, to_left = {"chan_0": right}, {"chan_0": lefts}
    to_z, to_core = {"chan_1": 1 - z}, {"chan_2": 1 - core}

    smalls = []
    for k, (here, there) in enumerate(
        (
            (rate_hbm, rate_in),
            (residue_hbm, residue_in),
            (taps_hbm, taps),
            (skip_hbm, skip_in),
        )
    ):
        copy = pltpu.make_async_copy(here, there, small_sem.at[k])
        copy.start()
        smalls.append(copy)

    def load_of(v):
        at = pl.ds(pl.multiple_of(v * LANES, LANES), LANES)
        return pltpu.make_async_copy(feat_hbm.at[:, :, at], feat.at[:, :, at], load_sem.at[v])

    for v in range(blocks):
        load_of(v).start()
    my_cols = pl.ds(pl.multiple_of(core * cols, cols), cols)
    other_cols = pl.ds(pl.multiple_of((1 - core) * cols, cols), cols)
    load_weight = pltpu.make_async_copy(
        weight_hbm.at[:, my_cols], weight.at[pl.ds(0, depth), :], load_sem.at[blocks]
    )
    load_weight.start()

    barrier = pltpu.get_barrier_semaphore()
    greeted = [{"ctx": lax.rem(ctx + d, peers)} for d in range(1, peers)]
    greeted += [to_right, to_left, to_z, to_core]
    for to in greeted:
        pl.semaphore_signal(barrier, inc=1, device_id=to, device_id_type=MESH)

    lane = lax.broadcasted_iota(jnp.int32, (1, LANES), 1)
    lane_group = lane // GROUP
    lane_wide = lax.broadcasted_iota(jnp.int32, (MODES, width), 1)
    lane_mode = lax.broadcasted_iota(jnp.int32, (MODES, LANES), 1)
    row = lax.broadcasted_iota(jnp.int32, (STEP, LANES), 0)
    col = lax.broadcasted_iota(jnp.int32, (STEP, LANES), 1)
    after = (row + 1).astype(F32)
    back = lax.rem(STEP - lane_mode, STEP).astype(F32)
    ahead = (STEP - 1 - lane_mode).astype(F32)

    for copy in smalls:
        copy.wait()
    rate_all = rate_in[...]
    scale_all = residue_in[...] * jnp.sqrt(one_less_exp(2.0 * rate_all))
    for f in range(filters):
        rates[f] = jnp.broadcast_to(rate_all[:, f : f + 1], (MODES, LANES))
        scales[f] = jnp.broadcast_to(scale_all[:, f : f + 1], (MODES, LANES))
    square[...] = jnp.zeros_like(square)
    for k in range(3):
        square[k * MODES : (k + 1) * MODES, 0:filters] = rate_all
    rate_row[...] = square[...].T[:filters]
    for k in range(3):
        square[k * MODES : (k + 1) * MODES, 0:filters] = scale_all
    scale_row[...] = square[...].T[:filters]
    skip[...] = skip_in[...].reshape(1, channels)
    source[:, STEP + 3 * MODES :, :] = jnp.zeros(
        (filters, source.shape[1] - STEP - 3 * MODES, width), BF16
    )

    def gate(v, c, earlier_of):
        at = pl.ds(pl.multiple_of(v * LANES, LANES), LANES)
        here = pl.ds(pl.multiple_of(c * STEP, STEP), STEP)
        parts = []
        for i in range(3):
            rows = jnp.concatenate(
                [earlier_of(i, at).astype(F32), feat[i, here, at].astype(F32)], axis=0
            )
            tap = taps[:, i, at]
            value = (
                tap[0:1] * rows[RIM:]
                + tap[1:2] * pltpu.roll(rows, 1, 0)[RIM:]
                + tap[2:3] * pltpu.roll(rows, 2, 0)[RIM:]
            )
            parts.append(value)
        query[here, at] = parts[0].astype(BF16)
        gated[here, at] = (parts[1] * parts[2]).astype(BF16)

    def gate_block(v, carry):
        load_of(v).wait()

        def one_chunk(c, inner):
            before = pl.ds(pl.multiple_of(c * STEP - RIM, RIM), RIM)
            gate(v, c, lambda i, at: feat[i, before, at])
            return inner

        lax.fori_loop(1, chunks, one_chunk, 0)
        return carry

    def gate_first(v, carry):
        gate(v, 0, lambda i, at: jnp.where(ctx > 0, rim[i, :, at].astype(F32), 0.0))
        return carry

    def swap_in(v, h):
        at = pl.ds(pl.multiple_of(v * LANES, LANES), LANES)

        def one_strip(s, inner):
            rows = pl.ds(pl.multiple_of(s * STRIP, STRIP), STRIP)
            parts = []
            for k in range(PACK):
                here = pl.ds(pl.multiple_of((h * PACK + k) * STEP + s * STRIP, STRIP), STRIP)
                parts.append(gated[here, at])
            for g, part in enumerate(swapped(parts, lane_group)):
                source[v * PACK + g, rows, h * LANES : (h + 1) * LANES] = part
            return inner

        lax.fori_loop(0, STEP // STRIP, one_strip, 0)

    lax.fori_loop(0, blocks // 2, gate_block, 0)

    with jax.named_scope("c_barrier"):
        pl.semaphore_wait(barrier, len(greeted))
    rim_copy = pltpu.make_async_remote_copy(
        src_ref=feat_hbm.at[:, pl.ds(tokens - RIM, RIM), :],
        dst_ref=rim,
        send_sem=rim_sem.at[0],
        recv_sem=rim_sem.at[1],
        device_id={"ctx": lax.rem(ctx + 1, peers)},
        device_id_type=MESH,
    )
    rim_copy.start()
    used = []

    def sent(src, dst, to):
        k = len(used)
        copy = pltpu.make_async_remote_copy(
            src_ref=src,
            dst_ref=dst,
            send_sem=send_sem.at[k],
            recv_sem=recv_sem.at[k],
            device_id=to,
            device_id_type=MESH,
        )
        copy.start()
        used.append(copy)
        return copy

    weight_copy = sent(weight_hbm.at[:, other_cols], weight.at[pl.ds(depth, depth), :], to_core)

    lax.fori_loop(blocks // 2, blocks, gate_block, 0)

    def swap_later(v, carry):
        for h in range(1, halves):
            swap_in(v, h)
        return carry

    lax.fori_loop(0, blocks, swap_later, 0)
    with jax.named_scope("c_rim"):
        rim_copy.wait()
    lax.fori_loop(0, blocks, gate_first, 0)

    def state_block(v, carry):
        at = pl.ds(pl.multiple_of(v * LANES, LANES), LANES)
        swap_in(v, 0)
        packed = jnp.zeros((MODES, LANES), F32)
        for g in range(PACK):
            f = v * PACK + g
            rate = rates[f]
            hi, lo = hi_lo(jnp.exp(-rate * ahead))
            factor = jnp.concatenate([hi, lo], axis=0).astype(BF16)
            product = jnp.dot(factor, source[f, :STEP, :], preferred_element_type=F32)
            ends = product[:MODES] + product[MODES:]
            local[f] = ends
            summed = chunk_scan(ends, jnp.concatenate([rate] * halves, axis=1), lane_wide)
            last = summed[:, width - LANES :]
            last = pltpu.roll(last, (g * GROUP + GROUP) % LANES, 1)
            packed = jnp.where(lane_group == g, last, packed)
        total[:, at] = packed
        return carry

    lax.fori_loop(0, blocks, state_block, 0)

    sums = []
    for d in range(1, peers):
        copy = pltpu.make_async_remote_copy(
            src_ref=total,
            dst_ref=totals.at[d - 1],
            send_sem=sum_send.at[d - 1],
            recv_sem=sum_recv.at[d - 1],
            device_id={"ctx": lax.rem(ctx + d, peers)},
            device_id_type=MESH,
        )
        copy.start()
        sums.append(copy)

    def build(f, carry):
        first = jnp.sum(scales[f] * jnp.exp(-rates[f] * back), axis=0, keepdims=True)
        turned = pltpu.roll(
            jnp.broadcast_to(first, (STEP, LANES)), 0, 1, stride=1, stride_axis=0
        )
        left[f, :, :LANES] = jnp.where(col <= row, turned, 0.0).astype(BF16)
        hi, lo = hi_lo(scale_row[pl.ds(f, 1), :] * jnp.exp(-rate_row[pl.ds(f, 1), :] * after))
        second = (col >= MODES) & (col < 2 * MODES)
        left[f, :, LANES:] = jnp.where(second, lo, hi).astype(BF16)
        return carry

    with jax.named_scope("c_build"):
        lax.fori_loop(0, filters, build, 0)
    with jax.named_scope("c_sums"):
        for copy in sums:
            copy.wait()
    for v in range(blocks):
        at = pl.ds(v * LANES, LANES)
        chan_rate = rates[v * PACK]
        for g in range(1, PACK):
            chan_rate = jnp.where(lane_group == g, rates[v * PACK + g], chan_rate)
        carried = jnp.zeros((MODES, LANES), F32)
        for d in range(1, peers):
            decay = jnp.exp(chan_rate * (-float((d - 1) * tokens)))
            carried = carried + jnp.where(ctx >= d, decay * totals[d - 1, :, at], 0.0)
        total[:, at] = carried

    def state_rows(v, carry):
        at = pl.ds(pl.multiple_of(v * LANES, LANES), LANES)
        incoming = total[:, at]
        for g in range(PACK):
            f = v * PACK + g
            entry = pltpu.roll(incoming, (LANES - g * GROUP) % LANES, 1)
            entry = jnp.concatenate([entry] * halves, axis=1)
            states = jnp.where(lane_wide < GROUP, entry, pltpu.roll(local[f], GROUP, 1))
            states = chunk_scan(
                states, jnp.concatenate([rates[f]] * halves, axis=1), lane_wide
            )
            hi, lo = hi_lo(states)
            source[f, STEP : STEP + 3 * MODES, :] = jnp.concatenate([hi, hi, lo], axis=0).astype(
                BF16
            )
        return carry

    with jax.named_scope("c_states"):
        lax.fori_loop(0, blocks, state_rows, 0)

    def block_out(h):
        def one_block(v, carry):
            at = pl.ds(pl.multiple_of(v * LANES, LANES), LANES)
            wide = pl.ds(pl.multiple_of(h * LANES, LANES), LANES)
            for g in range(PACK):
                f = v * PACK + g
                result[g] = jnp.dot(
                    left[f], source[f, :, wide], preferred_element_type=F32
                ).astype(BF16)

            def one_strip(s, inner):
                rows = pl.ds(pl.multiple_of(s * STRIP, STRIP), STRIP)
                parts = swapped([result[g, rows, :] for g in range(PACK)], lane_group)
                for k in range(PACK):
                    here = pl.ds(
                        pl.multiple_of((h * PACK + k) * STEP + s * STRIP, STRIP), STRIP
                    )
                    value = parts[k].astype(F32) + skip[:, at] * gated[here, at].astype(F32)
                    mixed[here, at] = (query[here, at].astype(F32) * value).astype(BF16)
                return inner

            lax.fori_loop(0, STEP // STRIP, one_strip, 0)
            return carry

        return one_block

    def passed_on(at):
        rows = pl.ds(pl.multiple_of(at * block, block), block)
        return sent(
            mixed.at[rows, pl.ds(0, depth)], mixed.at[rows, pl.ds(depth, depth)], to_core
        )

    first_half = far // 2
    with jax.named_scope("c_half1"):
        lax.fori_loop(0, blocks, block_out(first_half), 0)
    passed = [passed_on(far), passed_on(far + 1 - 2 * lax.rem(far, 2))]
    lax.fori_loop(0, 1, block_out(1 - first_half), 0)

    def tiles(token, rows, first, count, store):
        wide = count // TILE

        def one(n, carry):
            i, j = n // wide, lax.rem(n, wide)
            r = pl.multiple_of(i * sub, sub)
            c = pl.multiple_of(j * TILE, TILE)
            value = jnp.dot(
                mixed[pl.ds(pl.multiple_of(token + r, sub), sub), :],
                weight[:, pl.ds(pl.multiple_of(first + c, TILE), TILE)],
                preferred_element_type=F32,
            )
            store(pl.ds(r, sub), pl.ds(c, TILE), value)
            return carry

        lax.fori_loop(0, (rows // sub) * wide, one, 0)

    def start_of(at):
        return at * block

    def plain(dst, extra=()):
        def store(r, c, value):
            for e in extra:
                value = value + e[r, c].astype(F32)
            dst[r, c] = value.astype(BF16)

        return store

    mine, others = z * sub, (1 - z) * sub
    order = (far, right, lefts, x)

    def z_first(k):
        at = order[k]
        tiles(start_of(at) + others, sub, half, half, plain(z_send.at[k]))
        return sent(z_send.at[k], z_recv.at[k], to_z)

    with jax.named_scope("c_w_start"):
        load_weight.wait()
        weight_copy.wait_recv()
        passed[0].wait_recv()
    zs = [z_first(0)]
    fars = []
    for s, to in ((0, to_right), (1, to_left)):
        tiles(start_of(far), block, s * quarter, quarter, plain(far_send.at[s]))
        fars.append(sent(far_send.at[s], far_recv.at[s], to))

    with jax.named_scope("c_half2"):
        lax.fori_loop(1, blocks, block_out(1 - first_half), 0)
    passed += [passed_on(x + 1 - 2 * lax.rem(x, 2)), passed_on(x)]
    with jax.named_scope("c_w_passed"):
        for copy in passed[1:]:
            copy.wait_recv()
    zs.append(z_first(1))
    sides = ((0, right, to_right), (1, lefts, to_left))
    nears = {}
    for s, at, to in sides:
        side = 1 - s
        tiles(start_of(at), block, side * quarter, quarter, plain(near_send.at[s, side]))
        nears[s, side] = sent(near_send.at[s, side], near_recv.at[s, side], to)
    zs.append(z_first(2))
    zs.append(z_first(3))

    with jax.named_scope("c_w_z0"):
        zs[0].wait_recv()
    fars2 = []
    for s, to in ((0, to_right), (1, to_left)):
        at = pl.ds(s * quarter, quarter)
        tiles(
            start_of(far) + mine,
            sub,
            half + s * quarter,
            quarter,
            plain(far2_send.at[s], (z_recv.at[0, :, at],)),
        )
        fars2.append(sent(far2_send.at[s], far2_recv.at[s], to))
    for s, at, to in sides:
        with jax.named_scope("c_w_far"):
            fars[s].wait_recv()
        tiles(
            start_of(at), block, s * quarter, quarter, plain(near_send.at[s, s], (far_recv.at[s],))
        )
        nears[s, s] = sent(near_send.at[s, s], near_recv.at[s, s], to)

    nears2 = {}
    for s, at, to in sides:
        with jax.named_scope("c_w_z12"):
            zs[1 + s].wait_recv()
        side = 1 - s
        piece = pl.ds(side * quarter, quarter)
        tiles(
            start_of(at) + mine,
            sub,
            half + side * quarter,
            quarter,
            plain(near2_send.at[s, side], (z_recv.at[1 + s, :, piece],)),
        )
        nears2[s, side] = sent(near2_send.at[s, side], near2_recv.at[s, side], to)
    for s, at, to in sides:
        with jax.named_scope("c_w_far2"):
            fars2[s].wait_recv()
        piece = pl.ds(s * quarter, quarter)
        tiles(
            start_of(at) + mine,
            sub,
            half + s * quarter,
            quarter,
            plain(near2_send.at[s, s], (z_recv.at[1 + s, :, piece], far2_recv.at[s])),
        )
        nears2[s, s] = sent(near2_send.at[s, s], near2_recv.at[s, s], to)

    with jax.named_scope("c_w_near"):
        for copy in nears.values():
            copy.wait_recv()
    for side in (0, 1):
        piece = pl.ds(side * quarter, quarter)
        away = pl.ds(pl.multiple_of(others, sub), sub)
        tiles(
            start_of(x) + others,
            sub,
            side * quarter,
            quarter,
            plain(
                turn_send.at[:, piece],
                (near_recv.at[0, side, away], near_recv.at[1, side, away]),
            ),
        )
    turn = sent(turn_send, turn_recv, to_z)

    def kept(offset, extra):
        def store(r, c, value):
            for e in extra:
                value = value + e[r, c].astype(F32)
            held[r, pl.ds(pl.multiple_of(offset + c.start, TILE), TILE)] = value

        return store

    for side in (0, 1):
        here = pl.ds(pl.multiple_of(mine, sub), sub)
        tiles(
            start_of(x) + mine,
            sub,
            side * quarter,
            quarter,
            kept(side * quarter, (near_recv.at[0, side, here], near_recv.at[1, side, here])),
        )
    with jax.named_scope("c_w_z3"):
        zs[3].wait_recv()
    for side in (0, 1):
        piece = pl.ds(side * quarter, quarter)
        tiles(
            start_of(x) + mine,
            sub,
            half + side * quarter,
            quarter,
            kept(half + side * quarter, (z_recv.at[3, :, piece],)),
        )
    my_rows = pl.ds(pl.multiple_of(core * own, own), own)
    other_rows = pl.ds(pl.multiple_of((1 - core) * own, own), own)
    my_first = pl.multiple_of(core * cols, cols)
    with jax.named_scope("c_w_near2"):
        for copy in nears2.values():
            copy.wait_recv()
    for rows, keep in ((other_rows, False), (my_rows, True)):
        for side in (0, 1):
            at = pl.ds(half + side * quarter, quarter)
            value = (
                held[rows, at]
                + near2_recv[0, side, rows, :].astype(F32)
                + near2_recv[1, side, rows, :].astype(F32)
            ).astype(BF16)
            if keep:
                out_ref[:, pl.ds(my_first + half + side * quarter, quarter)] = value
            else:
                last_send[1, :, side * quarter : (side + 1) * quarter] = value
        if not keep:
            lasts = [sent(last_send.at[1], last_recv.at[1], to_core)]
    with jax.named_scope("c_w_turn"):
        turn.wait_recv()
    first = pl.ds(0, half)
    last_send[0] = (held[other_rows, first] + turn_recv[other_rows, :].astype(F32)).astype(BF16)
    lasts.append(sent(last_send.at[0], last_recv.at[0], to_core))
    out_ref[:, pl.ds(my_first, half)] = (
        held[my_rows, first] + turn_recv[my_rows, :].astype(F32)
    ).astype(BF16)
    for s, copy in ((1, lasts[0]), (0, lasts[1])):
        with jax.named_scope("c_w_last"):
            copy.wait_recv()
        out_ref[:, pl.ds(pl.multiple_of((1 - core) * cols + s * half, half), half)] = last_recv[s]
    for copy in used:
        copy.wait_send()


def on_device(featurized, short_filter, decay_rate, residue, skip_gain, weight):
    tokens, _, channels = featurized.shape
    filters = decay_rate.shape[0]
    peers = lax.axis_size("ctx")
    chunks = tokens // STEP
    width = chunks * GROUP
    outs = weight.shape[1]
    cols = outs // 2
    half, quarter = cols // 2, cols // 4
    block = tokens // 4
    sub = block // 2
    own = sub // 2
    pairs = [
        (4, sub, half),
        (2, block, quarter),
        (2, 2, block, quarter),
        (2, sub, quarter),
        (2, 2, sub, quarter),
        (sub, half),
    ]
    return pl.pallas_call(
        kernel,
        out_shape=jax.ShapeDtypeStruct((own, outs), BF16),
        in_specs=[pl.BlockSpec(memory_space=pl.ANY)] * 6,
        out_specs=pl.BlockSpec(memory_space=pltpu.VMEM),
        scratch_shapes=[
            pltpu.VMEM((3, tokens, channels), BF16),
            pltpu.VMEM(short_filter.shape, F32),
            pltpu.VMEM((MODES, filters), F32),
            pltpu.VMEM((MODES, filters), F32),
            pltpu.VMEM((channels,), F32),
            pltpu.VMEM((1, channels), F32),
            pltpu.VMEM((LANES, LANES), F32),
            pltpu.VMEM((filters, LANES), F32),
            pltpu.VMEM((filters, LANES), F32),
            pltpu.VMEM((filters, MODES, LANES), F32),
            pltpu.VMEM((filters, MODES, LANES), F32),
            pltpu.VMEM((3, RIM, channels), BF16),
            pltpu.VMEM((tokens, channels), BF16),
            pltpu.VMEM((tokens, channels), BF16),
            pltpu.VMEM((filters, 2 * STEP, width), BF16),
            pltpu.VMEM((filters, STEP, 2 * LANES), BF16),
            pltpu.VMEM((filters, MODES, width), F32),
            pltpu.VMEM((MODES, channels), F32),
            pltpu.VMEM((peers - 1, MODES, channels), F32),
            pltpu.VMEM((PACK, STEP, LANES), BF16),
            pltpu.VMEM((tokens, 2 * channels), BF16),
            pltpu.VMEM((2 * channels, cols), BF16),
        ]
        + [pltpu.VMEM(shape, BF16) for shape in pairs for _ in range(2)]
        + [
            pltpu.VMEM((sub, cols), F32),
            pltpu.VMEM((2, own, half), BF16),
            pltpu.VMEM((2, own, half), BF16),
            pltpu.SemaphoreType.DMA((4,)),
            pltpu.SemaphoreType.DMA((channels // LANES + 1,)),
            pltpu.SemaphoreType.DMA((2,)),
            pltpu.SemaphoreType.DMA((peers - 1,)),
            pltpu.SemaphoreType.DMA((peers - 1,)),
            pltpu.SemaphoreType.DMA((COPIES,)),
            pltpu.SemaphoreType.DMA((COPIES,)),
        ],
        compiler_params=pltpu.CompilerParams(
            collective_id=0, has_side_effects=True, vmem_limit_bytes=60 * 2**20
        ),
        name="hyena",
    )(
        featurized.transpose(1, 0, 2),
        short_filter,
        decay_rate.T,
        residue.T,
        skip_gain,
        weight,
    )


def solution(mesh):
    finer = Mesh(
        mesh.devices.reshape(mesh.shape["ctx"], 4, 2, 2), ("ctx", "chan_0", "chan_1", "chan_2")
    )
    placed = (
        P("ctx", None, CHAN),
        P(None, None, CHAN),
        P(CHAN, None),
        P(CHAN, None),
        P(CHAN),
        P(CHAN, None),
    )
    return jax.shard_map(
        on_device, mesh=finer, in_specs=placed, out_specs=P(CTX_CHAN, None), check_vma=False
    )
```

```python
import jax
import jax.numpy as jnp
from jax import lax
from jax.experimental import pallas as pl
from jax.experimental.pallas import tpu as pltpu
from jax.sharding import Mesh
from jax.sharding import PartitionSpec as P

CHAN = ("chan_0", "chan_1", "chan_2")
CTX_CHAN = ("ctx", "chan_0", "chan_1", "chan_2")
MESH = pl.DeviceIdType.MESH
F32 = jnp.float32
BF16 = jnp.bfloat16
LANES = 128
TILE = 256
COPIES = 25
STEP = 128
GROUP = 16
PACK = LANES // GROUP
MODES = 16
STRIP = 64
RIM = 16


def turned_to(parts, lane_group, sign):
    for bit in (1, 2, 4):
        move = (lane_group & bit) != 0
        parts = [
            jnp.where(move, parts[(k + sign * bit) % PACK], parts[k]) for k in range(PACK)
        ]
    return parts


def by_filter(parts, lane_group):
    parts = [pltpu.roll(part, k * GROUP, 1) if k else part for k, part in enumerate(parts)]
    parts = turned_to(parts, lane_group, 1)
    return [parts[-g % PACK] for g in range(PACK)]


def by_chunk(parts, lane_group):
    parts = turned_to([parts[-k % PACK] for k in range(PACK)], lane_group, -1)
    return [pltpu.roll(part, LANES - k * GROUP, 1) if k else part for k, part in enumerate(parts)]


def hi_lo(value):
    hi = value.astype(BF16).astype(F32)
    return hi, value - hi


def one_less_exp(x):
    series = jnp.ones_like(x)
    for n in range(9, 1, -1):
        series = 1.0 - x * (1.0 / n) * series
    return jnp.where(x < 0.5, x * series, 1.0 - jnp.exp(-x))


def chunk_scan(low, high, rate, place):
    for hop in (1, 2, 4):
        decay = jnp.exp(rate * (-float(hop * STEP)))
        inside = place >= hop
        a, b = pltpu.roll(low, hop * GROUP, 1), pltpu.roll(high, hop * GROUP, 1)
        low, high = (
            low + decay * jnp.where(inside, a, 0.0),
            high + decay * jnp.where(inside, b, a),
        )
    return low, high + jnp.exp(rate * (-float(PACK * STEP))) * low


def kernel(
    feat_hbm,
    taps_hbm,
    rate_hbm,
    residue_hbm,
    skip_hbm,
    weight_hbm,
    out_ref,
    feat,
    taps,
    rate_in,
    residue_in,
    skip_in,
    skip,
    square,
    rate_row,
    scale_row,
    rates,
    scales,
    rim,
    gated,
    query,
    source,
    left,
    local,
    chan_rates,
    amend,
    total,
    totals,
    result,
    mixed,
    weight,
    z_send,
    z_recv,
    far_send,
    far_recv,
    near_send,
    near_recv,
    far2_send,
    far2_recv,
    near2_send,
    near2_recv,
    turn_send,
    turn_recv,
    held,
    last_send,
    last_recv,
    small_sem,
    load_sem,
    rim_sem,
    sum_send,
    sum_recv,
    send_sem,
    recv_sem,
):
    tokens, channels = feat.shape[1], feat.shape[2]
    filters = rates.shape[0]
    chunks = tokens // STEP
    blocks = channels // LANES
    width = chunks * GROUP
    halves = width // LANES
    depth = channels
    cols = weight.shape[1]
    half = cols // 2
    quarter = cols // 4
    block = tokens // 4
    sub = block // 2
    own = sub // 2
    ctx = lax.axis_index("ctx")
    peers = lax.axis_size("ctx")
    x = lax.axis_index("chan_0")
    z = lax.axis_index("chan_1")
    core = lax.axis_index("chan_2")
    right, far, lefts = lax.rem(x + 1, 4), lax.rem(x + 2, 4), lax.rem(x + 3, 4)
    to_right, to_left = {"chan_0": right}, {"chan_0": lefts}
    to_z, to_core = {"chan_1": 1 - z}, {"chan_2": 1 - core}
    to_both = {"chan_1": 1 - z, "chan_2": 1 - core}

    smalls = []
    for k, (here, there) in enumerate(
        (
            (rate_hbm, rate_in),
            (residue_hbm, residue_in),
            (taps_hbm, taps),
            (skip_hbm, skip_in),
        )
    ):
        copy = pltpu.make_async_copy(here, there, small_sem.at[k])
        copy.start()
        smalls.append(copy)

    def load_of(v):
        at = pl.ds(pl.multiple_of(v * LANES, LANES), LANES)
        return pltpu.make_async_copy(feat_hbm.at[:, :, at], feat.at[:, :, at], load_sem.at[v])

    for v in range(blocks):
        load_of(v).start()
    my_cols = pl.ds(pl.multiple_of(core * cols, cols), cols)
    other_cols = pl.ds(pl.multiple_of((1 - core) * cols, cols), cols)
    load_weight = pltpu.make_async_copy(
        weight_hbm.at[:, my_cols], weight.at[pl.ds(0, depth), :], load_sem.at[blocks]
    )
    load_weight.start()

    barrier = pltpu.get_barrier_semaphore()
    greeted = [{"ctx": lax.rem(ctx + d, peers)} for d in range(1, peers)]
    greeted += [to_right, to_left, to_z, to_core, to_both]
    for to in greeted:
        pl.semaphore_signal(barrier, inc=1, device_id=to, device_id_type=MESH)

    lane = lax.broadcasted_iota(jnp.int32, (1, LANES), 1)
    lane_group = lane // GROUP
    lane_mode = lax.broadcasted_iota(jnp.int32, (MODES, LANES), 1)
    row = lax.broadcasted_iota(jnp.int32, (STEP, LANES), 0)
    col = lax.broadcasted_iota(jnp.int32, (STEP, LANES), 1)
    after = (row + 1).astype(F32)
    back = lax.rem(STEP - lane_mode, STEP).astype(F32)
    ahead = (STEP - 1 - lane_mode).astype(F32)

    for copy in smalls:
        copy.wait()
    rate_all = rate_in[...]
    scale_all = residue_in[...] * jnp.sqrt(one_less_exp(2.0 * rate_all))
    for f in range(filters):
        rates[f] = jnp.broadcast_to(rate_all[:, f : f + 1], (MODES, LANES))
        scales[f] = jnp.broadcast_to(scale_all[:, f : f + 1], (MODES, LANES))
    square[...] = jnp.zeros_like(square)
    for k in range(3):
        square[k * MODES : (k + 1) * MODES, 0:filters] = rate_all
    rate_row[...] = square[...].T[:filters]
    for k in range(3):
        square[k * MODES : (k + 1) * MODES, 0:filters] = scale_all
    scale_row[...] = square[...].T[:filters]
    skip[...] = skip_in[...].reshape(1, channels)
    source[:, STEP + 3 * MODES :, :] = jnp.zeros(
        (filters, source.shape[1] - STEP - 3 * MODES, width), BF16
    )

    def gate(v, c, earlier_of):
        at = pl.ds(pl.multiple_of(v * LANES, LANES), LANES)
        here = pl.ds(pl.multiple_of(c * STEP, STEP), STEP)
        parts = []
        for i in range(3):
            rows = jnp.concatenate(
                [earlier_of(i, at).astype(F32), feat[i, here, at].astype(F32)], axis=0
            )
            tap = taps[:, i, at]
            value = (
                tap[0:1] * rows[RIM:]
                + tap[1:2] * pltpu.roll(rows, 1, 0)[RIM:]
                + tap[2:3] * pltpu.roll(rows, 2, 0)[RIM:]
            )
            parts.append(value)
        query[here, at] = parts[0].astype(BF16)
        gated[here, at] = (parts[1] * parts[2]).astype(BF16)

    def gate_block(v, carry):
        load_of(v).wait()

        def one_chunk(c, inner):
            before = pl.ds(pl.multiple_of(c * STEP - RIM, RIM), RIM)
            gate(v, c, lambda i, at: feat[i, before, at])
            return inner

        gate(v, 0, lambda i, at: jnp.zeros((RIM, LANES), F32))
        lax.fori_loop(1, chunks, one_chunk, 0)
        return carry

    def swap_in(v, h, strips=STEP // STRIP):
        at = pl.ds(pl.multiple_of(v * LANES, LANES), LANES)

        def one_strip(s, inner):
            rows = pl.ds(pl.multiple_of(s * STRIP, STRIP), STRIP)
            parts = []
            for k in range(PACK):
                here = pl.ds(pl.multiple_of((h * PACK + k) * STEP + s * STRIP, STRIP), STRIP)
                parts.append(gated[here, at])
            for g, part in enumerate(by_filter(parts, lane_group)):
                source[v * PACK + g, rows, h * LANES : (h + 1) * LANES] = part
            return inner

        lax.fori_loop(0, strips, one_strip, 0)

    lax.fori_loop(0, blocks // 2, gate_block, 0)

    with jax.named_scope("c_barrier"):
        pl.semaphore_wait(barrier, len(greeted))
    rim_copy = pltpu.make_async_remote_copy(
        src_ref=feat_hbm.at[:, pl.ds(tokens - RIM, RIM), :],
        dst_ref=rim,
        send_sem=rim_sem.at[0],
        recv_sem=rim_sem.at[1],
        device_id={"ctx": lax.rem(ctx + 1, peers)},
        device_id_type=MESH,
    )
    rim_copy.start()
    used = []

    def sent(src, dst, to):
        k = len(used)
        copy = pltpu.make_async_remote_copy(
            src_ref=src,
            dst_ref=dst,
            send_sem=send_sem.at[k],
            recv_sem=recv_sem.at[k],
            device_id=to,
            device_id_type=MESH,
        )
        copy.start()
        used.append(copy)
        return copy

    weight_copy = sent(weight_hbm.at[:, other_cols], weight.at[pl.ds(depth, depth), :], to_core)

    lax.fori_loop(blocks // 2, blocks, gate_block, 0)

    def state_block(v, carry):
        at = pl.ds(pl.multiple_of(v * LANES, LANES), LANES)
        for h in range(halves):
            swap_in(v, h)
        packed = jnp.zeros((MODES, LANES), F32)
        for g in range(PACK):
            f = v * PACK + g
            rate = rates[f]
            hi, lo = hi_lo(jnp.exp(-rate * ahead))
            factor = jnp.concatenate([hi, lo], axis=0).astype(BF16)
            product = jnp.dot(factor, source[f, :STEP, :], preferred_element_type=F32)
            ends = product[:MODES] + product[MODES:]
            local[f] = ends
            place = (lane_group - g) & (PACK - 1)
            decay = jnp.exp(-rate * ((PACK - 1 - place) * STEP).astype(F32))
            whole = jnp.exp(rate * (-float(PACK * STEP)))
            last = decay * (whole * ends[:, :LANES] + ends[:, LANES:])
            for hop in (1, 2, 4):
                last = last + pltpu.roll(last, hop * GROUP, 1)
            packed = jnp.where(lane_group == g, last, packed)
        total[:, at] = packed
        return carry

    with jax.named_scope("c_state"):
        lax.fori_loop(0, blocks, state_block, 0)

    def amend_block(v, carry):
        at = pl.ds(pl.multiple_of(v * LANES, LANES), LANES)
        parts = []
        for i in range(3):
            rows = jnp.concatenate([rim[i, :, at], feat[i, :RIM, at]], axis=0).astype(F32)
            tap = taps[:, i, at]
            value = (
                tap[0:1] * rows[RIM:]
                + tap[1:2] * pltpu.roll(rows, 1, 0)[RIM:]
                + tap[2:3] * pltpu.roll(rows, 2, 0)[RIM:]
            )
            parts.append(value)
        new = (lax.broadcasted_iota(jnp.int32, (RIM, LANES), 0) < 2) & (ctx > 0)
        was = gated[:RIM, at].astype(F32)
        now = jnp.where(new, (parts[1] * parts[2]).astype(BF16).astype(F32), was)
        gated[:RIM, at] = now.astype(BF16)
        query[:RIM, at] = jnp.where(new, parts[0], query[:RIM, at].astype(F32)).astype(BF16)
        change = now - was
        rate = rates[v * PACK]
        for g in range(1, PACK):
            rate = jnp.where(lane_group == g, rates[v * PACK + g], rate)
        chan_rates[:, at] = rate

        def effect(count):
            return (
                jnp.exp(rate * (-float(count - 1))) * change[0:1]
                + jnp.exp(rate * (-float(count - 2))) * change[1:2]
            )

        total[:, at] = total[:, at] + effect(tokens)
        amend[:, at] = effect(STEP)
        return carry

    with jax.named_scope("c_rim"):
        rim_copy.wait()
    lax.fori_loop(0, blocks, amend_block, 0)

    sums = []
    for d in range(1, peers):
        copy = pltpu.make_async_remote_copy(
            src_ref=total,
            dst_ref=totals.at[d - 1],
            send_sem=sum_send.at[d - 1],
            recv_sem=sum_recv.at[d - 1],
            device_id={"ctx": lax.rem(ctx + d, peers)},
            device_id_type=MESH,
        )
        copy.start()
        sums.append(copy)

    def build(f, carry):
        first = jnp.sum(scales[f] * jnp.exp(-rates[f] * back), axis=0, keepdims=True)
        turned = pltpu.roll(
            jnp.broadcast_to(first, (STEP, LANES)), 0, 1, stride=1, stride_axis=0
        )
        left[f, :, :LANES] = jnp.where(col <= row, turned, 0.0).astype(BF16)
        hi, lo = hi_lo(scale_row[pl.ds(f, 1), :] * jnp.exp(-rate_row[pl.ds(f, 1), :] * after))
        second = (col >= MODES) & (col < 2 * MODES)
        left[f, :, LANES:] = jnp.where(second, lo, hi).astype(BF16)
        return carry

    def swap_again(v, carry):
        swap_in(v, 0, 1)
        return carry

    lax.fori_loop(0, blocks, swap_again, 0)
    with jax.named_scope("c_build"):
        lax.fori_loop(0, filters, build, 0)
    with jax.named_scope("c_sums"):
        for copy in sums:
            copy.wait()
    for v in range(blocks):
        at = pl.ds(v * LANES, LANES)
        chan_rate = chan_rates[:, at]
        carried = jnp.zeros((MODES, LANES), F32)
        for d in range(1, peers):
            decay = jnp.exp(chan_rate * (-float((d - 1) * tokens)))
            carried = carried + jnp.where(ctx >= d, decay * totals[d - 1, :, at], 0.0)
        total[:, at] = carried

    def state_rows(v, carry):
        at = pl.ds(pl.multiple_of(v * LANES, LANES), LANES)
        incoming = total[:, at]
        amended = pltpu.roll(amend[:, at], GROUP, 1)
        for g in range(PACK):
            f = v * PACK + g
            place = (lane_group - g) & (PACK - 1)
            a = pltpu.roll(local[f, :, :LANES], GROUP, 1)
            b = pltpu.roll(local[f, :, LANES:], GROUP, 1)
            low = jnp.where(place == 0, incoming, a + jnp.where(place == 1, amended, 0.0))
            high = jnp.where(place == 0, a, b)
            states = jnp.concatenate(chunk_scan(low, high, rates[f], place), axis=1)
            hi, lo = hi_lo(states)
            source[f, STEP : STEP + 3 * MODES, :] = jnp.concatenate([hi, hi, lo], axis=0).astype(
                BF16
            )
        return carry

    with jax.named_scope("c_states"):
        lax.fori_loop(0, blocks, state_rows, 0)

    def block_out(h):
        def one_block(v, carry):
            at = pl.ds(pl.multiple_of(v * LANES, LANES), LANES)
            wide = pl.ds(pl.multiple_of(h * LANES, LANES), LANES)
            for g in range(PACK):
                f = v * PACK + g
                result[g] = jnp.dot(
                    left[f], source[f, :, wide], preferred_element_type=F32
                ).astype(BF16)

            def one_strip(s, inner):
                rows = pl.ds(pl.multiple_of(s * STRIP, STRIP), STRIP)
                parts = by_chunk([result[g, rows, :] for g in range(PACK)], lane_group)
                for k in range(PACK):
                    here = pl.ds(
                        pl.multiple_of((h * PACK + k) * STEP + s * STRIP, STRIP), STRIP
                    )
                    value = parts[k].astype(F32) + skip[:, at] * gated[here, at].astype(F32)
                    mixed[here, at] = (query[here, at].astype(F32) * value).astype(BF16)
                return inner

            lax.fori_loop(0, STEP // STRIP, one_strip, 0)
            return carry

        return one_block

    def passed_on(at):
        rows = pl.ds(pl.multiple_of(at * block, block), block)
        return sent(
            mixed.at[rows, pl.ds(0, depth)], mixed.at[rows, pl.ds(depth, depth)], to_core
        )

    first_half = far // 2
    with jax.named_scope("c_half1"):
        lax.fori_loop(0, blocks, block_out(first_half), 0)
    passed = [passed_on(far), passed_on(far + 1 - 2 * lax.rem(far, 2))]
    lax.fori_loop(0, 1, block_out(1 - first_half), 0)

    def tiles(token, rows, first, count, store):
        wide = count // TILE

        def one(n, carry):
            i, j = n // wide, lax.rem(n, wide)
            r = pl.multiple_of(i * sub, sub)
            c = pl.multiple_of(j * TILE, TILE)
            value = jnp.dot(
                mixed[pl.ds(pl.multiple_of(token + r, sub), sub), :],
                weight[:, pl.ds(pl.multiple_of(first + c, TILE), TILE)],
                preferred_element_type=F32,
            )
            store(pl.ds(r, sub), pl.ds(c, TILE), value)
            return carry

        lax.fori_loop(0, (rows // sub) * wide, one, 0)

    def start_of(at):
        return at * block

    def plain(dst, extra=()):
        def store(r, c, value):
            for e in extra:
                value = value + e[r, c].astype(F32)
            dst[r, c] = value.astype(BF16)

        return store

    mine, others = z * sub, (1 - z) * sub
    order = (far, right, lefts, x)

    def z_first(k):
        at = order[k]
        tiles(start_of(at) + others, sub, half, half, plain(z_send.at[k]))
        return sent(z_send.at[k], z_recv.at[k], to_z)

    with jax.named_scope("c_w_start"):
        load_weight.wait()
        weight_copy.wait_recv()
        passed[0].wait_recv()
    zs = [z_first(0)]
    fars = []
    for s, to in ((0, to_right), (1, to_left)):
        tiles(start_of(far), block, s * quarter, quarter, plain(far_send.at[s]))
        fars.append(sent(far_send.at[s], far_recv.at[s], to))

    with jax.named_scope("c_half2"):
        lax.fori_loop(1, blocks, block_out(1 - first_half), 0)
    passed += [passed_on(x + 1 - 2 * lax.rem(x, 2)), passed_on(x)]
    with jax.named_scope("c_w_passed"):
        for copy in passed[1:]:
            copy.wait_recv()
    zs.append(z_first(1))
    sides = ((0, right, to_right), (1, lefts, to_left))
    nears = {}
    for s, at, to in sides:
        side = 1 - s
        tiles(start_of(at), block, side * quarter, quarter, plain(near_send.at[s, side]))
        nears[s, side] = sent(near_send.at[s, side], near_recv.at[s, side], to)
    zs.append(z_first(2))
    zs.append(z_first(3))

    with jax.named_scope("c_w_z0"):
        zs[0].wait_recv()
    fars2 = []
    for s, to in ((0, to_right), (1, to_left)):
        at = pl.ds(s * quarter, quarter)
        tiles(
            start_of(far) + mine,
            sub,
            half + s * quarter,
            quarter,
            plain(far2_send.at[s], (z_recv.at[0, :, at],)),
        )
        fars2.append(sent(far2_send.at[s], far2_recv.at[s], to))
    for s, at, to in sides:
        with jax.named_scope("c_w_far"):
            fars[s].wait_recv()
        tiles(
            start_of(at), block, s * quarter, quarter, plain(near_send.at[s, s], (far_recv.at[s],))
        )
        nears[s, s] = sent(near_send.at[s, s], near_recv.at[s, s], to)

    nears2 = {}
    for s, at, to in sides:
        with jax.named_scope("c_w_z12"):
            zs[1 + s].wait_recv()
        side = 1 - s
        piece = pl.ds(side * quarter, quarter)
        tiles(
            start_of(at) + mine,
            sub,
            half + side * quarter,
            quarter,
            plain(near2_send.at[s, side], (z_recv.at[1 + s, :, piece],)),
        )
        nears2[s, side] = sent(near2_send.at[s, side], near2_recv.at[s, side], to)
    for s, at, to in sides:
        with jax.named_scope("c_w_far2"):
            fars2[s].wait_recv()
        piece = pl.ds(s * quarter, quarter)
        tiles(
            start_of(at) + mine,
            sub,
            half + s * quarter,
            quarter,
            plain(near2_send.at[s, s], (z_recv.at[1 + s, :, piece], far2_recv.at[s])),
        )
        nears2[s, s] = sent(near2_send.at[s, s], near2_recv.at[s, s], to)

    with jax.named_scope("c_w_near"):
        for copy in nears.values():
            copy.wait_recv()
    for side in (0, 1):
        piece = pl.ds(side * quarter, quarter)
        away = pl.ds(pl.multiple_of(others, sub), sub)
        tiles(
            start_of(x) + others,
            sub,
            side * quarter,
            quarter,
            plain(
                turn_send.at[:, piece],
                (near_recv.at[0, side, away], near_recv.at[1, side, away]),
            ),
        )
    my_rows = pl.ds(pl.multiple_of(core * own, own), own)
    other_rows = pl.ds(pl.multiple_of((1 - core) * own, own), own)
    turns = [
        sent(turn_send.at[other_rows], turn_recv.at[1], to_both),
        sent(turn_send.at[my_rows], turn_recv.at[0], to_z),
    ]

    def kept(offset, extra):
        def store(r, c, value):
            for e in extra:
                value = value + e[r, c].astype(F32)
            held[r, pl.ds(pl.multiple_of(offset + c.start, TILE), TILE)] = value

        return store

    for side in (0, 1):
        here = pl.ds(pl.multiple_of(mine, sub), sub)
        tiles(
            start_of(x) + mine,
            sub,
            side * quarter,
            quarter,
            kept(side * quarter, (near_recv.at[0, side, here], near_recv.at[1, side, here])),
        )
    first = pl.ds(0, half)
    last_send[0] = held[other_rows, first].astype(BF16)
    lasts = [sent(last_send.at[0], last_recv.at[0], to_core)]
    with jax.named_scope("c_w_z3"):
        zs[3].wait_recv()
    for side in (0, 1):
        piece = pl.ds(side * quarter, quarter)
        tiles(
            start_of(x) + mine,
            sub,
            half + side * quarter,
            quarter,
            kept(half + side * quarter, (z_recv.at[3, :, piece],)),
        )
    my_first = pl.multiple_of(core * cols, cols)
    with jax.named_scope("c_w_near2"):
        for copy in nears2.values():
            copy.wait_recv()
    for rows, keep in ((other_rows, False), (my_rows, True)):
        for side in (0, 1):
            at = pl.ds(half + side * quarter, quarter)
            value = (
                held[rows, at]
                + near2_recv[0, side, rows, :].astype(F32)
                + near2_recv[1, side, rows, :].astype(F32)
            ).astype(BF16)
            if keep:
                out_ref[:, pl.ds(my_first + half + side * quarter, quarter)] = value
            else:
                last_send[1, :, side * quarter : (side + 1) * quarter] = value
        if not keep:
            lasts.append(sent(last_send.at[1], last_recv.at[1], to_core))
    other_first = pl.multiple_of((1 - core) * cols, cols)
    with jax.named_scope("c_w_last"):
        lasts[1].wait_recv()
    out_ref[:, pl.ds(other_first + half, half)] = last_recv[1]
    with jax.named_scope("c_w_turn"):
        lasts[0].wait_recv()
        turns[0].wait_recv()
    out_ref[:, pl.ds(other_first, half)] = (
        last_recv[0].astype(F32) + turn_recv[1].astype(F32)
    ).astype(BF16)
    turns[1].wait_recv()
    out_ref[:, pl.ds(my_first, half)] = (
        held[my_rows, first] + turn_recv[0].astype(F32)
    ).astype(BF16)
    for copy in used:
        copy.wait_send()


def on_device(featurized, short_filter, decay_rate, residue, skip_gain, weight):
    tokens, _, channels = featurized.shape
    filters = decay_rate.shape[0]
    peers = lax.axis_size("ctx")
    chunks = tokens // STEP
    width = chunks * GROUP
    outs = weight.shape[1]
    cols = outs // 2
    half, quarter = cols // 2, cols // 4
    block = tokens // 4
    sub = block // 2
    own = sub // 2
    pairs = [
        (4, sub, half),
        (2, block, quarter),
        (2, 2, block, quarter),
        (2, sub, quarter),
        (2, 2, sub, quarter),
    ]
    return pl.pallas_call(
        kernel,
        out_shape=jax.ShapeDtypeStruct((own, outs), BF16),
        in_specs=[pl.BlockSpec(memory_space=pltpu.HBM)] * 6,
        out_specs=pl.BlockSpec(memory_space=pltpu.VMEM),
        scratch_shapes=[
            pltpu.VMEM((3, tokens, channels), BF16),
            pltpu.VMEM(short_filter.shape, F32),
            pltpu.VMEM((MODES, filters), F32),
            pltpu.VMEM((MODES, filters), F32),
            pltpu.VMEM((channels,), F32),
            pltpu.VMEM((1, channels), F32),
            pltpu.VMEM((LANES, LANES), F32),
            pltpu.VMEM((filters, LANES), F32),
            pltpu.VMEM((filters, LANES), F32),
            pltpu.VMEM((filters, MODES, LANES), F32),
            pltpu.VMEM((filters, MODES, LANES), F32),
            pltpu.VMEM((3, RIM, channels), BF16),
            pltpu.VMEM((tokens, channels), BF16),
            pltpu.VMEM((tokens, channels), BF16),
            pltpu.VMEM((filters, 2 * STEP, width), BF16),
            pltpu.VMEM((filters, STEP, 2 * LANES), BF16),
            pltpu.VMEM((filters, MODES, width), F32),
            pltpu.VMEM((MODES, channels), F32),
            pltpu.VMEM((MODES, channels), F32),
            pltpu.VMEM((MODES, channels), F32),
            pltpu.VMEM((peers - 1, MODES, channels), F32),
            pltpu.VMEM((PACK, STEP, LANES), BF16),
            pltpu.VMEM((tokens, 2 * channels), BF16),
            pltpu.VMEM((2 * channels, cols), BF16),
        ]
        + [pltpu.VMEM(shape, BF16) for shape in pairs for _ in range(2)]
        + [
            pltpu.VMEM((sub, half), BF16),
            pltpu.VMEM((2, own, half), BF16),
            pltpu.VMEM((sub, cols), F32),
            pltpu.VMEM((2, own, half), BF16),
            pltpu.VMEM((2, own, half), BF16),
            pltpu.SemaphoreType.DMA((4,)),
            pltpu.SemaphoreType.DMA((channels // LANES + 1,)),
            pltpu.SemaphoreType.DMA((2,)),
            pltpu.SemaphoreType.DMA((peers - 1,)),
            pltpu.SemaphoreType.DMA((peers - 1,)),
            pltpu.SemaphoreType.DMA((COPIES,)),
            pltpu.SemaphoreType.DMA((COPIES,)),
        ],
        compiler_params=pltpu.CompilerParams(
            collective_id=0, has_side_effects=True, vmem_limit_bytes=50 * 2**20
        ),
        name="hyena",
    )(
        *(
            pltpu.with_memory_space_constraint(array, pltpu.HBM)
            for array in (
                featurized.transpose(1, 0, 2),
                short_filter,
                decay_rate.T,
                residue.T,
                skip_gain,
                weight,
            )
        )
    )


def solution(mesh):
    finer = Mesh(
        mesh.devices.reshape(mesh.shape["ctx"], 4, 2, 2), ("ctx", "chan_0", "chan_1", "chan_2")
    )
    placed = (
        P("ctx", None, CHAN),
        P(None, None, CHAN),
        P(CHAN, None),
        P(CHAN, None),
        P(CHAN),
        P(CHAN, None),
    )
    return jax.shard_map(
        on_device, mesh=finer, in_specs=placed, out_specs=P(CTX_CHAN, None), check_vma=False
    )
```

```python
import jax
import jax.numpy as jnp
from jax import lax
from jax.experimental import pallas as pl
from jax.experimental.pallas import tpu as pltpu
from jax.sharding import Mesh
from jax.sharding import PartitionSpec as P

CHAN = ("chan_0", "chan_1", "chan_2")
CTX_CHAN = ("ctx", "chan_0", "chan_1", "chan_2")
MESH = pl.DeviceIdType.MESH
F32 = jnp.float32
BF16 = jnp.bfloat16
LANES = 128
TILE = 256
COPIES = 31
STEP = 128
GROUP = 16
PACK = LANES // GROUP
MODES = 16
STRIP = 64
RIM = 16


def turned_to(parts, lane_group, sign):
    for bit in (1, 2, 4):
        move = (lane_group & bit) != 0
        parts = [
            jnp.where(move, parts[(k + sign * bit) % PACK], parts[k]) for k in range(PACK)
        ]
    return parts


def by_filter(parts, lane_group):
    parts = [pltpu.roll(part, k * GROUP, 1) if k else part for k, part in enumerate(parts)]
    parts = turned_to(parts, lane_group, 1)
    return [parts[-g % PACK] for g in range(PACK)]


def by_chunk(parts, lane_group):
    parts = turned_to([parts[-k % PACK] for k in range(PACK)], lane_group, -1)
    return [pltpu.roll(part, LANES - k * GROUP, 1) if k else part for k, part in enumerate(parts)]


def hi_lo(value):
    hi = value.astype(BF16).astype(F32)
    return hi, value - hi


def one_less_exp(x):
    series = jnp.ones_like(x)
    for n in range(9, 1, -1):
        series = 1.0 - x * (1.0 / n) * series
    return jnp.where(x < 0.5, x * series, 1.0 - jnp.exp(-x))


def chunk_scan(low, high, rate, place):
    for hop in (1, 2, 4):
        decay = jnp.exp(rate * (-float(hop * STEP)))
        inside = place >= hop
        a, b = pltpu.roll(low, hop * GROUP, 1), pltpu.roll(high, hop * GROUP, 1)
        low, high = (
            low + decay * jnp.where(inside, a, 0.0),
            high + decay * jnp.where(inside, b, a),
        )
    return low, high + jnp.exp(rate * (-float(PACK * STEP))) * low


def column_parts(cols):
    half = cols * 9 // 16
    split = cols * 5 // 16
    later = cols * 3 // 16
    x_parts = ((0, split), (split, half - split))
    z_parts = ((0, later), (later, cols - half - later))
    return half, x_parts, z_parts


def kernel(
    feat_hbm,
    taps_hbm,
    rate_hbm,
    residue_hbm,
    skip_hbm,
    weight_hbm,
    out_ref,
    feat,
    taps,
    rate_in,
    residue_in,
    skip_in,
    skip,
    square,
    rate_row,
    scale_row,
    rates,
    scales,
    rim,
    shifts,
    gated,
    query,
    source,
    left,
    local,
    chan_rates,
    amend,
    total,
    totals,
    result,
    mixed,
    weight,
    z_send,
    z_recv,
    far_send,
    far_recv,
    near_send,
    near_recv,
    far2_send,
    far2_recv,
    near2_send,
    near2_recv,
    turn_send,
    turn_recv,
    held,
    last_x_send,
    last_x_recv,
    last_z_send,
    last_z_recv,
    pass_send,
    pass_recv,
    small_sem,
    load_sem,
    rim_sem,
    sum_send,
    sum_recv,
    send_sem,
    recv_sem,
):
    tokens, channels = feat.shape[1], feat.shape[2]
    filters = rates.shape[0]
    chunks = tokens // STEP
    blocks = channels // LANES
    width = chunks * GROUP
    halves = width // LANES
    depth = channels
    cols = weight.shape[1]
    half, x_parts, z_parts = column_parts(cols)
    rest = cols - half
    block = tokens // 4
    sub = block // 2
    own = sub // 2
    ctx = lax.axis_index("ctx")
    peers = lax.axis_size("ctx")
    x = lax.axis_index("chan_0")
    z = lax.axis_index("chan_1")
    core = lax.axis_index("chan_2")
    right, far, lefts = lax.rem(x + 1, 4), lax.rem(x + 2, 4), lax.rem(x + 3, 4)
    to_right, to_left = {"chan_0": right}, {"chan_0": lefts}
    to_z, to_core = {"chan_1": 1 - z}, {"chan_2": 1 - core}
    to_both = {"chan_1": 1 - z, "chan_2": 1 - core}

    smalls = []
    for k, (here, there) in enumerate(
        (
            (taps_hbm, taps),
            (rate_hbm, rate_in),
            (residue_hbm, residue_in),
            (skip_hbm, skip_in),
        )
    ):
        copy = pltpu.make_async_copy(here, there, small_sem.at[k])
        copy.start()
        smalls.append(copy)

    def load_of(v):
        at = pl.ds(pl.multiple_of(v * LANES, LANES), LANES)
        return pltpu.make_async_copy(feat_hbm.at[:, :, at], feat.at[:, :, at], load_sem.at[v])

    for v in range(2):
        load_of(v).start()
    my_cols = pl.ds(pl.multiple_of(core * cols, cols), cols)
    other_cols = pl.ds(pl.multiple_of((1 - core) * cols, cols), cols)
    load_weight = pltpu.make_async_copy(
        weight_hbm.at[:, my_cols], weight.at[pl.ds(0, depth), :], load_sem.at[blocks]
    )

    barrier = pltpu.get_barrier_semaphore()
    greeted = [{"ctx": lax.rem(ctx + d, peers)} for d in range(1, peers)]
    greeted += [to_right, to_left, to_z, to_core, to_both]
    for to in greeted:
        pl.semaphore_signal(barrier, inc=1, device_id=to, device_id_type=MESH)

    lane = lax.broadcasted_iota(jnp.int32, (1, LANES), 1)
    lane_group = lane // GROUP
    lane_mode = lax.broadcasted_iota(jnp.int32, (MODES, LANES), 1)
    row = lax.broadcasted_iota(jnp.int32, (STEP, LANES), 0)
    col = lax.broadcasted_iota(jnp.int32, (STEP, LANES), 1)
    after = (row + 1).astype(F32)
    back = lax.rem(STEP - lane_mode, STEP).astype(F32)
    ahead = (STEP - 1 - lane_mode).astype(F32)

    def gate(v, c, slot):
        at = pl.ds(pl.multiple_of(v * LANES, LANES), LANES)
        here = pl.ds(pl.multiple_of(c * STEP, STEP), STEP)
        before = pl.ds(pl.multiple_of(jnp.maximum(c * STEP - RIM, 0), RIM), RIM)
        parts = []
        for i in range(3):
            earlier = feat[i, before, at].astype(F32)
            now = feat[i, here, at].astype(F32)
            shifts[slot, i, :RIM] = jnp.where(c > 0, earlier, 0.0)
            shifts[slot, i, RIM:] = now
            tap = taps[:, i, at]
            value = (
                tap[0:1] * now
                + tap[1:2] * shifts[slot, i, RIM - 1 : RIM - 1 + STEP]
                + tap[2:3] * shifts[slot, i, RIM - 2 : RIM - 2 + STEP]
            )
            parts.append(value)
        query[here, at] = parts[0].astype(BF16)
        gated[here, at] = (parts[1] * parts[2]).astype(BF16)

    def gate_block(v, carry):
        load_of(v).wait()

        @pl.when(v + 2 < blocks)
        def _():
            load_of(v + 2).start()

        def two_chunks(c, inner):
            gate(v, 2 * c, 0)
            gate(v, 2 * c + 1, 1)
            return inner

        with jax.named_scope("c_gate"):
            lax.fori_loop(0, chunks // 2, two_chunks, 0)
        return carry

    def swap_in(v, h, strips=STEP // STRIP):
        at = pl.ds(pl.multiple_of(v * LANES, LANES), LANES)

        def one_strip(s, inner):
            rows = pl.ds(pl.multiple_of(s * STRIP, STRIP), STRIP)
            parts = []
            for k in range(PACK):
                here = pl.ds(pl.multiple_of((h * PACK + k) * STEP + s * STRIP, STRIP), STRIP)
                parts.append(gated[here, at])
            for g, part in enumerate(by_filter(parts, lane_group)):
                source[v * PACK + g, rows, h * LANES : (h + 1) * LANES] = part
            return inner

        lax.fori_loop(0, strips, one_strip, 0)

    smalls[0].wait()
    lax.fori_loop(0, 2, gate_block, 0)
    load_weight.start()

    with jax.named_scope("c_smalls"):
        for copy in smalls[1:]:
            copy.wait()
    rate_all = rate_in[...]
    scale_all = residue_in[...] * jnp.sqrt(one_less_exp(2.0 * rate_all))
    for f in range(filters):
        rates[f] = jnp.broadcast_to(rate_all[:, f : f + 1], (MODES, LANES))
        scales[f] = jnp.broadcast_to(scale_all[:, f : f + 1], (MODES, LANES))
    square[...] = jnp.zeros_like(square)
    for k in range(3):
        square[k * MODES : (k + 1) * MODES, 0:filters] = rate_all
    rate_row[...] = square[...].T[:filters]
    for k in range(3):
        square[k * MODES : (k + 1) * MODES, 0:filters] = scale_all
    scale_row[...] = square[...].T[:filters]
    skip[...] = skip_in[...].reshape(1, channels)
    source[:, STEP + 3 * MODES :, :] = jnp.zeros(
        (filters, source.shape[1] - STEP - 3 * MODES, width), BF16
    )

    with jax.named_scope("c_barrier"):
        pl.semaphore_wait(barrier, len(greeted))
    rim_copy = pltpu.make_async_remote_copy(
        src_ref=feat_hbm.at[:, pl.ds(tokens - RIM, RIM), :],
        dst_ref=rim,
        send_sem=rim_sem.at[0],
        recv_sem=rim_sem.at[1],
        device_id={"ctx": lax.rem(ctx + 1, peers)},
        device_id_type=MESH,
    )
    rim_copy.start()
    used = []

    def sent(src, dst, to):
        k = len(used)
        copy = pltpu.make_async_remote_copy(
            src_ref=src,
            dst_ref=dst,
            send_sem=send_sem.at[k],
            recv_sem=recv_sem.at[k],
            device_id=to,
            device_id_type=MESH,
        )
        copy.start()
        used.append(copy)
        return copy

    weight_copy = sent(weight_hbm.at[:, other_cols], weight.at[pl.ds(depth, depth), :], to_core)

    lax.fori_loop(2, blocks, gate_block, 0)

    def state_block(v, carry):
        at = pl.ds(pl.multiple_of(v * LANES, LANES), LANES)
        for h in range(halves):
            swap_in(v, h)
        packed = jnp.zeros((MODES, LANES), F32)
        for g in range(PACK):
            f = v * PACK + g
            rate = rates[f]
            hi, lo = hi_lo(jnp.exp(-rate * ahead))
            factor = jnp.concatenate([hi, lo], axis=0).astype(BF16)
            product = jnp.dot(factor, source[f, :STEP, :], preferred_element_type=F32)
            ends = product[:MODES] + product[MODES:]
            local[f] = ends
            place = (lane_group - g) & (PACK - 1)
            decay = jnp.exp(-rate * ((PACK - 1 - place) * STEP).astype(F32))
            whole = jnp.exp(rate * (-float(PACK * STEP)))
            last = decay * (whole * ends[:, :LANES] + ends[:, LANES:])
            for hop in (1, 2, 4):
                last = last + pltpu.roll(last, hop * GROUP, 1)
            packed = jnp.where(lane_group == g, last, packed)
        total[:, at] = packed
        return carry

    with jax.named_scope("c_state"):
        lax.fori_loop(0, blocks, state_block, 0)

    def amend_block(v, carry):
        at = pl.ds(pl.multiple_of(v * LANES, LANES), LANES)
        parts = []
        for i in range(3):
            rows = jnp.concatenate([rim[i, :, at], feat[i, :RIM, at]], axis=0).astype(F32)
            tap = taps[:, i, at]
            value = (
                tap[0:1] * rows[RIM:]
                + tap[1:2] * pltpu.roll(rows, 1, 0)[RIM:]
                + tap[2:3] * pltpu.roll(rows, 2, 0)[RIM:]
            )
            parts.append(value)
        new = (lax.broadcasted_iota(jnp.int32, (RIM, LANES), 0) < 2) & (ctx > 0)
        was = gated[:RIM, at].astype(F32)
        now = jnp.where(new, (parts[1] * parts[2]).astype(BF16).astype(F32), was)
        gated[:RIM, at] = now.astype(BF16)
        query[:RIM, at] = jnp.where(new, parts[0], query[:RIM, at].astype(F32)).astype(BF16)
        change = now - was
        rate = rates[v * PACK]
        for g in range(1, PACK):
            rate = jnp.where(lane_group == g, rates[v * PACK + g], rate)
        chan_rates[:, at] = rate

        def effect(count):
            return (
                jnp.exp(rate * (-float(count - 1))) * change[0:1]
                + jnp.exp(rate * (-float(count - 2))) * change[1:2]
            )

        total[:, at] = total[:, at] + effect(tokens)
        amend[:, at] = effect(STEP)
        return carry

    with jax.named_scope("c_rim"):
        rim_copy.wait()
    lax.fori_loop(0, blocks, amend_block, 0)

    sums = []
    for d in range(1, peers):
        copy = pltpu.make_async_remote_copy(
            src_ref=total,
            dst_ref=totals.at[d - 1],
            send_sem=sum_send.at[d - 1],
            recv_sem=sum_recv.at[d - 1],
            device_id={"ctx": lax.rem(ctx + d, peers)},
            device_id_type=MESH,
        )
        copy.start()
        sums.append(copy)

    def build(f, carry):
        first = jnp.sum(scales[f] * jnp.exp(-rates[f] * back), axis=0, keepdims=True)
        turned = pltpu.roll(
            jnp.broadcast_to(first, (STEP, LANES)), 0, 1, stride=1, stride_axis=0
        )
        left[f, :, :LANES] = jnp.where(col <= row, turned, 0.0).astype(BF16)
        hi, lo = hi_lo(scale_row[pl.ds(f, 1), :] * jnp.exp(-rate_row[pl.ds(f, 1), :] * after))
        second = (col >= MODES) & (col < 2 * MODES)
        left[f, :, LANES:] = jnp.where(second, lo, hi).astype(BF16)
        return carry

    def swap_again(v, carry):
        swap_in(v, 0, 1)
        return carry

    lax.fori_loop(0, blocks, swap_again, 0)
    with jax.named_scope("c_build"):
        lax.fori_loop(0, filters, build, 0)
    with jax.named_scope("c_sums"):
        for copy in sums:
            copy.wait()
    for v in range(blocks):
        at = pl.ds(v * LANES, LANES)
        chan_rate = chan_rates[:, at]
        carried = jnp.zeros((MODES, LANES), F32)
        for d in range(1, peers):
            decay = jnp.exp(chan_rate * (-float((d - 1) * tokens)))
            carried = carried + jnp.where(ctx >= d, decay * totals[d - 1, :, at], 0.0)
        total[:, at] = carried

    def state_rows(v, carry):
        at = pl.ds(pl.multiple_of(v * LANES, LANES), LANES)
        incoming = total[:, at]
        amended = pltpu.roll(amend[:, at], GROUP, 1)
        for g in range(PACK):
            f = v * PACK + g
            place = (lane_group - g) & (PACK - 1)
            a = pltpu.roll(local[f, :, :LANES], GROUP, 1)
            b = pltpu.roll(local[f, :, LANES:], GROUP, 1)
            low = jnp.where(place == 0, incoming, a + jnp.where(place == 1, amended, 0.0))
            high = jnp.where(place == 0, a, b)
            states = jnp.concatenate(chunk_scan(low, high, rates[f], place), axis=1)
            hi, lo = hi_lo(states)
            source[f, STEP : STEP + 3 * MODES, :] = jnp.concatenate([hi, hi, lo], axis=0).astype(
                BF16
            )
        return carry

    with jax.named_scope("c_states"):
        lax.fori_loop(0, blocks, state_rows, 0)

    def far_pass(v):
        rows = pl.ds(pl.multiple_of(far * block, block), block)
        return pltpu.make_async_remote_copy(
            src_ref=mixed.at[rows, pl.ds(pl.multiple_of(v * LANES, LANES), LANES)],
            dst_ref=mixed.at[rows, pl.ds(pl.multiple_of(depth + v * LANES, LANES), LANES)],
            send_sem=pass_send.at[v],
            recv_sem=pass_recv.at[v],
            device_id=to_core,
            device_id_type=MESH,
        )

    def block_out(h, then=lambda v: None):
        def one_block(v, carry):
            at = pl.ds(pl.multiple_of(v * LANES, LANES), LANES)
            wide = pl.ds(pl.multiple_of(h * LANES, LANES), LANES)
            for g in range(PACK):
                f = v * PACK + g
                result[g] = jnp.dot(
                    left[f], source[f, :, wide], preferred_element_type=F32
                ).astype(BF16)

            def one_strip(s, inner):
                rows = pl.ds(pl.multiple_of(s * STRIP, STRIP), STRIP)
                parts = by_chunk([result[g, rows, :] for g in range(PACK)], lane_group)
                for k in range(PACK):
                    here = pl.ds(
                        pl.multiple_of((h * PACK + k) * STEP + s * STRIP, STRIP), STRIP
                    )
                    value = parts[k].astype(F32) + skip[:, at] * gated[here, at].astype(F32)
                    mixed[here, at] = (query[here, at].astype(F32) * value).astype(BF16)
                return inner

            lax.fori_loop(0, STEP // STRIP, one_strip, 0)
            then(v)
            return carry

        return one_block

    def passed_on(at):
        rows = pl.ds(pl.multiple_of(at * block, block), block)
        return sent(
            mixed.at[rows, pl.ds(0, depth)], mixed.at[rows, pl.ds(depth, depth)], to_core
        )

    first_half = far // 2
    with jax.named_scope("c_half1"):
        lax.fori_loop(0, blocks, block_out(first_half, lambda v: far_pass(v).start()), 0)
    passed = [passed_on(far + 1 - 2 * lax.rem(far, 2))]

    def tiles(token, rows, first, count, store):
        wide = count // TILE

        def one(n, carry, whole=True):
            i, j = (n // wide, lax.rem(n, wide)) if whole else (n, wide)
            r = pl.multiple_of(i * sub, sub)
            c = pl.multiple_of(j * TILE, TILE)
            size = TILE if whole else count - wide * TILE
            value = jnp.dot(
                mixed[pl.ds(pl.multiple_of(token + r, sub), sub), :],
                weight[:, pl.ds(pl.multiple_of(first + c, LANES), size)],
                preferred_element_type=F32,
            )
            store(pl.ds(r, sub), pl.ds(c, size), value)
            return carry

        lax.fori_loop(0, (rows // sub) * wide, one, 0)
        if count % TILE:
            lax.fori_loop(0, rows // sub, lambda n, carry: one(n, carry, False), 0)

    def start_of(at):
        return at * block

    def plain(dst, extra=()):
        def store(r, c, value):
            for e in extra:
                value = value + e[r, c].astype(F32)
            dst[r, c] = value.astype(BF16)

        return store

    mine, others = z * sub, (1 - z) * sub
    order = (far, right, lefts, x)
    bands = (others, mine)

    def z_first(k):
        at = order[k]
        tiles(start_of(at) + others, sub, half, rest, plain(z_send.at[k]))
        return sent(z_send.at[k], z_recv.at[k], to_z)

    with jax.named_scope("c_w_start"):
        load_weight.wait()
        weight_copy.wait_recv()
        for v in range(blocks):
            far_pass(v).wait_recv()
    starts, fars = [], ([], [])
    for part in (0, 1):
        first, size = z_parts[part]
        piece = pl.ds(first, size)
        view = z_send.at[0, :, piece]
        tiles(start_of(far) + others, sub, half + first, size, plain(view))
        starts.append(sent(view, z_recv.at[0, :, piece], to_z))
        for s, to in ((0, to_right), (1, to_left)):
            first, size = x_parts[s]
            rows, width = pl.ds(pl.multiple_of(bands[part], sub), sub), pl.ds(0, size)
            view = far_send.at[s, rows, width]
            tiles(start_of(far) + bands[part], sub, first, size, plain(view))
            fars[s].append(sent(view, far_recv.at[s, rows, width], to))

    with jax.named_scope("c_half2"):
        lax.fori_loop(0, blocks, block_out(1 - first_half), 0)
    passed += [passed_on(x + 1 - 2 * lax.rem(x, 2)), passed_on(x)]
    with jax.named_scope("c_w_passed"):
        for copy in passed:
            copy.wait_recv()
    zs = [None, z_first(1)]
    sides = ((0, right, to_right), (1, lefts, to_left))
    nears = ([], [])

    def near(s, side, part, at, to):
        first, size = x_parts[side]
        rows, width = pl.ds(pl.multiple_of(bands[part], sub), sub), pl.ds(0, size)
        view = near_send.at[s, side, rows, width]
        extra = ()
        if s == side:
            with jax.named_scope("c_w_far"):
                fars[s][part].wait_recv()
            extra = (far_recv.at[s, rows],)
        tiles(start_of(at) + bands[part], sub, first, size, plain(view, extra))
        nears[part].append(sent(view, near_recv.at[s, side, rows, width], to))

    for s, at, to in sides:
        near(s, 1 - s, 0, at, to)
    zs.append(z_first(2))
    for s, at, to in sides:
        near(s, s, 0, at, to)
    for s, at, to in sides:
        near(s, 1 - s, 1, at, to)
    zs.append(z_first(3))
    for s, at, to in sides:
        near(s, s, 1, at, to)

    with jax.named_scope("c_w_z0"):
        for copy in starts:
            copy.wait_recv()
    fars2 = []
    for s, to in ((0, to_right), (1, to_left)):
        first, size = z_parts[s]
        width = pl.ds(0, size)
        view = far2_send.at[s, :, width]
        tiles(
            start_of(far) + mine,
            sub,
            half + first,
            size,
            plain(view, (z_recv.at[0, :, pl.ds(first, size)],)),
        )
        fars2.append(sent(view, far2_recv.at[s, :, width], to))

    nears2 = {}

    def near2(s, side, at, to, extra):
        first, size = z_parts[side]
        width = pl.ds(0, size)
        view = near2_send.at[s, side, :, width]
        tiles(
            start_of(at) + mine,
            sub,
            half + first,
            size,
            plain(view, (z_recv.at[1 + s, :, pl.ds(first, size)],) + extra),
        )
        nears2[s, side] = sent(view, near2_recv.at[s, side, :, width], to)

    for s, at, to in sides:
        with jax.named_scope("c_w_z12"):
            zs[1 + s].wait_recv()
        near2(s, 1 - s, at, to, ())
    with jax.named_scope("c_w_near"):
        for copy in nears[0]:
            copy.wait_recv()
    for side in (0, 1):
        first, size = x_parts[side]
        away = pl.ds(pl.multiple_of(others, sub), sub)
        tiles(
            start_of(x) + others,
            sub,
            first,
            size,
            plain(
                turn_send.at[:, pl.ds(first, size)],
                (near_recv.at[0, side, away], near_recv.at[1, side, away]),
            ),
        )
    my_rows = pl.ds(pl.multiple_of(core * own, own), own)
    other_rows = pl.ds(pl.multiple_of((1 - core) * own, own), own)
    turns = [
        sent(turn_send.at[other_rows], turn_recv.at[1], to_both),
        sent(turn_send.at[my_rows], turn_recv.at[0], to_z),
    ]

    for s, at, to in sides:
        with jax.named_scope("c_w_far2"):
            fars2[s].wait_recv()
        near2(s, s, at, to, (far2_recv.at[s],))

    def kept(offset, extra):
        def store(r, c, value):
            for e in extra:
                value = value + e[r, c].astype(F32)
            held[r, pl.ds(pl.multiple_of(offset + c.start, LANES), c.size)] = value

        return store

    with jax.named_scope("c_w_near1"):
        for copy in nears[1]:
            copy.wait_recv()
    for side in (0, 1):
        first, size = x_parts[side]
        here = pl.ds(pl.multiple_of(mine, sub), sub)
        tiles(
            start_of(x) + mine,
            sub,
            first,
            size,
            kept(first, (near_recv.at[0, side, here], near_recv.at[1, side, here])),
        )
    x_cols = pl.ds(0, half)
    last_x_send[...] = held[other_rows, x_cols].astype(BF16)
    last_x = sent(last_x_send, last_x_recv, to_core)
    with jax.named_scope("c_w_z3"):
        zs[3].wait_recv()
    for side in (0, 1):
        first, size = z_parts[side]
        tiles(
            start_of(x) + mine,
            sub,
            half + first,
            size,
            kept(half + first, (z_recv.at[3, :, pl.ds(first, size)],)),
        )
    my_first = pl.multiple_of(core * cols, cols)
    other_first = pl.multiple_of((1 - core) * cols, cols)
    with jax.named_scope("c_w_near2"):
        for copy in nears2.values():
            copy.wait_recv()
    for rows, keep in ((other_rows, False), (my_rows, True)):
        for side in (0, 1):
            first, size = z_parts[side]
            value = (
                held[rows, pl.ds(half + first, size)]
                + near2_recv[0, side, rows, :size].astype(F32)
                + near2_recv[1, side, rows, :size].astype(F32)
            ).astype(BF16)
            if keep:
                out_ref[:, pl.ds(pl.multiple_of(my_first + half + first, LANES), size)] = value
            else:
                last_z_send[:, first : first + size] = value
        if not keep:
            last_z = sent(last_z_send, last_z_recv, to_core)
    with jax.named_scope("c_w_turn"):
        last_x.wait_recv()
        turns[0].wait_recv()
    out_ref[:, pl.ds(other_first, half)] = (
        last_x_recv[...].astype(F32) + turn_recv[1].astype(F32)
    ).astype(BF16)
    with jax.named_scope("c_w_turn2"):
        turns[1].wait_recv()
    out_ref[:, pl.ds(my_first, half)] = (
        held[my_rows, x_cols] + turn_recv[0].astype(F32)
    ).astype(BF16)
    with jax.named_scope("c_w_last"):
        last_z.wait_recv()
    out_ref[:, pl.ds(pl.multiple_of(other_first + half, LANES), rest)] = last_z_recv[...]
    for v in range(blocks):
        far_pass(v).wait_send()
    for copy in used:
        copy.wait_send()


def on_device(featurized, short_filter, decay_rate, residue, skip_gain, weight):
    tokens, _, channels = featurized.shape
    filters = decay_rate.shape[0]
    peers = lax.axis_size("ctx")
    chunks = tokens // STEP
    width = chunks * GROUP
    outs = weight.shape[1]
    cols = outs // 2
    half, x_parts, z_parts = column_parts(cols)
    rest = cols - half
    x_most = max(size for _, size in x_parts)
    z_most = max(size for _, size in z_parts)
    block = tokens // 4
    sub = block // 2
    own = sub // 2
    pairs = [
        (4, sub, rest),
        (2, block, x_most),
        (2, 2, block, x_most),
        (2, sub, z_most),
        (2, 2, sub, z_most),
    ]
    return pl.pallas_call(
        kernel,
        out_shape=jax.ShapeDtypeStruct((own, outs), BF16),
        in_specs=[pl.BlockSpec(memory_space=pltpu.HBM)] * 6,
        out_specs=pl.BlockSpec(memory_space=pltpu.VMEM),
        scratch_shapes=[
            pltpu.VMEM((3, tokens, channels), BF16),
            pltpu.VMEM(short_filter.shape, F32),
            pltpu.VMEM((MODES, filters), F32),
            pltpu.VMEM((MODES, filters), F32),
            pltpu.VMEM((channels,), F32),
            pltpu.VMEM((1, channels), F32),
            pltpu.VMEM((LANES, LANES), F32),
            pltpu.VMEM((filters, LANES), F32),
            pltpu.VMEM((filters, LANES), F32),
            pltpu.VMEM((filters, MODES, LANES), F32),
            pltpu.VMEM((filters, MODES, LANES), F32),
            pltpu.VMEM((3, RIM, channels), BF16),
            pltpu.VMEM((2, 3, RIM + STEP, LANES), F32),
            pltpu.VMEM((tokens, channels), BF16),
            pltpu.VMEM((tokens, channels), BF16),
            pltpu.VMEM((filters, 2 * STEP, width), BF16),
            pltpu.VMEM((filters, STEP, 2 * LANES), BF16),
            pltpu.VMEM((filters, MODES, width), F32),
            pltpu.VMEM((MODES, channels), F32),
            pltpu.VMEM((MODES, channels), F32),
            pltpu.VMEM((MODES, channels), F32),
            pltpu.VMEM((peers - 1, MODES, channels), F32),
            pltpu.VMEM((PACK, STEP, LANES), BF16),
            pltpu.VMEM((tokens, 2 * channels), BF16),
            pltpu.VMEM((2 * channels, cols), BF16),
        ]
        + [pltpu.VMEM(shape, BF16) for shape in pairs for _ in range(2)]
        + [
            pltpu.VMEM((sub, half), BF16),
            pltpu.VMEM((2, own, half), BF16),
            pltpu.VMEM((sub, cols), F32),
            pltpu.VMEM((own, half), BF16),
            pltpu.VMEM((own, half), BF16),
            pltpu.VMEM((own, rest), BF16),
            pltpu.VMEM((own, rest), BF16),
            pltpu.SemaphoreType.DMA((channels // LANES,)),
            pltpu.SemaphoreType.DMA((channels // LANES,)),
            pltpu.SemaphoreType.DMA((4,)),
            pltpu.SemaphoreType.DMA((channels // LANES + 1,)),
            pltpu.SemaphoreType.DMA((2,)),
            pltpu.SemaphoreType.DMA((peers - 1,)),
            pltpu.SemaphoreType.DMA((peers - 1,)),
            pltpu.SemaphoreType.DMA((COPIES,)),
            pltpu.SemaphoreType.DMA((COPIES,)),
        ],
        compiler_params=pltpu.CompilerParams(
            collective_id=0, has_side_effects=True, vmem_limit_bytes=50 * 2**20
        ),
        name="hyena",
    )(
        *(
            pltpu.with_memory_space_constraint(array, pltpu.HBM)
            for array in (
                featurized.transpose(1, 0, 2),
                short_filter,
                decay_rate.T,
                residue.T,
                skip_gain,
                weight,
            )
        )
    )


def solution(mesh):
    finer = Mesh(
        mesh.devices.reshape(mesh.shape["ctx"], 4, 2, 2), ("ctx", "chan_0", "chan_1", "chan_2")
    )
    placed = (
        P("ctx", None, CHAN),
        P(None, None, CHAN),
        P(CHAN, None),
        P(CHAN, None),
        P(CHAN),
        P(CHAN, None),
    )
    return jax.shard_map(
        on_device, mesh=finer, in_specs=placed, out_specs=P(CTX_CHAN, None), check_vma=False
    )
```

```python
import jax
import jax.numpy as jnp
from jax import lax
from jax.experimental import pallas as pl
from jax.experimental.pallas import tpu as pltpu
from jax.sharding import Mesh
from jax.sharding import PartitionSpec as P

CHAN = ("chan_0", "chan_1", "chan_2")
CTX_CHAN = ("ctx", "chan_0", "chan_1", "chan_2")
MESH = pl.DeviceIdType.MESH
F32 = jnp.float32
BF16 = jnp.bfloat16
LANES = 128
TILE = 256
COPIES = 33
UNROLL = 4
STEP = 128
GROUP = 16
PACK = LANES // GROUP
MODES = 16
STRIP = 32
RIM = 16


def turned_to(parts, lane_group, sign):
    for bit in (1, 2, 4):
        move = (lane_group & bit) != 0
        parts = [
            jnp.where(move, parts[(k + sign * bit) % PACK], parts[k]) for k in range(PACK)
        ]
    return parts


def by_filter(parts, lane_group):
    parts = [pltpu.roll(part, k * GROUP, 1) if k else part for k, part in enumerate(parts)]
    parts = turned_to(parts, lane_group, 1)
    return [parts[-g % PACK] for g in range(PACK)]


def by_chunk(parts, lane_group):
    parts = turned_to([parts[-k % PACK] for k in range(PACK)], lane_group, -1)
    return [pltpu.roll(part, LANES - k * GROUP, 1) if k else part for k, part in enumerate(parts)]


def hi_lo(value):
    hi = value.astype(BF16).astype(F32)
    return hi, value - hi


def one_less_exp(x):
    series = jnp.ones_like(x)
    for n in range(9, 1, -1):
        series = 1.0 - x * (1.0 / n) * series
    return jnp.where(x < 0.5, x * series, 1.0 - jnp.exp(-x))


def chunk_scan(low, high, rate, place):
    for hop in (1, 2, 4):
        decay = jnp.exp(rate * (-float(hop * STEP)))
        inside = place >= hop
        a, b = pltpu.roll(low, hop * GROUP, 1), pltpu.roll(high, hop * GROUP, 1)
        low, high = (
            low + decay * jnp.where(inside, a, 0.0),
            high + decay * jnp.where(inside, b, a),
        )
    return low, high + jnp.exp(rate * (-float(PACK * STEP))) * low


def column_parts(cols):
    half = cols * 9 // 16
    split = cols * 5 // 16
    later = cols * 3 // 16
    x_parts = ((0, split), (split, half - split))
    z_parts = ((0, later), (later, cols - half - later))
    return half, x_parts, z_parts


def kernel(
    feat_hbm,
    taps_hbm,
    rate_hbm,
    residue_hbm,
    skip_hbm,
    weight_hbm,
    out_ref,
    feat,
    taps,
    rate_in,
    residue_in,
    skip_in,
    skip,
    square,
    rate_row,
    scale_row,
    rates,
    scales,
    rim,
    shifts,
    gated,
    query,
    source,
    left,
    local,
    chan_rates,
    amend,
    total,
    passed_total,
    totals,
    result,
    mixed,
    weight,
    z_send,
    z_recv,
    far_send,
    far_recv,
    near_send,
    near_recv,
    far2_send,
    far2_recv,
    near2_send,
    near2_recv,
    cross_recv,
    turn_send,
    turn_recv,
    held,
    last_x_send,
    last_x_recv,
    last_z_send,
    last_z_recv,
    pass_send,
    pass_recv,
    small_sem,
    load_sem,
    rim_sem,
    sum_send,
    sum_recv,
    send_sem,
    recv_sem,
):
    tokens, channels = feat.shape[1], feat.shape[2]
    filters = rates.shape[0]
    chunks = tokens // STEP
    blocks = channels // LANES
    width = chunks * GROUP
    halves = width // LANES
    depth = channels
    cols = weight.shape[1]
    half, x_parts, z_parts = column_parts(cols)
    rest = cols - half
    block = tokens // 4
    sub = block // 2
    own = sub // 2
    ctx = lax.axis_index("ctx")
    peers = lax.axis_size("ctx")
    x = lax.axis_index("chan_0")
    z = lax.axis_index("chan_1")
    core = lax.axis_index("chan_2")
    right, far, lefts = lax.rem(x + 1, 4), lax.rem(x + 2, 4), lax.rem(x + 3, 4)
    to_right, to_left = {"chan_0": right}, {"chan_0": lefts}
    to_z, to_core = {"chan_1": 1 - z}, {"chan_2": 1 - core}
    to_both = {"chan_1": 1 - z, "chan_2": 1 - core}

    smalls = []
    for k, (here, there) in enumerate(
        (
            (taps_hbm, taps),
            (rate_hbm, rate_in),
            (residue_hbm, residue_in),
            (skip_hbm, skip_in),
        )
    ):
        copy = pltpu.make_async_copy(here, there, small_sem.at[k])
        copy.start()
        smalls.append(copy)

    def load_of(v):
        at = pl.ds(pl.multiple_of(v * LANES, LANES), LANES)
        return pltpu.make_async_copy(feat_hbm.at[:, :, at], feat.at[:, :, at], load_sem.at[v])

    for v in range(2):
        load_of(v).start()
    my_cols = pl.ds(pl.multiple_of(core * cols, cols), cols)
    other_cols = pl.ds(pl.multiple_of((1 - core) * cols, cols), cols)
    load_weight = pltpu.make_async_copy(
        weight_hbm.at[:, my_cols], weight.at[pl.ds(0, depth), :], load_sem.at[blocks]
    )

    rim[...] = jnp.zeros_like(rim)
    totals[...] = jnp.zeros_like(totals)
    barrier = pltpu.get_barrier_semaphore()
    greeted = [{"ctx": lax.rem(ctx + d, peers)} for d in range(1, peers)]
    greeted += [to_right, to_left, to_z, to_core, to_both]
    greeted += [{"chan_0": right, "chan_2": 1 - core}, {"chan_0": lefts, "chan_2": 1 - core}]
    for to in greeted:
        pl.semaphore_signal(barrier, inc=1, device_id=to, device_id_type=MESH)

    lane = lax.broadcasted_iota(jnp.int32, (1, LANES), 1)
    lane_group = lane // GROUP
    lane_mode = lax.broadcasted_iota(jnp.int32, (MODES, LANES), 1)
    row = lax.broadcasted_iota(jnp.int32, (STEP, LANES), 0)
    col = lax.broadcasted_iota(jnp.int32, (STEP, LANES), 1)
    after = (row + 1).astype(F32)
    back = lax.rem(STEP - lane_mode, STEP).astype(F32)
    ahead = (STEP - 1 - lane_mode).astype(F32)

    def gate(v, c, slot):
        at = pl.ds(pl.multiple_of(v * LANES, LANES), LANES)
        here = pl.ds(pl.multiple_of(c * STEP, STEP), STEP)
        before = pl.ds(pl.multiple_of(jnp.maximum(c * STEP - RIM, 0), RIM), RIM)
        parts = []
        for i in range(3):
            earlier = feat[i, before, at].astype(F32)
            now = feat[i, here, at].astype(F32)
            shifts[slot, i, :RIM] = jnp.where(c > 0, earlier, 0.0)
            shifts[slot, i, RIM:] = now
            tap = taps[:, i, at]
            value = (
                tap[0:1] * now
                + tap[1:2] * shifts[slot, i, RIM - 1 : RIM - 1 + STEP]
                + tap[2:3] * shifts[slot, i, RIM - 2 : RIM - 2 + STEP]
            )
            parts.append(value)
        query[here, at] = parts[0].astype(BF16)
        gated[here, at] = (parts[1] * parts[2]).astype(BF16)

    def gate_block(v, carry):
        load_of(v).wait()

        @pl.when(v + 2 < blocks)
        def _():
            load_of(v + 2).start()

        def some_chunks(c, inner):
            for k in range(UNROLL):
                gate(v, UNROLL * c + k, k)
            return inner

        with jax.named_scope("c_gate"):
            lax.fori_loop(0, chunks // UNROLL, some_chunks, 0)
        return carry

    def swap_in(v, h, strips=STEP // STRIP):
        at = pl.ds(pl.multiple_of(v * LANES, LANES), LANES)

        def one_strip(s, inner):
            rows = pl.ds(pl.multiple_of(s * STRIP, STRIP), STRIP)
            parts = []
            for k in range(PACK):
                here = pl.ds(pl.multiple_of((h * PACK + k) * STEP + s * STRIP, STRIP), STRIP)
                parts.append(gated[here, at])
            for g, part in enumerate(by_filter(parts, lane_group)):
                source[v * PACK + g, rows, h * LANES : (h + 1) * LANES] = part
            return inner

        for s in range(strips):
            one_strip(s, 0)

    smalls[0].wait()
    lax.fori_loop(0, 2, gate_block, 0)
    load_weight.start()

    with jax.named_scope("c_smalls"):
        for copy in smalls[1:]:
            copy.wait()
    rate_all = rate_in[...]
    scale_all = residue_in[...] * jnp.sqrt(one_less_exp(2.0 * rate_all))
    for f in range(filters):
        rates[f] = jnp.broadcast_to(rate_all[:, f : f + 1], (MODES, LANES))
        scales[f] = jnp.broadcast_to(scale_all[:, f : f + 1], (MODES, LANES))
    square[...] = jnp.zeros_like(square)
    for k in range(3):
        square[k * MODES : (k + 1) * MODES, 0:filters] = rate_all
    rate_row[...] = square[...].T[:filters]
    for k in range(3):
        square[k * MODES : (k + 1) * MODES, 0:filters] = scale_all
    scale_row[...] = square[...].T[:filters]
    skip[...] = skip_in[...].reshape(1, channels)
    source[:, STEP + 3 * MODES :, :] = jnp.zeros(
        (filters, source.shape[1] - STEP - 3 * MODES, width), BF16
    )

    with jax.named_scope("c_barrier"):
        pl.semaphore_wait(barrier, len(greeted))
    rim_copy = pltpu.make_async_remote_copy(
        src_ref=feat_hbm.at[:, pl.ds(tokens - RIM, RIM), :],
        dst_ref=rim,
        send_sem=rim_sem.at[0],
        recv_sem=rim_sem.at[1],
        device_id={"ctx": lax.rem(ctx + 1, peers)},
        device_id_type=MESH,
    )

    @pl.when(ctx < peers - 1)
    def _():
        rim_copy.start()

    used = []

    def sent(src, dst, to):
        k = len(used)
        copy = pltpu.make_async_remote_copy(
            src_ref=src,
            dst_ref=dst,
            send_sem=send_sem.at[k],
            recv_sem=recv_sem.at[k],
            device_id=to,
            device_id_type=MESH,
        )
        copy.start()
        used.append(copy)
        return copy

    weight_copy = sent(weight_hbm.at[:, other_cols], weight.at[pl.ds(depth, depth), :], to_core)

    lax.fori_loop(2, blocks, gate_block, 0)

    def state_block(v, carry):
        at = pl.ds(pl.multiple_of(v * LANES, LANES), LANES)
        for h in range(halves):
            swap_in(v, h)
        packed = jnp.zeros((MODES, LANES), F32)
        for g in range(PACK):
            f = v * PACK + g
            rate = rates[f]
            hi, lo = hi_lo(jnp.exp(-rate * ahead))
            factor = jnp.concatenate([hi, lo], axis=0).astype(BF16)
            product = jnp.dot(factor, source[f, :STEP, :], preferred_element_type=F32)
            ends = product[:MODES] + product[MODES:]
            local[f] = ends
            place = (lane_group - g) & (PACK - 1)
            decay = jnp.exp(-rate * ((PACK - 1 - place) * STEP).astype(F32))
            whole = jnp.exp(rate * (-float(PACK * STEP)))
            last = decay * (whole * ends[:, :LANES] + ends[:, LANES:])
            for hop in (1, 2, 4):
                last = last + pltpu.roll(last, hop * GROUP, 1)
            packed = jnp.where(lane_group == g, last, packed)
        total[:, at] = packed
        return carry

    with jax.named_scope("c_state"):
        lax.fori_loop(0, blocks, state_block, 0)

    def amend_block(v, carry):
        at = pl.ds(pl.multiple_of(v * LANES, LANES), LANES)
        parts = []
        for i in range(3):
            rows = jnp.concatenate([rim[i, :, at], feat[i, :RIM, at]], axis=0).astype(F32)
            tap = taps[:, i, at]
            value = (
                tap[0:1] * rows[RIM:]
                + tap[1:2] * pltpu.roll(rows, 1, 0)[RIM:]
                + tap[2:3] * pltpu.roll(rows, 2, 0)[RIM:]
            )
            parts.append(value)
        new = (lax.broadcasted_iota(jnp.int32, (RIM, LANES), 0) < 2) & (ctx > 0)
        was = gated[:RIM, at].astype(F32)
        now = jnp.where(new, (parts[1] * parts[2]).astype(BF16).astype(F32), was)
        gated[:RIM, at] = now.astype(BF16)
        query[:RIM, at] = jnp.where(new, parts[0], query[:RIM, at].astype(F32)).astype(BF16)
        change = now - was
        rate = rates[v * PACK]
        for g in range(1, PACK):
            rate = jnp.where(lane_group == g, rates[v * PACK + g], rate)
        chan_rates[:, at] = rate

        def effect(count):
            return (
                jnp.exp(rate * (-float(count - 1))) * change[0:1]
                + jnp.exp(rate * (-float(count - 2))) * change[1:2]
            )

        total[:, at] = total[:, at] + effect(tokens)
        amend[:, at] = effect(STEP)
        return carry

    with jax.named_scope("c_rim"):

        @pl.when(ctx > 0)
        def _():
            rim_copy.wait_recv()

    lax.fori_loop(0, blocks, amend_block, 0)

    passed_total[...] = total[...].astype(BF16)

    def sum_copy(d):
        return pltpu.make_async_remote_copy(
            src_ref=passed_total,
            dst_ref=totals.at[d - 1],
            send_sem=sum_send.at[d - 1],
            recv_sem=sum_recv.at[d - 1],
            device_id={"ctx": lax.rem(ctx + d, peers)},
            device_id_type=MESH,
        )

    for d in range(1, peers):

        @pl.when(ctx + d < peers)
        def _():
            sum_copy(d).start()

    def build(n, carry):
        for k in range(UNROLL):
            build_one(UNROLL * n + k)
        return carry

    def build_one(f):
        first = jnp.sum(scales[f] * jnp.exp(-rates[f] * back), axis=0, keepdims=True)
        turned = pltpu.roll(
            jnp.broadcast_to(first, (STEP, LANES)), 0, 1, stride=1, stride_axis=0
        )
        left[f, :, :LANES] = jnp.where(col <= row, turned, 0.0).astype(BF16)
        hi, lo = hi_lo(scale_row[pl.ds(f, 1), :] * jnp.exp(-rate_row[pl.ds(f, 1), :] * after))
        second = (col >= MODES) & (col < 2 * MODES)
        left[f, :, LANES:] = jnp.where(second, lo, hi).astype(BF16)

    def swap_again(v, carry):
        swap_in(v, 0, 1)
        return carry

    lax.fori_loop(0, blocks, swap_again, 0)
    with jax.named_scope("c_build"):
        lax.fori_loop(0, filters // UNROLL, build, 0)
    with jax.named_scope("c_sums"):
        for d in range(1, peers):

            @pl.when(ctx >= d)
            def _():
                sum_copy(d).wait_recv()

    for v in range(blocks):
        at = pl.ds(v * LANES, LANES)
        chan_rate = chan_rates[:, at]
        carried = jnp.zeros((MODES, LANES), F32)
        for d in range(1, peers):
            decay = jnp.exp(chan_rate * (-float((d - 1) * tokens)))
            carried = carried + jnp.where(ctx >= d, decay * totals[d - 1, :, at].astype(F32), 0.0)
        total[:, at] = carried

    def state_rows(v, carry):
        at = pl.ds(pl.multiple_of(v * LANES, LANES), LANES)
        incoming = total[:, at]
        amended = pltpu.roll(amend[:, at], GROUP, 1)
        for g in range(PACK):
            f = v * PACK + g
            place = (lane_group - g) & (PACK - 1)
            a = pltpu.roll(local[f, :, :LANES], GROUP, 1)
            b = pltpu.roll(local[f, :, LANES:], GROUP, 1)
            low = jnp.where(place == 0, incoming, a + jnp.where(place == 1, amended, 0.0))
            high = jnp.where(place == 0, a, b)
            states = jnp.concatenate(chunk_scan(low, high, rates[f], place), axis=1)
            hi, lo = hi_lo(states)
            source[f, STEP : STEP + 3 * MODES, :] = jnp.concatenate([hi, hi, lo], axis=0).astype(
                BF16
            )
        return carry

    with jax.named_scope("c_states"):
        lax.fori_loop(0, blocks, state_rows, 0)

    def far_pass(v):
        rows = pl.ds(pl.multiple_of(far * block, block), block)
        return pltpu.make_async_remote_copy(
            src_ref=mixed.at[rows, pl.ds(pl.multiple_of(v * LANES, LANES), LANES)],
            dst_ref=mixed.at[rows, pl.ds(pl.multiple_of(depth + v * LANES, LANES), LANES)],
            send_sem=pass_send.at[v],
            recv_sem=pass_recv.at[v],
            device_id=to_core,
            device_id_type=MESH,
        )

    def block_out(h, then=lambda v: None):
        def one_block(v, carry):
            at = pl.ds(pl.multiple_of(v * LANES, LANES), LANES)
            wide = pl.ds(pl.multiple_of(h * LANES, LANES), LANES)
            for g in range(PACK):
                f = v * PACK + g
                result[g] = jnp.dot(
                    left[f], source[f, :, wide], preferred_element_type=F32
                ).astype(BF16)

            def one_strip(s, inner):
                rows = pl.ds(pl.multiple_of(s * STRIP, STRIP), STRIP)
                parts = by_chunk([result[g, rows, :] for g in range(PACK)], lane_group)
                for k in range(PACK):
                    here = pl.ds(
                        pl.multiple_of((h * PACK + k) * STEP + s * STRIP, STRIP), STRIP
                    )
                    value = parts[k].astype(F32) + skip[:, at] * gated[here, at].astype(F32)
                    mixed[here, at] = (query[here, at].astype(F32) * value).astype(BF16)
                return inner

            for s in range(STEP // STRIP):
                one_strip(s, 0)
            then(v)
            return carry

        return one_block

    def passed_on(at):
        rows = pl.ds(pl.multiple_of(at * block, block), block)
        return sent(
            mixed.at[rows, pl.ds(0, depth)], mixed.at[rows, pl.ds(depth, depth)], to_core
        )

    first_half = far // 2
    with jax.named_scope("c_half1"):
        lax.fori_loop(0, blocks, block_out(first_half, lambda v: far_pass(v).start()), 0)
    passed = [passed_on(far + 1 - 2 * lax.rem(far, 2))]

    def tiles(token, rows, first, count, store):
        wide = count // TILE

        def one(n, carry, whole=True):
            i, j = (n // wide, lax.rem(n, wide)) if whole else (n, wide)
            r = pl.multiple_of(i * sub, sub)
            c = pl.multiple_of(j * TILE, TILE)
            size = TILE if whole else count - wide * TILE
            value = jnp.dot(
                mixed[pl.ds(pl.multiple_of(token + r, sub), sub), :],
                weight[:, pl.ds(pl.multiple_of(first + c, LANES), size)],
                preferred_element_type=F32,
            )
            store(pl.ds(r, sub), pl.ds(c, size), value)
            return carry

        lax.fori_loop(0, (rows // sub) * wide, one, 0)
        if count % TILE:
            lax.fori_loop(0, rows // sub, lambda n, carry: one(n, carry, False), 0)

    def start_of(at):
        return at * block

    def plain(dst, extra=()):
        def store(r, c, value):
            for e in extra:
                value = value + e[r, c].astype(F32)
            dst[r, c] = value.astype(BF16)

        return store

    mine, others = z * sub, (1 - z) * sub
    order = (far, right, lefts, x)
    bands = (others, mine)

    def z_first(k):
        at = order[k]
        tiles(start_of(at) + others, sub, half, rest, plain(z_send.at[k]))
        return sent(z_send.at[k], z_recv.at[k], to_z)

    with jax.named_scope("c_w_start"):
        load_weight.wait()
        weight_copy.wait_recv()
        for v in range(blocks):
            far_pass(v).wait_recv()
    starts, fars = [], ([], [])
    for part in (0, 1):
        first, size = z_parts[part]
        piece = pl.ds(first, size)
        view = z_send.at[0, :, piece]
        tiles(start_of(far) + others, sub, half + first, size, plain(view))
        starts.append(sent(view, z_recv.at[0, :, piece], to_z))
        for s, to in ((0, to_right), (1, to_left)):
            first, size = x_parts[s]
            rows, width = pl.ds(pl.multiple_of(bands[part], sub), sub), pl.ds(0, size)
            view = far_send.at[s, rows, width]
            tiles(start_of(far) + bands[part], sub, first, size, plain(view))
            fars[s].append(sent(view, far_recv.at[s, rows, width], to))

    with jax.named_scope("c_half2"):
        lax.fori_loop(0, blocks, block_out(1 - first_half), 0)
    passed += [passed_on(x + 1 - 2 * lax.rem(x, 2)), passed_on(x)]
    with jax.named_scope("c_w_passed"):
        for copy in passed:
            copy.wait_recv()
    zs = [None, z_first(1)]
    sides = ((0, right, to_right), (1, lefts, to_left))
    nears = ([], [])

    def near(s, side, part, at, to):
        first, size = x_parts[side]
        rows, width = pl.ds(pl.multiple_of(bands[part], sub), sub), pl.ds(0, size)
        view = near_send.at[s, side, rows, width]
        extra = ()
        if s == side:
            with jax.named_scope("c_w_far"):
                fars[s][part].wait_recv()
            extra = (far_recv.at[s, rows],)
        tiles(start_of(at) + bands[part], sub, first, size, plain(view, extra))
        nears[part].append(sent(view, near_recv.at[s, side, rows, width], to))

    for s, at, to in sides:
        near(s, 1 - s, 0, at, to)
    zs.append(z_first(2))
    for s, at, to in sides:
        near(s, s, 0, at, to)
    for s, at, to in sides:
        near(s, 1 - s, 1, at, to)
    zs.append(z_first(3))
    for s, at, to in sides:
        near(s, s, 1, at, to)

    with jax.named_scope("c_w_z0"):
        for copy in starts:
            copy.wait_recv()
    fars2 = []
    for s, to in ((0, to_right), (1, to_left)):
        first, size = z_parts[s]
        width = pl.ds(0, size)
        view = far2_send.at[s, :, width]
        tiles(
            start_of(far) + mine,
            sub,
            half + first,
            size,
            plain(view, (z_recv.at[0, :, pl.ds(first, size)],)),
        )
        fars2.append(sent(view, far2_recv.at[s, :, width], to))

    my_rows = pl.ds(pl.multiple_of(core * own, own), own)
    other_rows = pl.ds(pl.multiple_of((1 - core) * own, own), own)
    nears2, crosses = [], []

    def near2(s, side, at, to, extra):
        first, size = z_parts[side]
        width = pl.ds(0, size)
        view = near2_send.at[s, side, :, width]
        tiles(
            start_of(at) + mine,
            sub,
            half + first,
            size,
            plain(view, (z_recv.at[1 + s, :, pl.ds(first, size)],) + extra),
        )
        if s != side:
            nears2.append(sent(view, near2_recv.at[s, side, :, width], to))
            return
        view = near2_send.at[s, side, other_rows, width]
        across = {"chan_0": at, "chan_2": 1 - core}
        crosses.append(sent(view, cross_recv.at[s, :, width], across))
        view = near2_send.at[s, side, my_rows, width]
        crosses.append(sent(view, near2_recv.at[s, side, my_rows, width], to))

    for s, at, to in sides:
        with jax.named_scope("c_w_z12"):
            zs[1 + s].wait_recv()
        near2(s, 1 - s, at, to, ())
    with jax.named_scope("c_w_near"):
        for copy in nears[0]:
            copy.wait_recv()
    for side in (0, 1):
        first, size = x_parts[side]
        away = pl.ds(pl.multiple_of(others, sub), sub)
        tiles(
            start_of(x) + others,
            sub,
            first,
            size,
            plain(
                turn_send.at[:, pl.ds(first, size)],
                (near_recv.at[0, side, away], near_recv.at[1, side, away]),
            ),
        )
    turns = [
        sent(turn_send.at[other_rows], turn_recv.at[1], to_both),
        sent(turn_send.at[my_rows], turn_recv.at[0], to_z),
    ]

    for s, at, to in sides:
        with jax.named_scope("c_w_far2"):
            fars2[s].wait_recv()
        near2(s, s, at, to, (far2_recv.at[s],))

    def kept(offset, extra):
        def store(r, c, value):
            for e in extra:
                value = value + e[r, c].astype(F32)
            held[r, pl.ds(pl.multiple_of(offset + c.start, LANES), c.size)] = value

        return store

    with jax.named_scope("c_w_near1"):
        for copy in nears[1]:
            copy.wait_recv()
    for side in (0, 1):
        first, size = x_parts[side]
        here = pl.ds(pl.multiple_of(mine, sub), sub)
        tiles(
            start_of(x) + mine,
            sub,
            first,
            size,
            kept(first, (near_recv.at[0, side, here], near_recv.at[1, side, here])),
        )
    x_cols = pl.ds(0, half)
    last_x_send[...] = held[other_rows, x_cols].astype(BF16)
    last_x = sent(last_x_send, last_x_recv, to_core)
    with jax.named_scope("c_w_z3"):
        zs[3].wait_recv()
    for side in (0, 1):
        first, size = z_parts[side]
        tiles(
            start_of(x) + mine,
            sub,
            half + first,
            size,
            kept(half + first, (z_recv.at[3, :, pl.ds(first, size)],)),
        )
    my_first = pl.multiple_of(core * cols, cols)
    other_first = pl.multiple_of((1 - core) * cols, cols)
    with jax.named_scope("c_w_near2"):
        for copy in nears2:
            copy.wait_recv()
    for side in (0, 1):
        first, size = z_parts[side]
        last_z_send[:, first : first + size] = (
            held[other_rows, pl.ds(half + first, size)]
            + near2_recv[1 - side, side, other_rows, :size].astype(F32)
        ).astype(BF16)
    last_z = sent(last_z_send, last_z_recv, to_core)
    with jax.named_scope("c_w_turn"):
        last_x.wait_recv()
        turns[0].wait_recv()
    out_ref[:, pl.ds(other_first, half)] = (
        last_x_recv[...].astype(F32) + turn_recv[1].astype(F32)
    ).astype(BF16)
    with jax.named_scope("c_w_turn2"):
        turns[1].wait_recv()
    out_ref[:, pl.ds(my_first, half)] = (
        held[my_rows, x_cols] + turn_recv[0].astype(F32)
    ).astype(BF16)
    with jax.named_scope("c_w_last"):
        last_z.wait_recv()
    with jax.named_scope("c_w_cross"):
        for copy in crosses:
            copy.wait_recv()
    for side in (0, 1):
        first, size = z_parts[side]
        out_ref[:, pl.ds(pl.multiple_of(my_first + half + first, LANES), size)] = (
            held[my_rows, pl.ds(half + first, size)]
            + near2_recv[0, side, my_rows, :size].astype(F32)
            + near2_recv[1, side, my_rows, :size].astype(F32)
        ).astype(BF16)
        out_ref[:, pl.ds(pl.multiple_of(other_first + half + first, LANES), size)] = (
            last_z_recv[:, first : first + size].astype(F32)
            + cross_recv[side, :, :size].astype(F32)
        ).astype(BF16)
    for v in range(blocks):
        far_pass(v).wait_send()

    @pl.when(ctx < peers - 1)
    def _():
        rim_copy.wait_send()

    for d in range(1, peers):

        @pl.when(ctx + d < peers)
        def _():
            sum_copy(d).wait_send()

    for copy in used:
        copy.wait_send()


def on_device(featurized, short_filter, decay_rate, residue, skip_gain, weight):
    tokens, _, channels = featurized.shape
    filters = decay_rate.shape[0]
    peers = lax.axis_size("ctx")
    chunks = tokens // STEP
    width = chunks * GROUP
    outs = weight.shape[1]
    cols = outs // 2
    half, x_parts, z_parts = column_parts(cols)
    rest = cols - half
    x_most = max(size for _, size in x_parts)
    z_most = max(size for _, size in z_parts)
    block = tokens // 4
    sub = block // 2
    own = sub // 2
    pairs = [
        (4, sub, rest),
        (2, block, x_most),
        (2, 2, block, x_most),
        (2, sub, z_most),
        (2, 2, sub, z_most),
    ]
    return pl.pallas_call(
        kernel,
        out_shape=jax.ShapeDtypeStruct((own, outs), BF16),
        in_specs=[pl.BlockSpec(memory_space=pltpu.HBM)] * 6,
        out_specs=pl.BlockSpec(memory_space=pltpu.VMEM),
        scratch_shapes=[
            pltpu.VMEM((3, tokens, channels), BF16),
            pltpu.VMEM(short_filter.shape, F32),
            pltpu.VMEM((MODES, filters), F32),
            pltpu.VMEM((MODES, filters), F32),
            pltpu.VMEM((channels,), F32),
            pltpu.VMEM((1, channels), F32),
            pltpu.VMEM((LANES, LANES), F32),
            pltpu.VMEM((filters, LANES), F32),
            pltpu.VMEM((filters, LANES), F32),
            pltpu.VMEM((filters, MODES, LANES), F32),
            pltpu.VMEM((filters, MODES, LANES), F32),
            pltpu.VMEM((3, RIM, channels), BF16),
            pltpu.VMEM((UNROLL, 3, RIM + STEP, LANES), F32),
            pltpu.VMEM((tokens, channels), BF16),
            pltpu.VMEM((tokens, channels), BF16),
            pltpu.VMEM((filters, 2 * STEP, width), BF16),
            pltpu.VMEM((filters, STEP, 2 * LANES), BF16),
            pltpu.VMEM((filters, MODES, width), F32),
            pltpu.VMEM((MODES, channels), F32),
            pltpu.VMEM((MODES, channels), F32),
            pltpu.VMEM((MODES, channels), F32),
            pltpu.VMEM((MODES, channels), BF16),
            pltpu.VMEM((peers - 1, MODES, channels), BF16),
            pltpu.VMEM((PACK, STEP, LANES), BF16),
            pltpu.VMEM((tokens, 2 * channels), BF16),
            pltpu.VMEM((2 * channels, cols), BF16),
        ]
        + [pltpu.VMEM(shape, BF16) for shape in pairs for _ in range(2)]
        + [
            pltpu.VMEM((2, own, z_most), BF16),
            pltpu.VMEM((sub, half), BF16),
            pltpu.VMEM((2, own, half), BF16),
            pltpu.VMEM((sub, cols), F32),
            pltpu.VMEM((own, half), BF16),
            pltpu.VMEM((own, half), BF16),
            pltpu.VMEM((own, rest), BF16),
            pltpu.VMEM((own, rest), BF16),
            pltpu.SemaphoreType.DMA((channels // LANES,)),
            pltpu.SemaphoreType.DMA((channels // LANES,)),
            pltpu.SemaphoreType.DMA((4,)),
            pltpu.SemaphoreType.DMA((channels // LANES + 1,)),
            pltpu.SemaphoreType.DMA((2,)),
            pltpu.SemaphoreType.DMA((peers - 1,)),
            pltpu.SemaphoreType.DMA((peers - 1,)),
            pltpu.SemaphoreType.DMA((COPIES,)),
            pltpu.SemaphoreType.DMA((COPIES,)),
        ],
        compiler_params=pltpu.CompilerParams(
            collective_id=0, has_side_effects=True, vmem_limit_bytes=50 * 2**20
        ),
        name="hyena",
    )(
        *(
            pltpu.with_memory_space_constraint(array, pltpu.HBM)
            for array in (
                featurized.transpose(1, 0, 2),
                short_filter,
                decay_rate.T,
                residue.T,
                skip_gain,
                weight,
            )
        )
    )


def solution(mesh):
    finer = Mesh(
        mesh.devices.reshape(mesh.shape["ctx"], 4, 2, 2), ("ctx", "chan_0", "chan_1", "chan_2")
    )
    placed = (
        P("ctx", None, CHAN),
        P(None, None, CHAN),
        P(CHAN, None),
        P(CHAN, None),
        P(CHAN),
        P(CHAN, None),
    )
    return jax.shard_map(
        on_device, mesh=finer, in_specs=placed, out_specs=P(CTX_CHAN, None), check_vma=False
    )
```

```python
import jax
import jax.numpy as jnp
from jax import lax
from jax.experimental import pallas as pl
from jax.experimental.pallas import tpu as pltpu
from jax.sharding import Mesh
from jax.sharding import PartitionSpec as P

CHAN = ("chan_0", "chan_1", "chan_2")
CTX_CHAN = ("ctx", "chan_0", "chan_1", "chan_2")
MESH = pl.DeviceIdType.MESH
F32 = jnp.float32
BF16 = jnp.bfloat16
LANES = 128
TILE = 256
COPIES = 33
UNROLL = 4
STEP = 128
GROUP = 16
PACK = LANES // GROUP
MODES = 16
STRIP = 32
RIM = 16


def turned_to(parts, lane_group, sign):
    for bit in (1, 2, 4):
        move = (lane_group & bit) != 0
        parts = [
            jnp.where(move, parts[(k + sign * bit) % PACK], parts[k]) for k in range(PACK)
        ]
    return parts


def by_filter(parts, lane_group):
    parts = [pltpu.roll(part, k * GROUP, 1) if k else part for k, part in enumerate(parts)]
    parts = turned_to(parts, lane_group, 1)
    return [parts[-g % PACK] for g in range(PACK)]


def by_chunk(parts, lane_group):
    parts = turned_to([parts[-k % PACK] for k in range(PACK)], lane_group, -1)
    return [pltpu.roll(part, LANES - k * GROUP, 1) if k else part for k, part in enumerate(parts)]


def hi_lo(value):
    hi = value.astype(BF16).astype(F32)
    return hi, value - hi


def one_less_exp(x):
    series = jnp.ones_like(x)
    for n in range(9, 1, -1):
        series = 1.0 - x * (1.0 / n) * series
    return jnp.where(x < 0.5, x * series, 1.0 - jnp.exp(-x))


def chunk_scan(low, high, rate, place):
    for hop in (1, 2, 4):
        decay = jnp.exp(rate * (-float(hop * STEP)))
        inside = place >= hop
        a, b = pltpu.roll(low, hop * GROUP, 1), pltpu.roll(high, hop * GROUP, 1)
        low, high = (
            low + decay * jnp.where(inside, a, 0.0),
            high + decay * jnp.where(inside, b, a),
        )
    return low, high + jnp.exp(rate * (-float(PACK * STEP))) * low


def column_parts(cols):
    half = cols * 9 // 16
    split = cols * 5 // 16
    later = cols * 3 // 16
    x_parts = ((0, split), (split, half - split))
    z_parts = ((0, later), (later, cols - half - later))
    return half, x_parts, z_parts


def kernel(
    feat_hbm,
    taps_hbm,
    rate_hbm,
    residue_hbm,
    skip_hbm,
    weight_hbm,
    out_ref,
    feat,
    taps,
    rate_in,
    residue_in,
    skip_in,
    skip,
    square,
    rate_row,
    scale_row,
    rates,
    scales,
    rim,
    shifts,
    gated,
    query,
    source,
    left,
    local,
    chan_rates,
    amend,
    total,
    passed_total,
    totals,
    result,
    mixed,
    weight,
    z_send,
    z_recv,
    far_send,
    far_recv,
    near_send,
    near_recv,
    far2_send,
    far2_recv,
    near2_send,
    near2_recv,
    cross_recv,
    turn_send,
    turn_recv,
    held,
    last_x_send,
    last_x_recv,
    last_z_send,
    last_z_recv,
    pass_send,
    pass_recv,
    small_sem,
    load_sem,
    rim_sem,
    sum_send,
    sum_recv,
    send_sem,
    recv_sem,
):
    tokens, channels = feat.shape[1], feat.shape[2]
    filters = rates.shape[0]
    chunks = tokens // STEP
    blocks = channels // LANES
    width = chunks * GROUP
    halves = width // LANES
    depth = channels
    cols = weight.shape[1]
    half, x_parts, z_parts = column_parts(cols)
    rest = cols - half
    block = tokens // 4
    sub = block // 2
    own = sub // 2
    ctx = lax.axis_index("ctx")
    peers = lax.axis_size("ctx")
    x = lax.axis_index("chan_0")
    z = lax.axis_index("chan_1")
    core = lax.axis_index("chan_2")
    right, far, lefts = lax.rem(x + 1, 4), lax.rem(x + 2, 4), lax.rem(x + 3, 4)
    to_right, to_left = {"chan_0": right}, {"chan_0": lefts}
    to_z, to_core = {"chan_1": 1 - z}, {"chan_2": 1 - core}
    to_both = {"chan_1": 1 - z, "chan_2": 1 - core}

    smalls = []
    for k, (here, there) in enumerate(
        (
            (taps_hbm, taps),
            (rate_hbm, rate_in),
            (residue_hbm, residue_in),
            (skip_hbm, skip_in),
        )
    ):
        copy = pltpu.make_async_copy(here, there, small_sem.at[k])
        copy.start()
        smalls.append(copy)

    def load_of(v):
        at = pl.ds(pl.multiple_of(v * LANES, LANES), LANES)
        return pltpu.make_async_copy(feat_hbm.at[:, :, at], feat.at[:, :, at], load_sem.at[v])

    for v in range(2):
        load_of(v).start()
    my_cols = pl.ds(pl.multiple_of(core * cols, cols), cols)
    other_cols = pl.ds(pl.multiple_of((1 - core) * cols, cols), cols)
    load_weight = pltpu.make_async_copy(
        weight_hbm.at[:, my_cols], weight.at[pl.ds(0, depth), :], load_sem.at[blocks]
    )

    rim[...] = jnp.zeros_like(rim)
    totals[...] = jnp.zeros_like(totals)
    barrier = pltpu.get_barrier_semaphore()
    greeted = [{"ctx": lax.rem(ctx + d, peers)} for d in range(1, peers)]
    greeted += [to_right, to_left, to_z, to_core, to_both]
    greeted += [{"chan_0": right, "chan_2": 1 - core}, {"chan_0": lefts, "chan_2": 1 - core}]
    for to in greeted:
        pl.semaphore_signal(barrier, inc=1, device_id=to, device_id_type=MESH)

    lane = lax.broadcasted_iota(jnp.int32, (1, LANES), 1)
    lane_group = lane // GROUP
    lane_mode = lax.broadcasted_iota(jnp.int32, (MODES, LANES), 1)
    row = lax.broadcasted_iota(jnp.int32, (STEP, LANES), 0)
    col = lax.broadcasted_iota(jnp.int32, (STEP, LANES), 1)
    after = (row + 1).astype(F32)
    back = lax.rem(STEP - lane_mode, STEP).astype(F32)
    ahead = (STEP - 1 - lane_mode).astype(F32)

    def shortened(i, v, c, slot, outside):
        at = pl.ds(pl.multiple_of(v * LANES, LANES), LANES)
        here = pl.ds(pl.multiple_of(c * STEP, STEP), STEP)
        before = pl.ds(pl.multiple_of(jnp.maximum(c * STEP - RIM, 0), RIM), RIM)
        now = feat[i, here, at].astype(F32)
        shifts[slot, i, :RIM] = jnp.where(c > 0, feat[i, before, at].astype(F32), outside)
        shifts[slot, i, RIM:] = now
        tap = taps[:, i, at]
        return (
            tap[0:1] * now
            + tap[1:2] * shifts[slot, i, RIM - 1 : RIM - 1 + STEP]
            + tap[2:3] * shifts[slot, i, RIM - 2 : RIM - 2 + STEP]
        )

    def gate(v, c, slot):
        at = pl.ds(pl.multiple_of(v * LANES, LANES), LANES)
        here = pl.ds(pl.multiple_of(c * STEP, STEP), STEP)
        key = shortened(1, v, c, slot, 0.0)
        gated[here, at] = (key * shortened(2, v, c, slot, 0.0)).astype(BF16)

    def query_block(v, carry):
        at = pl.ds(pl.multiple_of(v * LANES, LANES), LANES)

        def some_chunks(n, inner):
            for k in range(UNROLL):
                c = UNROLL * n + k
                here = pl.ds(pl.multiple_of(c * STEP, STEP), STEP)
                value = shortened(0, v, c, k, rim[0, :, at].astype(F32))
                query[here, at] = value.astype(BF16)
            return inner

        lax.fori_loop(0, chunks // UNROLL, some_chunks, 0)
        return carry

    def gate_block(v, carry):
        load_of(v).wait()

        @pl.when(v + 2 < blocks)
        def _():
            load_of(v + 2).start()

        def some_chunks(c, inner):
            for k in range(UNROLL):
                gate(v, UNROLL * c + k, k)
            return inner

        with jax.named_scope("c_gate"):
            lax.fori_loop(0, chunks // UNROLL, some_chunks, 0)
        return carry

    def swap_in(v, h, strips=STEP // STRIP):
        at = pl.ds(pl.multiple_of(v * LANES, LANES), LANES)

        def one_strip(s, inner):
            rows = pl.ds(pl.multiple_of(s * STRIP, STRIP), STRIP)
            parts = []
            for k in range(PACK):
                here = pl.ds(pl.multiple_of((h * PACK + k) * STEP + s * STRIP, STRIP), STRIP)
                parts.append(gated[here, at])
            for g, part in enumerate(by_filter(parts, lane_group)):
                source[v * PACK + g, rows, h * LANES : (h + 1) * LANES] = part
            return inner

        for s in range(strips):
            one_strip(s, 0)

    smalls[0].wait()
    lax.fori_loop(0, 2, gate_block, 0)
    load_weight.start()

    with jax.named_scope("c_smalls"):
        for copy in smalls[1:]:
            copy.wait()
    rate_all = rate_in[...]
    scale_all = residue_in[...] * jnp.sqrt(one_less_exp(2.0 * rate_all))
    for f in range(filters):
        rates[f] = jnp.broadcast_to(rate_all[:, f : f + 1], (MODES, LANES))
        scales[f] = jnp.broadcast_to(scale_all[:, f : f + 1], (MODES, LANES))
    square[...] = jnp.zeros_like(square)
    for k in range(3):
        square[k * MODES : (k + 1) * MODES, 0:filters] = rate_all
    rate_row[...] = square[...].T[:filters]
    for k in range(3):
        square[k * MODES : (k + 1) * MODES, 0:filters] = scale_all
    scale_row[...] = square[...].T[:filters]
    skip[...] = skip_in[...].reshape(1, channels)
    source[:, STEP + 3 * MODES :, :] = jnp.zeros(
        (filters, source.shape[1] - STEP - 3 * MODES, width), BF16
    )

    with jax.named_scope("c_barrier"):
        pl.semaphore_wait(barrier, len(greeted))
    rim_copy = pltpu.make_async_remote_copy(
        src_ref=feat_hbm.at[:, pl.ds(tokens - RIM, RIM), :],
        dst_ref=rim,
        send_sem=rim_sem.at[0],
        recv_sem=rim_sem.at[1],
        device_id={"ctx": lax.rem(ctx + 1, peers)},
        device_id_type=MESH,
    )

    @pl.when(ctx < peers - 1)
    def _():
        rim_copy.start()

    used = []

    def sent(src, dst, to):
        k = len(used)
        copy = pltpu.make_async_remote_copy(
            src_ref=src,
            dst_ref=dst,
            send_sem=send_sem.at[k],
            recv_sem=recv_sem.at[k],
            device_id=to,
            device_id_type=MESH,
        )
        copy.start()
        used.append(copy)
        return copy

    weight_copy = sent(weight_hbm.at[:, other_cols], weight.at[pl.ds(depth, depth), :], to_core)

    lax.fori_loop(2, blocks, gate_block, 0)

    def state_block(v, carry):
        at = pl.ds(pl.multiple_of(v * LANES, LANES), LANES)
        for h in range(halves):
            swap_in(v, h)
        packed = jnp.zeros((MODES, LANES), F32)
        for g in range(PACK):
            f = v * PACK + g
            rate = rates[f]
            hi, lo = hi_lo(jnp.exp(-rate * ahead))
            factor = jnp.concatenate([hi, lo], axis=0).astype(BF16)
            product = jnp.dot(factor, source[f, :STEP, :], preferred_element_type=F32)
            ends = product[:MODES] + product[MODES:]
            local[f] = ends
            place = (lane_group - g) & (PACK - 1)
            decay = jnp.exp(-rate * ((PACK - 1 - place) * STEP).astype(F32))
            whole = jnp.exp(rate * (-float(PACK * STEP)))
            last = decay * (whole * ends[:, :LANES] + ends[:, LANES:])
            for hop in (1, 2, 4):
                last = last + pltpu.roll(last, hop * GROUP, 1)
            packed = jnp.where(lane_group == g, last, packed)
        total[:, at] = packed
        return carry

    with jax.named_scope("c_state"):
        lax.fori_loop(0, blocks, state_block, 0)

    def amend_block(v, carry):
        at = pl.ds(pl.multiple_of(v * LANES, LANES), LANES)
        parts = []
        for i in (1, 2):
            rows = jnp.concatenate([rim[i, :, at], feat[i, :RIM, at]], axis=0).astype(F32)
            tap = taps[:, i, at]
            value = (
                tap[0:1] * rows[RIM:]
                + tap[1:2] * pltpu.roll(rows, 1, 0)[RIM:]
                + tap[2:3] * pltpu.roll(rows, 2, 0)[RIM:]
            )
            parts.append(value)
        new = (lax.broadcasted_iota(jnp.int32, (RIM, LANES), 0) < 2) & (ctx > 0)
        was = gated[:RIM, at].astype(F32)
        now = jnp.where(new, (parts[0] * parts[1]).astype(BF16).astype(F32), was)
        gated[:RIM, at] = now.astype(BF16)
        change = now - was
        rate = rates[v * PACK]
        for g in range(1, PACK):
            rate = jnp.where(lane_group == g, rates[v * PACK + g], rate)
        chan_rates[:, at] = rate

        def effect(count):
            return (
                jnp.exp(rate * (-float(count - 1))) * change[0:1]
                + jnp.exp(rate * (-float(count - 2))) * change[1:2]
            )

        total[:, at] = total[:, at] + effect(tokens)
        amend[:, at] = effect(STEP)
        return carry

    with jax.named_scope("c_rim"):

        @pl.when(ctx > 0)
        def _():
            rim_copy.wait_recv()

    lax.fori_loop(0, blocks, amend_block, 0)

    passed_total[...] = total[...].astype(BF16)

    def sum_copy(d):
        return pltpu.make_async_remote_copy(
            src_ref=passed_total,
            dst_ref=totals.at[d - 1],
            send_sem=sum_send.at[d - 1],
            recv_sem=sum_recv.at[d - 1],
            device_id={"ctx": lax.rem(ctx + d, peers)},
            device_id_type=MESH,
        )

    for d in range(1, peers):

        @pl.when(ctx + d < peers)
        def _():
            sum_copy(d).start()

    def build(n, carry):
        for k in range(UNROLL):
            build_one(UNROLL * n + k)
        return carry

    def build_one(f):
        first = jnp.sum(scales[f] * jnp.exp(-rates[f] * back), axis=0, keepdims=True)
        turned = pltpu.roll(
            jnp.broadcast_to(first, (STEP, LANES)), 0, 1, stride=1, stride_axis=0
        )
        left[f, :, :LANES] = jnp.where(col <= row, turned, 0.0).astype(BF16)
        hi, lo = hi_lo(scale_row[pl.ds(f, 1), :] * jnp.exp(-rate_row[pl.ds(f, 1), :] * after))
        second = (col >= MODES) & (col < 2 * MODES)
        left[f, :, LANES:] = jnp.where(second, lo, hi).astype(BF16)

    def swap_again(v, carry):
        swap_in(v, 0, 1)
        return carry

    lax.fori_loop(0, blocks, swap_again, 0)
    with jax.named_scope("c_query"):
        lax.fori_loop(0, blocks, query_block, 0)
    with jax.named_scope("c_build"):
        lax.fori_loop(0, filters // UNROLL, build, 0)
    with jax.named_scope("c_sums"):
        for d in range(1, peers):

            @pl.when(ctx >= d)
            def _():
                sum_copy(d).wait_recv()

    for v in range(blocks):
        at = pl.ds(v * LANES, LANES)
        chan_rate = chan_rates[:, at]
        carried = jnp.zeros((MODES, LANES), F32)
        for d in range(1, peers):
            decay = jnp.exp(chan_rate * (-float((d - 1) * tokens)))
            carried = carried + jnp.where(ctx >= d, decay * totals[d - 1, :, at].astype(F32), 0.0)
        total[:, at] = carried

    def state_rows(v, carry):
        at = pl.ds(pl.multiple_of(v * LANES, LANES), LANES)
        incoming = total[:, at]
        amended = pltpu.roll(amend[:, at], GROUP, 1)
        for g in range(PACK):
            f = v * PACK + g
            place = (lane_group - g) & (PACK - 1)
            a = pltpu.roll(local[f, :, :LANES], GROUP, 1)
            b = pltpu.roll(local[f, :, LANES:], GROUP, 1)
            low = jnp.where(place == 0, incoming, a + jnp.where(place == 1, amended, 0.0))
            high = jnp.where(place == 0, a, b)
            states = jnp.concatenate(chunk_scan(low, high, rates[f], place), axis=1)
            hi, lo = hi_lo(states)
            source[f, STEP : STEP + 3 * MODES, :] = jnp.concatenate([hi, hi, lo], axis=0).astype(
                BF16
            )
        return carry

    with jax.named_scope("c_states"):
        lax.fori_loop(0, blocks, state_rows, 0)

    def far_pass(v):
        rows = pl.ds(pl.multiple_of(far * block, block), block)
        return pltpu.make_async_remote_copy(
            src_ref=mixed.at[rows, pl.ds(pl.multiple_of(v * LANES, LANES), LANES)],
            dst_ref=mixed.at[rows, pl.ds(pl.multiple_of(depth + v * LANES, LANES), LANES)],
            send_sem=pass_send.at[v],
            recv_sem=pass_recv.at[v],
            device_id=to_core,
            device_id_type=MESH,
        )

    def block_out(h, then=lambda v: None):
        def one_block(v, carry):
            at = pl.ds(pl.multiple_of(v * LANES, LANES), LANES)
            wide = pl.ds(pl.multiple_of(h * LANES, LANES), LANES)
            for g in range(PACK):
                f = v * PACK + g
                result[g] = jnp.dot(
                    left[f], source[f, :, wide], preferred_element_type=F32
                ).astype(BF16)

            def one_strip(s, inner):
                rows = pl.ds(pl.multiple_of(s * STRIP, STRIP), STRIP)
                parts = by_chunk([result[g, rows, :] for g in range(PACK)], lane_group)
                for k in range(PACK):
                    here = pl.ds(
                        pl.multiple_of((h * PACK + k) * STEP + s * STRIP, STRIP), STRIP
                    )
                    value = parts[k].astype(F32) + skip[:, at] * gated[here, at].astype(F32)
                    mixed[here, at] = (query[here, at].astype(F32) * value).astype(BF16)
                return inner

            for s in range(STEP // STRIP):
                one_strip(s, 0)
            then(v)
            return carry

        return one_block

    def passed_on(at):
        rows = pl.ds(pl.multiple_of(at * block, block), block)
        return sent(
            mixed.at[rows, pl.ds(0, depth)], mixed.at[rows, pl.ds(depth, depth)], to_core
        )

    first_half = far // 2
    with jax.named_scope("c_half1"):
        lax.fori_loop(0, blocks, block_out(first_half, lambda v: far_pass(v).start()), 0)
    passed = [passed_on(far + 1 - 2 * lax.rem(far, 2))]

    def tiles(token, rows, first, count, store):
        wide = count // TILE

        def one(n, carry, whole=True):
            i, j = (n // wide, lax.rem(n, wide)) if whole else (n, wide)
            r = pl.multiple_of(i * sub, sub)
            c = pl.multiple_of(j * TILE, TILE)
            size = TILE if whole else count - wide * TILE
            value = jnp.dot(
                mixed[pl.ds(pl.multiple_of(token + r, sub), sub), :],
                weight[:, pl.ds(pl.multiple_of(first + c, LANES), size)],
                preferred_element_type=F32,
            )
            store(pl.ds(r, sub), pl.ds(c, size), value)
            return carry

        lax.fori_loop(0, (rows // sub) * wide, one, 0)
        if count % TILE:
            lax.fori_loop(0, rows // sub, lambda n, carry: one(n, carry, False), 0)

    def start_of(at):
        return at * block

    def plain(dst, extra=()):
        def store(r, c, value):
            for e in extra:
                value = value + e[r, c].astype(F32)
            dst[r, c] = value.astype(BF16)

        return store

    mine, others = z * sub, (1 - z) * sub
    order = (far, right, lefts, x)
    bands = (others, mine)

    def z_first(k):
        at = order[k]
        tiles(start_of(at) + others, sub, half, rest, plain(z_send.at[k]))
        return sent(z_send.at[k], z_recv.at[k], to_z)

    with jax.named_scope("c_w_start"):
        load_weight.wait()
        weight_copy.wait_recv()
        for v in range(blocks):
            far_pass(v).wait_recv()
    starts, fars = [], ([], [])
    for part in (0, 1):
        for s, to in ((0, to_right), (1, to_left)):
            first, size = x_parts[s]
            rows, width = pl.ds(pl.multiple_of(bands[part], sub), sub), pl.ds(0, size)
            view = far_send.at[s, rows, width]
            tiles(start_of(far) + bands[part], sub, first, size, plain(view))
            fars[s].append(sent(view, far_recv.at[s, rows, width], to))
        first, size = z_parts[part]
        piece = pl.ds(first, size)
        view = z_send.at[0, :, piece]
        tiles(start_of(far) + others, sub, half + first, size, plain(view))
        starts.append(sent(view, z_recv.at[0, :, piece], to_z))

    with jax.named_scope("c_half2"):
        lax.fori_loop(0, blocks, block_out(1 - first_half), 0)
    passed += [passed_on(x + 1 - 2 * lax.rem(x, 2)), passed_on(x)]
    with jax.named_scope("c_w_passed"):
        for copy in passed:
            copy.wait_recv()
    zs = [None, z_first(1)]
    sides = ((0, right, to_right), (1, lefts, to_left))
    nears = ([], [])

    def near(s, side, part, at, to):
        first, size = x_parts[side]
        rows, width = pl.ds(pl.multiple_of(bands[part], sub), sub), pl.ds(0, size)
        view = near_send.at[s, side, rows, width]
        extra = ()
        if s == side:
            with jax.named_scope("c_w_far"):
                fars[s][part].wait_recv()
            extra = (far_recv.at[s, rows],)
        tiles(start_of(at) + bands[part], sub, first, size, plain(view, extra))
        nears[part].append(sent(view, near_recv.at[s, side, rows, width], to))

    for s, at, to in sides:
        near(s, 1 - s, 0, at, to)
    zs.append(z_first(2))
    for s, at, to in sides:
        near(s, s, 0, at, to)
    with jax.named_scope("c_w_z0"):
        for copy in starts:
            copy.wait_recv()
    fars2 = []
    for s, to in ((0, to_right), (1, to_left)):
        first, size = z_parts[s]
        width = pl.ds(0, size)
        view = far2_send.at[s, :, width]
        tiles(
            start_of(far) + mine,
            sub,
            half + first,
            size,
            plain(view, (z_recv.at[0, :, pl.ds(first, size)],)),
        )
        fars2.append(sent(view, far2_recv.at[s, :, width], to))

    for s, at, to in sides:
        near(s, 1 - s, 1, at, to)
    zs.append(z_first(3))
    for s, at, to in sides:
        near(s, s, 1, at, to)

    my_rows = pl.ds(pl.multiple_of(core * own, own), own)
    other_rows = pl.ds(pl.multiple_of((1 - core) * own, own), own)
    nears2, crosses = [], []

    def near2(s, side, at, to, extra):
        first, size = z_parts[side]
        width = pl.ds(0, size)
        view = near2_send.at[s, side, :, width]
        tiles(
            start_of(at) + mine,
            sub,
            half + first,
            size,
            plain(view, (z_recv.at[1 + s, :, pl.ds(first, size)],) + extra),
        )
        if s != side:
            nears2.append(sent(view, near2_recv.at[s, side, :, width], to))
            return
        view = near2_send.at[s, side, other_rows, width]
        across = {"chan_0": at, "chan_2": 1 - core}
        crosses.append(sent(view, cross_recv.at[s, :, width], across))
        view = near2_send.at[s, side, my_rows, width]
        crosses.append(sent(view, near2_recv.at[s, side, my_rows, width], to))

    for s, at, to in sides:
        with jax.named_scope("c_w_z12"):
            zs[1 + s].wait_recv()
        near2(s, 1 - s, at, to, ())
    for s, at, to in sides:
        with jax.named_scope("c_w_far2"):
            fars2[s].wait_recv()
        near2(s, s, at, to, (far2_recv.at[s],))

    with jax.named_scope("c_w_near"):
        for copy in nears[0]:
            copy.wait_recv()
    for side in (0, 1):
        first, size = x_parts[side]
        away = pl.ds(pl.multiple_of(others, sub), sub)
        tiles(
            start_of(x) + others,
            sub,
            first,
            size,
            plain(
                turn_send.at[:, pl.ds(first, size)],
                (near_recv.at[0, side, away], near_recv.at[1, side, away]),
            ),
        )
    turns = [
        sent(turn_send.at[other_rows], turn_recv.at[1], to_both),
        sent(turn_send.at[my_rows], turn_recv.at[0], to_z),
    ]

    def kept(offset, extra):
        def store(r, c, value):
            for e in extra:
                value = value + e[r, c].astype(F32)
            held[r, pl.ds(pl.multiple_of(offset + c.start, LANES), c.size)] = value

        return store

    with jax.named_scope("c_w_near1"):
        for copy in nears[1]:
            copy.wait_recv()
    for side in (0, 1):
        first, size = x_parts[side]
        here = pl.ds(pl.multiple_of(mine, sub), sub)
        tiles(
            start_of(x) + mine,
            sub,
            first,
            size,
            kept(first, (near_recv.at[0, side, here], near_recv.at[1, side, here])),
        )
    x_cols = pl.ds(0, half)
    last_x_send[...] = held[other_rows, x_cols].astype(BF16)
    last_x = sent(last_x_send, last_x_recv, to_core)
    with jax.named_scope("c_w_z3"):
        zs[3].wait_recv()
    for side in (0, 1):
        first, size = z_parts[side]
        tiles(
            start_of(x) + mine,
            sub,
            half + first,
            size,
            kept(half + first, (z_recv.at[3, :, pl.ds(first, size)],)),
        )
    my_first = pl.multiple_of(core * cols, cols)
    other_first = pl.multiple_of((1 - core) * cols, cols)
    with jax.named_scope("c_w_near2"):
        for copy in nears2:
            copy.wait_recv()
    for side in (0, 1):
        first, size = z_parts[side]
        last_z_send[:, first : first + size] = (
            held[other_rows, pl.ds(half + first, size)]
            + near2_recv[1 - side, side, other_rows, :size].astype(F32)
        ).astype(BF16)
        held[my_rows, pl.ds(half + first, size)] = (
            held[my_rows, pl.ds(half + first, size)]
            + near2_recv[1 - side, side, my_rows, :size].astype(F32)
        )
    last_z = sent(last_z_send, last_z_recv, to_core)
    with jax.named_scope("c_w_turn"):
        last_x.wait_recv()
        turns[0].wait_recv()
    out_ref[:, pl.ds(other_first, half)] = (
        last_x_recv[...].astype(F32) + turn_recv[1].astype(F32)
    ).astype(BF16)
    with jax.named_scope("c_w_turn2"):
        turns[1].wait_recv()
    out_ref[:, pl.ds(my_first, half)] = (
        held[my_rows, x_cols] + turn_recv[0].astype(F32)
    ).astype(BF16)
    with jax.named_scope("c_w_last"):
        last_z.wait_recv()
    with jax.named_scope("c_w_cross"):
        for copy in crosses:
            copy.wait_recv()
    for side in (0, 1):
        first, size = z_parts[side]
        out_ref[:, pl.ds(pl.multiple_of(my_first + half + first, LANES), size)] = (
            held[my_rows, pl.ds(half + first, size)]
            + near2_recv[side, side, my_rows, :size].astype(F32)
        ).astype(BF16)
        out_ref[:, pl.ds(pl.multiple_of(other_first + half + first, LANES), size)] = (
            last_z_recv[:, first : first + size].astype(F32)
            + cross_recv[side, :, :size].astype(F32)
        ).astype(BF16)
    for v in range(blocks):
        far_pass(v).wait_send()

    @pl.when(ctx < peers - 1)
    def _():
        rim_copy.wait_send()

    for d in range(1, peers):

        @pl.when(ctx + d < peers)
        def _():
            sum_copy(d).wait_send()

    for copy in used:
        copy.wait_send()


def on_device(featurized, short_filter, decay_rate, residue, skip_gain, weight):
    tokens, _, channels = featurized.shape
    filters = decay_rate.shape[0]
    peers = lax.axis_size("ctx")
    chunks = tokens // STEP
    width = chunks * GROUP
    outs = weight.shape[1]
    cols = outs // 2
    half, x_parts, z_parts = column_parts(cols)
    rest = cols - half
    x_most = max(size for _, size in x_parts)
    z_most = max(size for _, size in z_parts)
    block = tokens // 4
    sub = block // 2
    own = sub // 2
    pairs = [
        (4, sub, rest),
        (2, block, x_most),
        (2, 2, block, x_most),
        (2, sub, z_most),
        (2, 2, sub, z_most),
    ]
    return pl.pallas_call(
        kernel,
        out_shape=jax.ShapeDtypeStruct((own, outs), BF16),
        in_specs=[pl.BlockSpec(memory_space=pltpu.HBM)] * 6,
        out_specs=pl.BlockSpec(memory_space=pltpu.VMEM),
        scratch_shapes=[
            pltpu.VMEM((3, tokens, channels), BF16),
            pltpu.VMEM(short_filter.shape, F32),
            pltpu.VMEM((MODES, filters), F32),
            pltpu.VMEM((MODES, filters), F32),
            pltpu.VMEM((channels,), F32),
            pltpu.VMEM((1, channels), F32),
            pltpu.VMEM((LANES, LANES), F32),
            pltpu.VMEM((filters, LANES), F32),
            pltpu.VMEM((filters, LANES), F32),
            pltpu.VMEM((filters, MODES, LANES), F32),
            pltpu.VMEM((filters, MODES, LANES), F32),
            pltpu.VMEM((3, RIM, channels), BF16),
            pltpu.VMEM((UNROLL, 3, RIM + STEP, LANES), F32),
            pltpu.VMEM((tokens, channels), BF16),
            pltpu.VMEM((tokens, channels), BF16),
            pltpu.VMEM((filters, 2 * STEP, width), BF16),
            pltpu.VMEM((filters, STEP, 2 * LANES), BF16),
            pltpu.VMEM((filters, MODES, width), F32),
            pltpu.VMEM((MODES, channels), F32),
            pltpu.VMEM((MODES, channels), F32),
            pltpu.VMEM((MODES, channels), F32),
            pltpu.VMEM((MODES, channels), BF16),
            pltpu.VMEM((peers - 1, MODES, channels), BF16),
            pltpu.VMEM((PACK, STEP, LANES), BF16),
            pltpu.VMEM((tokens, 2 * channels), BF16),
            pltpu.VMEM((2 * channels, cols), BF16),
        ]
        + [pltpu.VMEM(shape, BF16) for shape in pairs for _ in range(2)]
        + [
            pltpu.VMEM((2, own, z_most), BF16),
            pltpu.VMEM((sub, half), BF16),
            pltpu.VMEM((2, own, half), BF16),
            pltpu.VMEM((sub, cols), F32),
            pltpu.VMEM((own, half), BF16),
            pltpu.VMEM((own, half), BF16),
            pltpu.VMEM((own, rest), BF16),
            pltpu.VMEM((own, rest), BF16),
            pltpu.SemaphoreType.DMA((channels // LANES,)),
            pltpu.SemaphoreType.DMA((channels // LANES,)),
            pltpu.SemaphoreType.DMA((4,)),
            pltpu.SemaphoreType.DMA((channels // LANES + 1,)),
            pltpu.SemaphoreType.DMA((2,)),
            pltpu.SemaphoreType.DMA((peers - 1,)),
            pltpu.SemaphoreType.DMA((peers - 1,)),
            pltpu.SemaphoreType.DMA((COPIES,)),
            pltpu.SemaphoreType.DMA((COPIES,)),
        ],
        compiler_params=pltpu.CompilerParams(
            collective_id=0, has_side_effects=True, vmem_limit_bytes=50 * 2**20
        ),
        name="hyena",
    )(
        *(
            pltpu.with_memory_space_constraint(array, pltpu.HBM)
            for array in (
                featurized.transpose(1, 0, 2),
                short_filter,
                decay_rate.T,
                residue.T,
                skip_gain,
                weight,
            )
        )
    )


def solution(mesh):
    finer = Mesh(
        mesh.devices.reshape(mesh.shape["ctx"], 4, 2, 2), ("ctx", "chan_0", "chan_1", "chan_2")
    )
    placed = (
        P("ctx", None, CHAN),
        P(None, None, CHAN),
        P(CHAN, None),
        P(CHAN, None),
        P(CHAN),
        P(CHAN, None),
    )
    return jax.shard_map(
        on_device, mesh=finer, in_specs=placed, out_specs=P(CTX_CHAN, None), check_vma=False
    )
```

```python
import jax
import jax.numpy as jnp
from jax import lax
from jax.experimental import pallas as pl
from jax.experimental.pallas import tpu as pltpu
from jax.sharding import Mesh
from jax.sharding import PartitionSpec as P

CHAN = ("chan_0", "chan_1", "chan_2")
CTX_CHAN = ("ctx", "chan_0", "chan_1", "chan_2")
MESH = pl.DeviceIdType.MESH
F32 = jnp.float32
BF16 = jnp.bfloat16
LANES = 128
TILE = 256
COPIES = 33
UNROLL = 4
STEP = 128
GROUP = 16
PACK = LANES // GROUP
MODES = 16
STRIP = 32
RIM = 16


def turned_to(parts, lane_group, sign):
    for bit in (1, 2, 4):
        move = (lane_group & bit) != 0
        parts = [
            jnp.where(move, parts[(k + sign * bit) % PACK], parts[k]) for k in range(PACK)
        ]
    return parts


def by_filter(parts, lane_group):
    parts = [pltpu.roll(part, k * GROUP, 1) if k else part for k, part in enumerate(parts)]
    parts = turned_to(parts, lane_group, 1)
    return [parts[-g % PACK] for g in range(PACK)]


def by_chunk(parts, lane_group):
    parts = turned_to([parts[-k % PACK] for k in range(PACK)], lane_group, -1)
    return [pltpu.roll(part, LANES - k * GROUP, 1) if k else part for k, part in enumerate(parts)]


def hi_lo(value):
    hi = value.astype(BF16).astype(F32)
    return hi, value - hi


def one_less_exp(x):
    series = jnp.ones_like(x)
    for n in range(9, 1, -1):
        series = 1.0 - x * (1.0 / n) * series
    return jnp.where(x < 0.5, x * series, 1.0 - jnp.exp(-x))


def chunk_scan(low, high, rate, place):
    for hop in (1, 2, 4):
        decay = jnp.exp(rate * (-float(hop * STEP)))
        inside = place >= hop
        a, b = pltpu.roll(low, hop * GROUP, 1), pltpu.roll(high, hop * GROUP, 1)
        low, high = (
            low + decay * jnp.where(inside, a, 0.0),
            high + decay * jnp.where(inside, b, a),
        )
    return low, high + jnp.exp(rate * (-float(PACK * STEP))) * low


def column_parts(cols):
    half = cols * 9 // 16
    split = cols * 5 // 16
    later = cols * 3 // 16
    x_parts = ((0, split), (split, half - split))
    z_parts = ((0, later), (later, cols - half - later))
    return half, x_parts, z_parts


def kernel(
    feat_hbm,
    taps_hbm,
    rate_hbm,
    residue_hbm,
    skip_hbm,
    weight_hbm,
    out_ref,
    feat,
    taps,
    rate_in,
    residue_in,
    skip_in,
    skip,
    square,
    rate_row,
    scale_row,
    rates,
    scales,
    rim,
    shifts,
    gated,
    query,
    source,
    left,
    local,
    chan_rates,
    amend,
    total,
    passed_total,
    totals,
    result,
    mixed,
    weight,
    z_send,
    z_recv,
    far_send,
    far_recv,
    near_send,
    near_recv,
    far2_send,
    far2_recv,
    near2_send,
    near2_recv,
    cross_recv,
    turn_send,
    turn_recv,
    held,
    last_x_send,
    last_x_recv,
    last_z_send,
    last_z_recv,
    pass_send,
    pass_recv,
    small_sem,
    load_sem,
    rim_sem,
    sum_send,
    sum_recv,
    send_sem,
    recv_sem,
):
    tokens, channels = feat.shape[1], feat.shape[2]
    filters = rates.shape[0]
    chunks = tokens // STEP
    blocks = channels // LANES
    width = chunks * GROUP
    halves = width // LANES
    depth = channels
    cols = weight.shape[1]
    half, x_parts, z_parts = column_parts(cols)
    rest = cols - half
    block = tokens // 4
    sub = block // 2
    own = sub // 2
    ctx = lax.axis_index("ctx")
    peers = lax.axis_size("ctx")
    x = lax.axis_index("chan_0")
    z = lax.axis_index("chan_1")
    core = lax.axis_index("chan_2")
    right, far, lefts = lax.rem(x + 1, 4), lax.rem(x + 2, 4), lax.rem(x + 3, 4)
    to_right, to_left = {"chan_0": right}, {"chan_0": lefts}
    to_z, to_core = {"chan_1": 1 - z}, {"chan_2": 1 - core}
    to_both = {"chan_1": 1 - z, "chan_2": 1 - core}

    smalls = []
    for k, (here, there) in enumerate(
        (
            (taps_hbm, taps),
            (rate_hbm, rate_in),
            (residue_hbm, residue_in),
            (skip_hbm, skip_in),
        )
    ):
        copy = pltpu.make_async_copy(here, there, small_sem.at[k])
        copy.start()
        smalls.append(copy)

    def load_of(v):
        at = pl.ds(pl.multiple_of(v * LANES, LANES), LANES)
        return pltpu.make_async_copy(feat_hbm.at[:, :, at], feat.at[:, :, at], load_sem.at[v])

    for v in range(2):
        load_of(v).start()
    my_cols = pl.ds(pl.multiple_of(core * cols, cols), cols)
    other_cols = pl.ds(pl.multiple_of((1 - core) * cols, cols), cols)
    load_weight = pltpu.make_async_copy(
        weight_hbm.at[:, my_cols], weight.at[pl.ds(0, depth), :], load_sem.at[blocks]
    )

    rim[...] = jnp.zeros_like(rim)
    totals[...] = jnp.zeros_like(totals)
    barrier = pltpu.get_barrier_semaphore()
    greeted = [{"ctx": lax.rem(ctx + d, peers)} for d in range(1, peers)]
    greeted += [to_right, to_left, to_z, to_core, to_both]
    greeted += [{"chan_0": right, "chan_2": 1 - core}, {"chan_0": lefts, "chan_2": 1 - core}]
    for to in greeted:
        pl.semaphore_signal(barrier, inc=1, device_id=to, device_id_type=MESH)

    lane = lax.broadcasted_iota(jnp.int32, (1, LANES), 1)
    lane_group = lane // GROUP
    lane_mode = lax.broadcasted_iota(jnp.int32, (MODES, LANES), 1)
    row = lax.broadcasted_iota(jnp.int32, (STEP, LANES), 0)
    col = lax.broadcasted_iota(jnp.int32, (STEP, LANES), 1)
    after = (row + 1).astype(F32)
    back = lax.rem(STEP - lane_mode, STEP).astype(F32)
    ahead = (STEP - 1 - lane_mode).astype(F32)

    def gate(v, c, slot):
        at = pl.ds(pl.multiple_of(v * LANES, LANES), LANES)
        here = pl.ds(pl.multiple_of(c * STEP, STEP), STEP)
        before = pl.ds(pl.multiple_of(jnp.maximum(c * STEP - RIM, 0), RIM), RIM)
        parts = []
        for i in range(3):
            earlier = feat[i, before, at].astype(F32)
            now = feat[i, here, at].astype(F32)
            shifts[slot, i, :RIM] = jnp.where(c > 0, earlier, 0.0)
            shifts[slot, i, RIM:] = now
            tap = taps[:, i, at]
            value = (
                tap[0:1] * now
                + tap[1:2] * shifts[slot, i, RIM - 1 : RIM - 1 + STEP]
                + tap[2:3] * shifts[slot, i, RIM - 2 : RIM - 2 + STEP]
            )
            parts.append(value)
        query[here, at] = parts[0].astype(BF16)
        gated[here, at] = (parts[1] * parts[2]).astype(BF16)

    def gate_block(v, carry):
        load_of(v).wait()

        @pl.when(v + 2 < blocks)
        def _():
            load_of(v + 2).start()

        def some_chunks(c, inner):
            for k in range(UNROLL):
                gate(v, UNROLL * c + k, k)
            return inner

        with jax.named_scope("c_gate"):
            lax.fori_loop(0, chunks // UNROLL, some_chunks, 0)
        return carry

    def swap_in(v, h, strips=STEP // STRIP):
        at = pl.ds(pl.multiple_of(v * LANES, LANES), LANES)

        def one_strip(s, inner):
            rows = pl.ds(pl.multiple_of(s * STRIP, STRIP), STRIP)
            parts = []
            for k in range(PACK):
                here = pl.ds(pl.multiple_of((h * PACK + k) * STEP + s * STRIP, STRIP), STRIP)
                parts.append(gated[here, at])
            for g, part in enumerate(by_filter(parts, lane_group)):
                source[v * PACK + g, rows, h * LANES : (h + 1) * LANES] = part
            return inner

        for s in range(strips):
            one_strip(s, 0)

    smalls[0].wait()
    lax.fori_loop(0, 2, gate_block, 0)
    load_weight.start()

    with jax.named_scope("c_smalls"):
        for copy in smalls[1:]:
            copy.wait()
    rate_all = rate_in[...]
    scale_all = residue_in[...] * jnp.sqrt(one_less_exp(2.0 * rate_all))
    for f in range(filters):
        rates[f] = jnp.broadcast_to(rate_all[:, f : f + 1], (MODES, LANES))
        scales[f] = jnp.broadcast_to(scale_all[:, f : f + 1], (MODES, LANES))
    square[...] = jnp.zeros_like(square)
    for k in range(3):
        square[k * MODES : (k + 1) * MODES, 0:filters] = rate_all
    rate_row[...] = square[...].T[:filters]
    for k in range(3):
        square[k * MODES : (k + 1) * MODES, 0:filters] = scale_all
    scale_row[...] = square[...].T[:filters]
    skip[...] = skip_in[...].reshape(1, channels)
    source[:, STEP + 3 * MODES :, :] = jnp.zeros(
        (filters, source.shape[1] - STEP - 3 * MODES, width), BF16
    )

    with jax.named_scope("c_barrier"):
        pl.semaphore_wait(barrier, len(greeted))
    rim_copy = pltpu.make_async_remote_copy(
        src_ref=feat_hbm.at[:, pl.ds(tokens - RIM, RIM), :],
        dst_ref=rim,
        send_sem=rim_sem.at[0],
        recv_sem=rim_sem.at[1],
        device_id={"ctx": lax.rem(ctx + 1, peers)},
        device_id_type=MESH,
    )

    @pl.when(ctx < peers - 1)
    def _():
        rim_copy.start()

    used = []

    def sent(src, dst, to):
        k = len(used)
        copy = pltpu.make_async_remote_copy(
            src_ref=src,
            dst_ref=dst,
            send_sem=send_sem.at[k],
            recv_sem=recv_sem.at[k],
            device_id=to,
            device_id_type=MESH,
        )
        copy.start()
        used.append(copy)
        return copy

    weight_copy = sent(weight_hbm.at[:, other_cols], weight.at[pl.ds(depth, depth), :], to_core)

    lax.fori_loop(2, blocks, gate_block, 0)

    def state_block(v, carry):
        at = pl.ds(pl.multiple_of(v * LANES, LANES), LANES)
        for h in range(halves):
            swap_in(v, h)
        packed = jnp.zeros((MODES, LANES), F32)
        for g in range(PACK):
            f = v * PACK + g
            rate = rates[f]
            hi, lo = hi_lo(jnp.exp(-rate * ahead))
            factor = jnp.concatenate([hi, lo], axis=0).astype(BF16)
            product = jnp.dot(factor, source[f, :STEP, :], preferred_element_type=F32)
            ends = product[:MODES] + product[MODES:]
            local[f] = ends
            place = (lane_group - g) & (PACK - 1)
            decay = jnp.exp(-rate * ((PACK - 1 - place) * STEP).astype(F32))
            whole = jnp.exp(rate * (-float(PACK * STEP)))
            last = decay * (whole * ends[:, :LANES] + ends[:, LANES:])
            for hop in (1, 2, 4):
                last = last + pltpu.roll(last, hop * GROUP, 1)
            packed = jnp.where(lane_group == g, last, packed)
        total[:, at] = packed
        return carry

    with jax.named_scope("c_state"):
        lax.fori_loop(0, blocks, state_block, 0)

    def amend_block(v, carry):
        at = pl.ds(pl.multiple_of(v * LANES, LANES), LANES)
        parts = []
        for i in range(3):
            rows = jnp.concatenate([rim[i, :, at], feat[i, :RIM, at]], axis=0).astype(F32)
            tap = taps[:, i, at]
            value = (
                tap[0:1] * rows[RIM:]
                + tap[1:2] * pltpu.roll(rows, 1, 0)[RIM:]
                + tap[2:3] * pltpu.roll(rows, 2, 0)[RIM:]
            )
            parts.append(value)
        new = (lax.broadcasted_iota(jnp.int32, (RIM, LANES), 0) < 2) & (ctx > 0)
        was = gated[:RIM, at].astype(F32)
        now = jnp.where(new, (parts[1] * parts[2]).astype(BF16).astype(F32), was)
        gated[:RIM, at] = now.astype(BF16)
        query[:RIM, at] = jnp.where(new, parts[0], query[:RIM, at].astype(F32)).astype(BF16)
        change = now - was
        rate = rates[v * PACK]
        for g in range(1, PACK):
            rate = jnp.where(lane_group == g, rates[v * PACK + g], rate)
        chan_rates[:, at] = rate

        def effect(count):
            return (
                jnp.exp(rate * (-float(count - 1))) * change[0:1]
                + jnp.exp(rate * (-float(count - 2))) * change[1:2]
            )

        total[:, at] = total[:, at] + effect(tokens)
        amend[:, at] = effect(STEP)
        return carry

    with jax.named_scope("c_rim"):

        @pl.when(ctx > 0)
        def _():
            rim_copy.wait_recv()

    lax.fori_loop(0, blocks, amend_block, 0)

    passed_total[...] = total[...].astype(BF16)

    def sum_copy(d):
        return pltpu.make_async_remote_copy(
            src_ref=passed_total,
            dst_ref=totals.at[d - 1],
            send_sem=sum_send.at[d - 1],
            recv_sem=sum_recv.at[d - 1],
            device_id={"ctx": lax.rem(ctx + d, peers)},
            device_id_type=MESH,
        )

    for d in range(1, peers):

        @pl.when(ctx + d < peers)
        def _():
            sum_copy(d).start()

    def build(n, carry):
        for k in range(UNROLL):
            build_one(UNROLL * n + k)
        return carry

    def build_one(f):
        first = jnp.sum(scales[f] * jnp.exp(-rates[f] * back), axis=0, keepdims=True)
        turned = pltpu.roll(
            jnp.broadcast_to(first, (STEP, LANES)), 0, 1, stride=1, stride_axis=0
        )
        left[f, :, :LANES] = jnp.where(col <= row, turned, 0.0).astype(BF16)
        hi, lo = hi_lo(scale_row[pl.ds(f, 1), :] * jnp.exp(-rate_row[pl.ds(f, 1), :] * after))
        second = (col >= MODES) & (col < 2 * MODES)
        left[f, :, LANES:] = jnp.where(second, lo, hi).astype(BF16)

    def swap_again(v, carry):
        swap_in(v, 0, 1)
        return carry

    lax.fori_loop(0, blocks, swap_again, 0)
    with jax.named_scope("c_build"):
        lax.fori_loop(0, filters // UNROLL, build, 0)
    with jax.named_scope("c_sums"):
        for d in range(1, peers):

            @pl.when(ctx >= d)
            def _():
                sum_copy(d).wait_recv()

    for v in range(blocks):
        at = pl.ds(v * LANES, LANES)
        chan_rate = chan_rates[:, at]
        carried = jnp.zeros((MODES, LANES), F32)
        for d in range(1, peers):
            decay = jnp.exp(chan_rate * (-float((d - 1) * tokens)))
            carried = carried + jnp.where(ctx >= d, decay * totals[d - 1, :, at].astype(F32), 0.0)
        total[:, at] = carried

    def state_rows(v, carry):
        at = pl.ds(pl.multiple_of(v * LANES, LANES), LANES)
        incoming = total[:, at]
        amended = pltpu.roll(amend[:, at], GROUP, 1)
        for g in range(PACK):
            f = v * PACK + g
            place = (lane_group - g) & (PACK - 1)
            a = pltpu.roll(local[f, :, :LANES], GROUP, 1)
            b = pltpu.roll(local[f, :, LANES:], GROUP, 1)
            low = jnp.where(place == 0, incoming, a + jnp.where(place == 1, amended, 0.0))
            high = jnp.where(place == 0, a, b)
            states = jnp.concatenate(chunk_scan(low, high, rates[f], place), axis=1)
            hi, lo = hi_lo(states)
            source[f, STEP : STEP + 3 * MODES, :] = jnp.concatenate([hi, hi, lo], axis=0).astype(
                BF16
            )
        return carry

    with jax.named_scope("c_states"):
        lax.fori_loop(0, blocks, state_rows, 0)

    def far_pass(v):
        rows = pl.ds(pl.multiple_of(far * block, block), block)
        return pltpu.make_async_remote_copy(
            src_ref=mixed.at[rows, pl.ds(pl.multiple_of(v * LANES, LANES), LANES)],
            dst_ref=mixed.at[rows, pl.ds(pl.multiple_of(depth + v * LANES, LANES), LANES)],
            send_sem=pass_send.at[v],
            recv_sem=pass_recv.at[v],
            device_id=to_core,
            device_id_type=MESH,
        )

    def block_out(h, then=lambda v: None):
        def one_block(v, carry):
            at = pl.ds(pl.multiple_of(v * LANES, LANES), LANES)
            wide = pl.ds(pl.multiple_of(h * LANES, LANES), LANES)
            for g in range(PACK):
                f = v * PACK + g
                result[g] = jnp.dot(
                    left[f], source[f, :, wide], preferred_element_type=F32
                ).astype(BF16)

            def one_strip(s, inner):
                rows = pl.ds(pl.multiple_of(s * STRIP, STRIP), STRIP)
                parts = by_chunk([result[g, rows, :] for g in range(PACK)], lane_group)
                for k in range(PACK):
                    here = pl.ds(
                        pl.multiple_of((h * PACK + k) * STEP + s * STRIP, STRIP), STRIP
                    )
                    value = parts[k].astype(F32) + skip[:, at] * gated[here, at].astype(F32)
                    mixed[here, at] = (query[here, at].astype(F32) * value).astype(BF16)
                return inner

            for s in range(STEP // STRIP):
                one_strip(s, 0)
            then(v)
            return carry

        return one_block

    def passed_on(at):
        rows = pl.ds(pl.multiple_of(at * block, block), block)
        return sent(
            mixed.at[rows, pl.ds(0, depth)], mixed.at[rows, pl.ds(depth, depth)], to_core
        )

    first_half = far // 2
    with jax.named_scope("c_half1"):
        lax.fori_loop(0, blocks, block_out(first_half, lambda v: far_pass(v).start()), 0)
    passed = [passed_on(far + 1 - 2 * lax.rem(far, 2))]

    def tiles(token, rows, first, count, store):
        wide = count // TILE

        def one(n, carry, whole=True):
            i, j = (n // wide, lax.rem(n, wide)) if whole else (n, wide)
            r = pl.multiple_of(i * sub, sub)
            c = pl.multiple_of(j * TILE, TILE)
            size = TILE if whole else count - wide * TILE
            value = jnp.dot(
                mixed[pl.ds(pl.multiple_of(token + r, sub), sub), :],
                weight[:, pl.ds(pl.multiple_of(first + c, LANES), size)],
                preferred_element_type=F32,
            )
            store(pl.ds(r, sub), pl.ds(c, size), value)
            return carry

        lax.fori_loop(0, (rows // sub) * wide, one, 0)
        if count % TILE:
            lax.fori_loop(0, rows // sub, lambda n, carry: one(n, carry, False), 0)

    def start_of(at):
        return at * block

    def plain(dst, extra=()):
        def store(r, c, value):
            for e in extra:
                value = value + e[r, c].astype(F32)
            dst[r, c] = value.astype(BF16)

        return store

    mine, others = z * sub, (1 - z) * sub
    order = (far, right, lefts, x)
    bands = (others, mine)

    def z_first(k):
        at = order[k]
        tiles(start_of(at) + others, sub, half, rest, plain(z_send.at[k]))
        return sent(z_send.at[k], z_recv.at[k], to_z)

    with jax.named_scope("c_w_start"):
        load_weight.wait()
        weight_copy.wait_recv()
        for v in range(blocks):
            far_pass(v).wait_recv()
    starts, fars = [], ([], [])
    for part in (0, 1):
        for s, to in ((0, to_right), (1, to_left)):
            first, size = x_parts[s]
            rows, width = pl.ds(pl.multiple_of(bands[part], sub), sub), pl.ds(0, size)
            view = far_send.at[s, rows, width]
            tiles(start_of(far) + bands[part], sub, first, size, plain(view))
            fars[s].append(sent(view, far_recv.at[s, rows, width], to))
        first, size = z_parts[part]
        piece = pl.ds(first, size)
        view = z_send.at[0, :, piece]
        tiles(start_of(far) + others, sub, half + first, size, plain(view))
        starts.append(sent(view, z_recv.at[0, :, piece], to_z))

    with jax.named_scope("c_half2"):
        lax.fori_loop(0, blocks, block_out(1 - first_half), 0)
    passed += [passed_on(x + 1 - 2 * lax.rem(x, 2)), passed_on(x)]
    with jax.named_scope("c_w_passed"):
        for copy in passed:
            copy.wait_recv()
    zs = [None, z_first(1)]
    sides = ((0, right, to_right), (1, lefts, to_left))
    nears = ([], [])

    def near(s, side, part, at, to):
        first, size = x_parts[side]
        rows, width = pl.ds(pl.multiple_of(bands[part], sub), sub), pl.ds(0, size)
        view = near_send.at[s, side, rows, width]
        extra = ()
        if s == side:
            with jax.named_scope("c_w_far"):
                fars[s][part].wait_recv()
            extra = (far_recv.at[s, rows],)
        tiles(start_of(at) + bands[part], sub, first, size, plain(view, extra))
        nears[part].append(sent(view, near_recv.at[s, side, rows, width], to))

    for s, at, to in sides:
        near(s, 1 - s, 0, at, to)
    zs.append(z_first(2))
    for s, at, to in sides:
        near(s, s, 0, at, to)
    with jax.named_scope("c_w_z0"):
        for copy in starts:
            copy.wait_recv()
    fars2 = []
    for s, to in ((0, to_right), (1, to_left)):
        first, size = z_parts[s]
        width = pl.ds(0, size)
        view = far2_send.at[s, :, width]
        tiles(
            start_of(far) + mine,
            sub,
            half + first,
            size,
            plain(view, (z_recv.at[0, :, pl.ds(first, size)],)),
        )
        fars2.append(sent(view, far2_recv.at[s, :, width], to))

    for s, at, to in sides:
        near(s, 1 - s, 1, at, to)
    zs.append(z_first(3))
    for s, at, to in sides:
        near(s, s, 1, at, to)

    my_rows = pl.ds(pl.multiple_of(core * own, own), own)
    other_rows = pl.ds(pl.multiple_of((1 - core) * own, own), own)
    nears2, crosses = [], []

    def near2(s, side, at, to, extra):
        first, size = z_parts[side]
        width = pl.ds(0, size)
        view = near2_send.at[s, side, :, width]
        tiles(
            start_of(at) + mine,
            sub,
            half + first,
            size,
            plain(view, (z_recv.at[1 + s, :, pl.ds(first, size)],) + extra),
        )
        if s != side:
            nears2.append(sent(view, near2_recv.at[s, side, :, width], to))
            return
        view = near2_send.at[s, side, other_rows, width]
        across = {"chan_0": at, "chan_2": 1 - core}
        crosses.append(sent(view, cross_recv.at[s, :, width], across))
        view = near2_send.at[s, side, my_rows, width]
        crosses.append(sent(view, near2_recv.at[s, side, my_rows, width], to))

    for s, at, to in sides:
        with jax.named_scope("c_w_z12"):
            zs[1 + s].wait_recv()
        near2(s, 1 - s, at, to, ())
    for s, at, to in sides:
        with jax.named_scope("c_w_far2"):
            fars2[s].wait_recv()
        near2(s, s, at, to, (far2_recv.at[s],))

    with jax.named_scope("c_w_near"):
        for copy in nears[0]:
            copy.wait_recv()
    for side in (0, 1):
        first, size = x_parts[side]
        away = pl.ds(pl.multiple_of(others, sub), sub)
        tiles(
            start_of(x) + others,
            sub,
            first,
            size,
            plain(
                turn_send.at[:, pl.ds(first, size)],
                (near_recv.at[0, side, away], near_recv.at[1, side, away]),
            ),
        )
    turns = [
        sent(turn_send.at[other_rows], turn_recv.at[1], to_both),
        sent(turn_send.at[my_rows], turn_recv.at[0], to_z),
    ]

    def kept(offset, extra):
        def store(r, c, value):
            for e in extra:
                value = value + e[r, c].astype(F32)
            held[r, pl.ds(pl.multiple_of(offset + c.start, LANES), c.size)] = value

        return store

    with jax.named_scope("c_w_near1"):
        for copy in nears[1]:
            copy.wait_recv()
    for side in (0, 1):
        first, size = x_parts[side]
        here = pl.ds(pl.multiple_of(mine, sub), sub)
        tiles(
            start_of(x) + mine,
            sub,
            first,
            size,
            kept(first, (near_recv.at[0, side, here], near_recv.at[1, side, here])),
        )
    x_cols = pl.ds(0, half)
    last_x_send[...] = held[other_rows, x_cols].astype(BF16)
    last_x = sent(last_x_send, last_x_recv, to_core)
    with jax.named_scope("c_w_z3"):
        zs[3].wait_recv()
    for side in (0, 1):
        first, size = z_parts[side]
        tiles(
            start_of(x) + mine,
            sub,
            half + first,
            size,
            kept(half + first, (z_recv.at[3, :, pl.ds(first, size)],)),
        )
    my_first = pl.multiple_of(core * cols, cols)
    other_first = pl.multiple_of((1 - core) * cols, cols)
    with jax.named_scope("c_w_near2"):
        for copy in nears2:
            copy.wait_recv()
    for side in (0, 1):
        first, size = z_parts[side]
        last_z_send[:, first : first + size] = (
            held[other_rows, pl.ds(half + first, size)]
            + near2_recv[1 - side, side, other_rows, :size].astype(F32)
        ).astype(BF16)
        held[my_rows, pl.ds(half + first, size)] = (
            held[my_rows, pl.ds(half + first, size)]
            + near2_recv[1 - side, side, my_rows, :size].astype(F32)
        )
    last_z = sent(last_z_send, last_z_recv, to_core)
    with jax.named_scope("c_w_turn"):
        last_x.wait_recv()
        turns[0].wait_recv()
    out_ref[:, pl.ds(other_first, half)] = (
        last_x_recv[...].astype(F32) + turn_recv[1].astype(F32)
    ).astype(BF16)
    with jax.named_scope("c_w_turn2"):
        turns[1].wait_recv()
    out_ref[:, pl.ds(my_first, half)] = (
        held[my_rows, x_cols] + turn_recv[0].astype(F32)
    ).astype(BF16)
    with jax.named_scope("c_w_last"):
        last_z.wait_recv()
    with jax.named_scope("c_w_cross"):
        for copy in crosses:
            copy.wait_recv()
    for side in (0, 1):
        first, size = z_parts[side]
        out_ref[:, pl.ds(pl.multiple_of(my_first + half + first, LANES), size)] = (
            held[my_rows, pl.ds(half + first, size)]
            + near2_recv[side, side, my_rows, :size].astype(F32)
        ).astype(BF16)
        out_ref[:, pl.ds(pl.multiple_of(other_first + half + first, LANES), size)] = (
            last_z_recv[:, first : first + size].astype(F32)
            + cross_recv[side, :, :size].astype(F32)
        ).astype(BF16)
    for v in range(blocks):
        far_pass(v).wait_send()

    @pl.when(ctx < peers - 1)
    def _():
        rim_copy.wait_send()

    for d in range(1, peers):

        @pl.when(ctx + d < peers)
        def _():
            sum_copy(d).wait_send()

    for copy in used:
        copy.wait_send()


def on_device(featurized, short_filter, decay_rate, residue, skip_gain, weight):
    tokens, _, channels = featurized.shape
    filters = decay_rate.shape[0]
    peers = lax.axis_size("ctx")
    chunks = tokens // STEP
    width = chunks * GROUP
    outs = weight.shape[1]
    cols = outs // 2
    half, x_parts, z_parts = column_parts(cols)
    rest = cols - half
    x_most = max(size for _, size in x_parts)
    z_most = max(size for _, size in z_parts)
    block = tokens // 4
    sub = block // 2
    own = sub // 2
    pairs = [
        (4, sub, rest),
        (2, block, x_most),
        (2, 2, block, x_most),
        (2, sub, z_most),
        (2, 2, sub, z_most),
    ]
    return pl.pallas_call(
        kernel,
        out_shape=jax.ShapeDtypeStruct((own, outs), BF16),
        in_specs=[pl.BlockSpec(memory_space=pltpu.HBM)] * 6,
        out_specs=pl.BlockSpec(memory_space=pltpu.VMEM),
        scratch_shapes=[
            pltpu.VMEM((3, tokens, channels), BF16),
            pltpu.VMEM(short_filter.shape, F32),
            pltpu.VMEM((MODES, filters), F32),
            pltpu.VMEM((MODES, filters), F32),
            pltpu.VMEM((channels,), F32),
            pltpu.VMEM((1, channels), F32),
            pltpu.VMEM((LANES, LANES), F32),
            pltpu.VMEM((filters, LANES), F32),
            pltpu.VMEM((filters, LANES), F32),
            pltpu.VMEM((filters, MODES, LANES), F32),
            pltpu.VMEM((filters, MODES, LANES), F32),
            pltpu.VMEM((3, RIM, channels), BF16),
            pltpu.VMEM((UNROLL, 3, RIM + STEP, LANES), F32),
            pltpu.VMEM((tokens, channels), BF16),
            pltpu.VMEM((tokens, channels), BF16),
            pltpu.VMEM((filters, 2 * STEP, width), BF16),
            pltpu.VMEM((filters, STEP, 2 * LANES), BF16),
            pltpu.VMEM((filters, MODES, width), F32),
            pltpu.VMEM((MODES, channels), F32),
            pltpu.VMEM((MODES, channels), F32),
            pltpu.VMEM((MODES, channels), F32),
            pltpu.VMEM((MODES, channels), BF16),
            pltpu.VMEM((peers - 1, MODES, channels), BF16),
            pltpu.VMEM((PACK, STEP, LANES), BF16),
            pltpu.VMEM((tokens, 2 * channels), BF16),
            pltpu.VMEM((2 * channels, cols), BF16),
        ]
        + [pltpu.VMEM(shape, BF16) for shape in pairs for _ in range(2)]
        + [
            pltpu.VMEM((2, own, z_most), BF16),
            pltpu.VMEM((sub, half), BF16),
            pltpu.VMEM((2, own, half), BF16),
            pltpu.VMEM((sub, cols), F32),
            pltpu.VMEM((own, half), BF16),
            pltpu.VMEM((own, half), BF16),
            pltpu.VMEM((own, rest), BF16),
            pltpu.VMEM((own, rest), BF16),
            pltpu.SemaphoreType.DMA((channels // LANES,)),
            pltpu.SemaphoreType.DMA((channels // LANES,)),
            pltpu.SemaphoreType.DMA((4,)),
            pltpu.SemaphoreType.DMA((channels // LANES + 1,)),
            pltpu.SemaphoreType.DMA((2,)),
            pltpu.SemaphoreType.DMA((peers - 1,)),
            pltpu.SemaphoreType.DMA((peers - 1,)),
            pltpu.SemaphoreType.DMA((COPIES,)),
            pltpu.SemaphoreType.DMA((COPIES,)),
        ],
        compiler_params=pltpu.CompilerParams(
            collective_id=0, has_side_effects=True, vmem_limit_bytes=50 * 2**20
        ),
        name="hyena",
    )(
        *(
            pltpu.with_memory_space_constraint(array, pltpu.HBM)
            for array in (
                featurized.transpose(1, 0, 2),
                short_filter,
                decay_rate.T,
                residue.T,
                skip_gain,
                weight,
            )
        )
    )


def solution(mesh):
    finer = Mesh(
        mesh.devices.reshape(mesh.shape["ctx"], 4, 2, 2), ("ctx", "chan_0", "chan_1", "chan_2")
    )
    placed = (
        P("ctx", None, CHAN),
        P(None, None, CHAN),
        P(CHAN, None),
        P(CHAN, None),
        P(CHAN),
        P(CHAN, None),
    )
    return jax.shard_map(
        on_device, mesh=finer, in_specs=placed, out_specs=P(CTX_CHAN, None), check_vma=False
    )
```
